32 devices in a mesh: beam: 2 (over y), chan: 16 (over z, x, core).
Axes of the slice: x: 2, y: 2, z: 4, core: 2. Of those that a mesh axis runs over, the one named last changes fastest.
Arguments:
- filterbank: bfloat16 [2048, 4096], P(('beam', 'chan')), parts along dimension 0
- shift_table: int32 [511], replicated, may hold values from 0 to 511, as said below
- box_widths: int32 [8], replicated, may hold values from 1 to 255, as said below
Outputs:
- dedispersed: bfloat16 [512, 4096], P(('beam', 'chan')), parts along dimension 0
- peaks: float32 [16, 256], P('beam', 'chan'), parts along dimension 0
The draws below stay inside these ranges and needn't reach their ends.
There are 2 independent parts, one for each index of `beam`. The reference program is written for one: setup_inputs(seed, part) draws one part's arguments, and reference() takes and returns one part's arrays. A program takes and returns all parts, laid end to end along the dimension named above; an argument that names none is the same for every part. Nothing has to cross between parts.
Inputs may be any that keep to these rules, and one draw needn't show every extreme that they name: `shift_table`: entry k - 1 + j, for k a power of two up to 256 and j < k, is the delay for merged trial j of a section with k trials; it equals 2 j or 2 j + 1. `box_widths`: entry i lies between 2**i and 2**(i+1) - 1.
All inputs are finite; a program needn't handle non-finite values.
Results may differ from the reference program's by a relative error of at most 0.001.
Values sent between devices are 32-bit elements; how exact they have to be, the bound alone decides.
No kernel may reach another device: no remote copies, remote signals or barrier semaphores. Data moves between devices by JAX's collectives and lax.ppermute only.
A program may use at most 64 MiB of HBM per device.

```python
import math
import jax
import jax.numpy as jnp
from jax import lax

CH_DEV = 64
ROWS = 16
TIME = 4096
WIDTHS = 8
CHANNELS = 1024
TRIALS = 256
CROSS = 4
N_CHAN = 16


def draw_filterbank(key, part):
    subkeys = jax.random.split(key, 4)
    chan_scale = jnp.exp(jax.random.uniform(subkeys[0], (CHANNELS, 1), jnp.float32, 0.0, math.log(10.0)))
    offset = jax.random.uniform(subkeys[1], (CHANNELS, 1), jnp.float32, -5.0, 5.0)
    time_scale = jnp.exp(jax.random.uniform(subkeys[2], (1, TIME), jnp.float32, 0.0, math.log(10.0)))
    fluctuation = jax.random.normal(subkeys[3], (CHANNELS, TIME), jnp.float32)
    values = offset + chan_scale * fluctuation * time_scale
    return values.astype(jnp.bfloat16)


def draw_shift_table(key, part):
    entries = 2 * TRIALS - 1
    position = jnp.arange(entries, dtype=jnp.int32) + 1
    section_size = jnp.ones((entries,), jnp.int32)
    for exponent in range(1, 31):
        section_size = jnp.where(position >= 2 ** exponent, 2 ** exponent, section_size)
    within = position - section_size
    parity = jax.random.randint(key, (entries,), 0, 2, dtype=jnp.int32)
    parity = jnp.where(within == 0, jnp.minimum(section_size - 1, 1), parity)
    parity = jnp.where(position == entries, 1, parity)
    return 2 * within + parity


def draw_box_widths(key, part):
    exponent = jnp.arange(WIDTHS, dtype=jnp.int32)
    lowest = jnp.left_shift(jnp.ones((WIDTHS,), jnp.int32), exponent)
    jitter = jax.random.randint(key, (WIDTHS,), 0, 2 ** 30, dtype=jnp.int32) % lowest
    widths_out = lowest + jitter
    return jnp.where(exponent == WIDTHS - 1, 2 * lowest - 1, widths_out)


def setup_inputs(seed: int = 0, part: int = 0) -> dict:
    splits = jax.random.split(jax.random.key(seed), 4)
    part_keys = jax.random.split(jax.random.fold_in(splits[3], part), 4)
    filterbank = draw_filterbank(jax.random.fold_in(jax.random.fold_in(splits[3], part), 71), part)
    shift_table = draw_shift_table(jax.random.fold_in(splits[3], 71), part)
    box_widths = draw_box_widths(jax.random.fold_in(splits[3], 71), part)
    return dict(filterbank=filterbank, shift_table=shift_table, box_widths=box_widths)


epsilon = 1e-05

def advance(rows_in, shifts):
    length = rows_in.shape[-1]
    padded = jnp.concatenate([rows_in, jnp.zeros_like(rows_in)], axis=-1)

    def single(strip, amount):
        return lax.dynamic_slice_in_dim(strip, jnp.minimum(amount, length), length, strip.ndim - 1)
    return jax.vmap(single, in_axes=(-2, 0), out_axes=-2)(padded, shifts)

def merge_pairs(subbands, shift_table, trials_now):
    paired = subbands.reshape(subbands.shape[0] // 2, 2, subbands.shape[1], subbands.shape[2])
    lower_rows = paired[:, 0]
    upper_rows = paired[:, 1]
    if trials_now > subbands.shape[1]:
        lower_rows = jnp.repeat(lower_rows, 2, axis=1)
        upper_rows = jnp.repeat(upper_rows, 2, axis=1)
    return lower_rows + advance(upper_rows, shift_table[trials_now - 1:2 * trials_now - 1])

def local_tree(spectra, shift_table):
    chan_count = spectra.shape[0]
    subbands = spectra[:, None, :]
    band_span = 1
    while band_span < chan_count:
        band_span *= 2
        subbands = merge_pairs(subbands, shift_table, max(1, band_span * ROWS // chan_count))
    return subbands[0]

def normalize(channel_block):
    values = channel_block.astype(jnp.float32)
    centre = lax.optimization_barrier(jnp.mean(values, axis=1, keepdims=True))
    spread = lax.optimization_barrier(jnp.mean(jnp.square(values - centre), axis=1, keepdims=True))
    return (values - centre) * lax.rsqrt(spread + epsilon)

def boxcar_peaks(scaled, box_widths):
    length = scaled.shape[1]
    running = jnp.cumsum(scaled, axis=1)
    padded = jnp.concatenate([jnp.zeros_like(running), running], axis=1)

    def single(box_width):
        earlier = lax.dynamic_slice_in_dim(padded, length - box_width, length, 1)
        box_sums = (running - earlier) * lax.rsqrt(box_width.astype(jnp.float32))
        return lax.optimization_barrier(jnp.max(box_sums, axis=1))
    return lax.map(single, box_widths)

def reference(filterbank, shift_table, box_widths):
    groups = filterbank.reshape(N_CHAN, CH_DEV, TIME)

    def add_group(summed, channel_block):
        return (summed + lax.optimization_barrier(jnp.sum(normalize(channel_block), axis=0)), None)
    summed, _ = lax.scan(add_group, jnp.zeros((TIME,), jnp.float32), groups)
    channel_mean = summed / CHANNELS

    def local_part(channel_block):
        return local_tree(normalize(channel_block) - channel_mean, shift_table)
    subbands = lax.map(local_part, groups)
    while subbands.shape[0] > 1:
        subbands = merge_pairs(subbands, shift_table, 2 * subbands.shape[1])
    series = subbands[0]
    block_index = jnp.arange(N_CHAN, dtype=jnp.int32)
    reversed_block = jnp.zeros((N_CHAN,), jnp.int32)
    for bit_number in range(CROSS):
        reversed_block = reversed_block + (block_index >> bit_number & 1) * 2 ** (CROSS - 1 - bit_number)
    ordered = series.reshape(N_CHAN, ROWS, TIME)[reversed_block].reshape(TRIALS, TIME)
    centre = lax.optimization_barrier(jnp.mean(ordered, axis=1, keepdims=True))
    spread = lax.optimization_barrier(jnp.mean(jnp.square(ordered - centre), axis=1, keepdims=True))
    scaled = (ordered - centre) * lax.rsqrt(spread + epsilon)
    dedispersed = scaled.astype(jnp.bfloat16)
    peaks = boxcar_peaks(scaled, box_widths)
    return (dedispersed, peaks)
```

```python
import functools

import jax
import jax.numpy as jnp
from jax import lax
from jax.experimental import pallas as pl
from jax.experimental.pallas import tpu as pltpu
from jax.sharding import PartitionSpec as P

ROWS = 16
LANES = 128
PAD = 8

epsilon = 1e-05


def reverse4(value):
    return (value & 1) << 3 | (value & 2) << 1 | (value & 4) >> 1 | (value & 8) >> 3


def lane_index(blocks):
    return lax.broadcasted_iota(jnp.int32, (blocks, LANES), 1)


def later(ref, row, blocks, lane, whole, part):
    here = ref[row, pl.ds(whole, blocks), :]
    beyond = ref[row, pl.ds(whole + 1, blocks), :]
    return pltpu.roll(jnp.where(lane >= part, here, beyond), (LANES - part) % LANES, axis=1)


def clear_tail(ref, count, blocks):
    for row in range(count):
        ref[row, pl.ds(blocks, PAD), :] = jnp.zeros((PAD, LANES), jnp.float32)


def tree_section(source, target, blocks, lane, subbands, trials_in, trials_out, shift_of):
    for trial in range(trials_out):
        shift = shift_of(trial)
        whole, part = shift // LANES, shift % LANES
        old = trial * trials_in // trials_out
        for band in range(subbands // 2):
            low = source[2 * band * trials_in + old, pl.ds(0, blocks), :]
            high = later(source, (2 * band + 1) * trials_in + old, blocks, lane, whole, part)
            target[band * trials_out + trial, pl.ds(0, blocks), :] = low + high


def local_kernel(me_ref, table_ref, x_ref, keep_ref, send_ref, normal, first, second):
    channels, length = x_ref.shape
    blocks = length // LANES
    stride = blocks + PAD
    lane = lane_index(blocks)
    flat = normal.reshape(channels * stride, LANES)
    for group in range(channels // 16):
        rows = pl.ds(16 * group, 16)

        def piece(block):
            return x_ref[rows, pl.ds(block * LANES, LANES)].astype(jnp.float32)

        total = piece(0)
        for block in range(1, blocks):
            total = total + piece(block)
        centre = jnp.sum(total, axis=1, keepdims=True) / length
        centre = jnp.broadcast_to(centre, (16, LANES))
        total = jnp.square(piece(0) - centre)
        for block in range(1, blocks):
            total = total + jnp.square(piece(block) - centre)
        spread = jnp.sum(total, axis=1, keepdims=True) / length
        gain = jnp.broadcast_to(lax.rsqrt(spread + epsilon), (16, LANES))
        for block in range(blocks):
            value = (piece(block) - centre) * gain
            for half in range(2):
                start = (16 * group + 8 * half) * stride + block
                flat[pl.ds(start, 8, stride=stride), :] = value[8 * half : 8 * half + 8]
    clear_tail(normal, channels, blocks)
    clear_tail(first, channels // 2, blocks)
    clear_tail(second, channels // 4, blocks)

    partial = normal[0, pl.ds(0, blocks), :]
    for channel in range(1, channels):
        partial = partial + normal[channel, pl.ds(0, blocks), :]
    send_ref[8] = partial

    bands, trials = channels, 1
    source = normal
    buffers = (first, second)
    step = 0
    while bands > 2:
        fresh = max(1, 2 * channels // bands * ROWS // channels)
        target = buffers[step % 2]
        tree_section(
            source, target, blocks, lane, bands, trials, fresh, lambda trial: table_ref[fresh - 1 + trial]
        )
        source = target
        bands, trials = bands // 2, fresh
        step += 1
    mine = reverse4(me_ref[0] % 16)
    for trial in range(ROWS):
        shift = table_ref[ROWS - 1 + trial]
        old = trial * trials // ROWS
        high = later(source, trials + old, blocks, lane, shift // LANES, shift % LANES)
        value = source[old, pl.ds(0, blocks), :] + high
        place = mine ^ trial
        keep_ref[place] = value
    for place in range(8):
        send_ref[place] = keep_ref[8 + place]


def local_rows(filterbank, shift_table, me):
    channels, length = filterbank.shape
    blocks = length // LANES
    stride = blocks + PAD
    smem = pl.BlockSpec(memory_space=pltpu.SMEM)
    vmem = pl.BlockSpec(memory_space=pltpu.VMEM)
    return pl.pallas_call(
        local_kernel,
        out_shape=(
            jax.ShapeDtypeStruct((ROWS, blocks, LANES), jnp.float32),
            jax.ShapeDtypeStruct((9, blocks, LANES), jnp.float32),
        ),
        in_specs=[smem, smem, vmem],
        out_specs=(vmem, vmem),
        scratch_shapes=[
            pltpu.VMEM((channels, stride, LANES), jnp.float32),
            pltpu.VMEM((channels // 2, stride, LANES), jnp.float32),
            pltpu.VMEM((channels // 4, stride, LANES), jnp.float32),
        ],
        compiler_params=pltpu.CompilerParams(vmem_limit_bytes=32 << 20),
        name="local_tree",
    )(me, shift_table, filterbank)


def mean_path(mean, table_ref, scratch, blocks, lane, channels, row):
    clear_tail(scratch, 2, blocks)
    bands = channels
    value = mean
    step = 0
    while bands > 1:
        bands //= 2
        trials = max(1, channels // bands * ROWS // channels)
        shift = table_ref[trials - 1 + row * trials // ROWS]
        scratch[step % 2, pl.ds(0, blocks), :] = value
        value = value + later(scratch, step % 2, blocks, lane, shift // LANES, shift % LANES)
        step += 1
    return value


def cross_tree(me, table_ref, first, second, blocks, lane):
    row = reverse4(me % 16)
    bands, trials = ROWS, 1
    source, target = first, second
    while bands > 1:
        fresh = 2 * trials
        base = ROWS * fresh - 1 + row * fresh
        tree_section(
            source, target, blocks, lane, bands, trials, fresh, lambda trial: table_ref[base + trial]
        )
        source, target = target, source
        bands, trials = bands // 2, fresh
    return source


def split_bf16(value):
    high = value.astype(jnp.bfloat16)
    rest = value - high.astype(jnp.float32)
    middle = rest.astype(jnp.bfloat16)
    low = (rest - middle.astype(jnp.float32)).astype(jnp.bfloat16)
    return high, middle, low


def finish(rows, width_ref, out_ref, peaks_ref, prefix, blocks):
    length = blocks * LANES
    stride = blocks + PAD
    lane = lane_index(blocks)
    upper = lax.broadcasted_iota(jnp.int32, (LANES, LANES), 0)
    right = lax.broadcasted_iota(jnp.int32, (LANES, LANES), 1)
    running = jnp.where(upper <= right, 1.0, 0.0).astype(jnp.bfloat16)
    ones = jnp.ones((LANES, LANES), jnp.bfloat16)
    row_i = lax.broadcasted_iota(jnp.int32, (blocks, blocks), 0)
    row_j = lax.broadcasted_iota(jnp.int32, (blocks, blocks), 1)
    before = jnp.where(row_j < row_i, 1.0, 0.0).astype(jnp.bfloat16)

    def dots(left, right_side):
        return jnp.dot(left, right_side, preferred_element_type=jnp.float32)

    for trial in range(ROWS):
        value = rows[trial, pl.ds(0, blocks), :]
        centre = jnp.sum(value, axis=(0, 1), keepdims=True) / length
        value = value - centre
        spread = jnp.sum(jnp.square(value), axis=(0, 1), keepdims=True) / length
        value = value * lax.rsqrt(spread + epsilon)
        rows[trial, pl.ds(0, blocks), :] = value
        parts = split_bf16(value)
        within = sum(dots(part, running) for part in parts)
        totals = split_bf16(sum(dots(part, ones) for part in parts))
        offset = sum(dots(before, part) for part in totals)
        prefix[trial, pl.ds(PAD, blocks), :] = within + offset
        prefix[trial, pl.ds(0, PAD), :] = jnp.zeros((PAD, LANES), jnp.float32)
    flat = rows.reshape(ROWS * stride, LANES)
    for block in range(blocks):
        top = flat[pl.ds(block, 8, stride=stride), :]
        bottom = flat[pl.ds(block + 8 * stride, 8, stride=stride), :]
        both = jnp.concatenate([top, bottom], axis=0)
        out_ref[:, pl.ds(block * LANES, LANES)] = both.astype(jnp.bfloat16)
    widths = peaks_ref.shape[0]
    for index in range(widths):
        width = width_ref[index]
        back = PAD * LANES - width
        whole, part = back // LANES, back % LANES
        best = []
        for trial in range(ROWS):
            here = prefix[trial, pl.ds(whole, blocks), :]
            beyond = prefix[trial, pl.ds(whole + 1, blocks), :]
            earlier = pltpu.roll(jnp.where(lane >= part, here, beyond), (LANES - part) % LANES, axis=1)
            gap = prefix[trial, pl.ds(PAD, blocks), :] - earlier
            best.append(jnp.max(gap, axis=0, keepdims=True))
        best = jnp.max(jnp.concatenate(best, axis=0), axis=1, keepdims=True)
        scale = lax.rsqrt(jnp.full((ROWS, 1), width, jnp.int32).astype(jnp.float32))
        peaks_ref[index : index + 1, :] = jnp.transpose(best * scale)


def cross_kernel(
    channels, count, finishing, me_ref, table_ref, width_ref,
    keep_ref, core_ref, x_ref, z1_ref, z2_ref, z3_ref, mean_ref,
    *rest,
):
    blocks = keep_ref.shape[1]
    lane = lane_index(blocks)
    if finishing:
        out_ref, peaks_ref, first, second, prefix = rest
    else:
        series_ref, first, second, prefix = rest
    me = me_ref[0]
    here = me % 16
    mean = mean_ref[0]
    if finishing:
        mean = mean + z1_ref[4] + z2_ref[4] + z3_ref[4]
    mean = mean / (channels * count)
    dropped = mean_path(mean, table_ref, prefix, blocks, lane, channels, reverse4(here))
    clear_tail(first, ROWS, blocks)
    clear_tail(second, ROWS, blocks)

    def place(offset, value):
        first[here ^ offset, pl.ds(0, blocks), :] = value - dropped

    place(0, keep_ref[0])
    place(1, core_ref[0])
    place(2, x_ref[0])
    place(3, x_ref[4])
    for step, ref in ((1, z1_ref), (2, z2_ref), (3, z3_ref)):
        for inner in range(4):
            place(4 * step + inner, ref[inner])
    rows = cross_tree(me, table_ref, first, second, blocks, lane)
    if finishing:
        finish(rows, width_ref, out_ref, peaks_ref, prefix, blocks)
    else:
        for trial in range(ROWS):
            series_ref[trial] = rows[trial, pl.ds(0, blocks), :]


def finish_kernel(width_ref, series_ref, out_ref, peaks_ref, rows, prefix):
    blocks = series_ref.shape[1]
    for trial in range(ROWS):
        rows[trial, pl.ds(0, blocks), :] = series_ref[trial]
    finish(rows, width_ref, out_ref, peaks_ref, prefix, blocks)


def row_scratch(blocks):
    return pltpu.VMEM((ROWS, blocks + PAD, LANES), jnp.float32)


def final_shapes(blocks, widths):
    return (
        jax.ShapeDtypeStruct((ROWS, blocks * LANES), jnp.bfloat16),
        jax.ShapeDtypeStruct((widths, ROWS), jnp.float32),
    )


def swapped(block, distance):
    count = lax.axis_size("chan")
    return lax.ppermute(block, "chan", [(device, device ^ distance) for device in range(count)])


def advance(rows_in, shifts, start):
    count, length = rows_in.shape
    padded = jnp.concatenate([rows_in, jnp.zeros_like(rows_in)], axis=1)
    moved = lax.dynamic_slice_in_dim(padded, jnp.minimum(2 * start, length), length, 1)
    moved = jnp.concatenate([moved, jnp.zeros((count, 2 * count), moved.dtype)], axis=1)
    width = length + 2 * count
    flat = jnp.concatenate([moved.reshape(-1), jnp.zeros((2 * count,), moved.dtype)])
    skewed = flat.reshape(count, width + 2)[:, :length]
    odd = jnp.concatenate([skewed[:, 1:], jnp.zeros((count, 1), moved.dtype)], axis=1)
    parity = shifts - 2 * (start + jnp.arange(count, dtype=jnp.int32))
    return jnp.where((parity == 1)[:, None], odd, skewed)


def wider_sections(current, shift_table, me, section_count):
    half = ROWS // 2
    position = reverse4(me % 16)
    for bit in range(4, section_count):
        side = me >> bit & 1
        trials_now = 2 * ROWS << bit
        theirs = lax.dynamic_slice_in_dim(current, (1 - side) * half, half, 0)
        ours = lax.dynamic_slice_in_dim(current, side * half, half, 0)
        arrived = swapped(theirs, 1 << bit)
        lower = jnp.where(side == 0, ours, arrived)
        upper = jnp.where(side == 0, arrived, ours)
        first_trial = 2 * (position * ROWS + side * half)
        shifts = lax.dynamic_slice_in_dim(shift_table, trials_now - 1 + first_trial, ROWS)
        current = jnp.repeat(lower, 2, axis=0) + advance(jnp.repeat(upper, 2, axis=0), shifts, first_trial)
        position = 2 * position + side
    return current


def shards(filterbank, shift_table, box_widths):
    channels, length = filterbank.shape
    blocks = length // LANES
    widths = box_widths.shape[0]
    count = lax.axis_size("chan")
    section_count = count.bit_length() - 1
    me = lax.axis_index("chan")
    me_array = jnp.reshape(me, (1,)).astype(jnp.int32)
    keep, send = local_rows(filterbank, shift_table, me_array)
    small = section_count == 4

    core = swapped(send, 1)
    mean = send[8:] + core[8:]
    across = swapped(jnp.concatenate([keep[4:8], core[4:8], mean], axis=0), 2)
    mean = mean + across[8:]
    arrived = []
    for step in (1, 2, 3):
        low = (0, 2, 1, 3)[step]
        parts = [rows[low : low + 1] for rows in (keep, core, across, across[4:8])]
        if small:
            parts.append(mean)
        arrived.append(swapped(jnp.concatenate(parts, axis=0), 4 * step))
    if not small:
        mean = lax.psum(send[8:], "chan")

    smem = pl.BlockSpec(memory_space=pltpu.SMEM)
    vmem = pl.BlockSpec(memory_space=pltpu.VMEM)
    params = pltpu.CompilerParams(vmem_limit_bytes=32 << 20)
    call = pl.pallas_call(
        functools.partial(cross_kernel, channels, count, small),
        out_shape=final_shapes(blocks, widths)
        if small
        else jax.ShapeDtypeStruct((ROWS, blocks, LANES), jnp.float32),
        in_specs=[smem] * 3 + [vmem] * 7,
        out_specs=(vmem, vmem) if small else vmem,
        scratch_shapes=[row_scratch(blocks)] * 3,
        compiler_params=params,
        name="cross_tree",
    )
    result = call(me_array, shift_table, box_widths, keep, core, across, *arrived, mean)
    if small:
        return tuple(result)
    current = wider_sections(result.reshape(ROWS, length), shift_table, me, section_count)
    return tuple(
        pl.pallas_call(
            finish_kernel,
            out_shape=final_shapes(blocks, widths),
            in_specs=[smem, vmem],
            out_specs=(vmem, vmem),
            scratch_shapes=[row_scratch(blocks)] * 2,
            compiler_params=params,
            name="finish",
        )(box_widths, current.reshape(ROWS, blocks, LANES))
    )


def solution(mesh):
    placed = (P(("beam", "chan"), None), P(), P())
    return jax.shard_map(
        shards,
        mesh=mesh,
        in_specs=placed,
        out_specs=(P(("beam", "chan"), None), P("beam", "chan")),
        check_vma=False,
    )
```

```python
import functools

import jax
import jax.numpy as jnp
from jax import lax
from jax.experimental import pallas as pl
from jax.experimental.pallas import tpu as pltpu
from jax.sharding import PartitionSpec as P

ROWS = 16
LANES = 128
PAD = 8

epsilon = 1e-05


def reverse4(value):
    return (value & 1) << 3 | (value & 2) << 1 | (value & 4) >> 1 | (value & 8) >> 3


def lane_index(blocks):
    return lax.broadcasted_iota(jnp.int32, (blocks, LANES), 1)


def later(ref, row, blocks, lane, shift):
    whole, part = shift >> 7, shift & 127
    here = ref[row, pl.ds(whole, blocks), :]
    beyond = ref[row, pl.ds(whole + 1, blocks), :]
    return pltpu.roll(jnp.where(lane >= part, here, beyond), (LANES - part) & 127, axis=1)


def clear_tail(ref, count, blocks):
    for row in range(count):
        ref[row, pl.ds(blocks, PAD), :] = jnp.zeros((PAD, LANES), jnp.float32)


def tree_section(source, target, blocks, lane, subbands, trials_in, trials_out, shift_of, taken=None):
    for trial in range(trials_out):
        shift = shift_of(trial)
        old = trial * trials_in // trials_out
        for band in range(subbands // 2):
            low = source[2 * band * trials_in + old, pl.ds(0, blocks), :]
            high = later(source, (2 * band + 1) * trials_in + old, blocks, lane, shift)
            value = low + high
            if taken is not None:
                value = value - taken[trial]
            target[band * trials_out + trial, pl.ds(0, blocks), :] = value


def local_kernel(table_hbm, x_hbm, rows_ref, table_ref, x_ref, normal, first, second, table_sem, x_sem):
    channels, length = x_ref.shape
    blocks = length // LANES
    stride = blocks + PAD
    groups = channels // 16
    table_copy = pltpu.make_async_copy(table_hbm, table_ref, table_sem)
    copies = [
        pltpu.make_async_copy(x_hbm.at[pl.ds(16 * group, 16)], x_ref.at[pl.ds(16 * group, 16)], x_sem.at[group])
        for group in range(groups)
    ]
    for copy in copies:
        copy.start()
    table_copy.start()
    lane = lane_index(blocks)
    flat = normal.reshape(channels * stride, LANES)
    clear_tail(normal, channels, blocks)
    clear_tail(first, channels // 2, blocks)
    clear_tail(second, channels // 4, blocks)
    for group in range(groups):
        rows = pl.ds(16 * group, 16)

        def piece(block):
            return x_ref[rows, pl.ds(block * LANES, LANES)].astype(jnp.float32)

        copies[group].wait()
        total = piece(0)
        for block in range(1, blocks):
            total = total + piece(block)
        centre = jnp.sum(total, axis=1, keepdims=True) / length
        centre = jnp.broadcast_to(centre, (16, LANES))
        total = jnp.square(piece(0) - centre)
        for block in range(1, blocks):
            total = total + jnp.square(piece(block) - centre)
        spread = jnp.sum(total, axis=1, keepdims=True) / length
        gain = jnp.broadcast_to(lax.rsqrt(spread + epsilon), (16, LANES))
        for block in range(blocks):
            value = (piece(block) - centre) * gain
            for half in range(2):
                start = (16 * group + 8 * half) * stride + block
                flat[pl.ds(start, 8, stride=stride), :] = value[8 * half : 8 * half + 8]

    partial = normal[0, pl.ds(0, blocks), :]
    for channel in range(1, channels):
        partial = partial + normal[channel, pl.ds(0, blocks), :]
    rows_ref[ROWS] = partial
    table_copy.wait()

    bands, trials = channels, 1
    source = normal
    buffers = (first, second)
    step = 0
    while bands > 2:
        fresh = max(1, 2 * channels // bands * ROWS // channels)
        target = buffers[step % 2]
        tree_section(
            source, target, blocks, lane, bands, trials, fresh, lambda trial: table_ref[fresh - 1 + trial]
        )
        source = target
        bands, trials = bands // 2, fresh
        step += 1
    mine = reverse4(lax.axis_index("chan") & 15)
    for trial in range(ROWS):
        shift = table_ref[ROWS - 1 + trial]
        old = trial * trials // ROWS
        high = later(source, trials + old, blocks, lane, shift)
        rows_ref[mine ^ trial] = source[old, pl.ds(0, blocks), :] + high


def local_rows(filterbank, shift_table):
    channels, length = filterbank.shape
    blocks = length // LANES
    stride = blocks + PAD
    hbm = pl.BlockSpec(memory_space=pltpu.HBM)
    return pl.pallas_call(
        local_kernel,
        out_shape=jax.ShapeDtypeStruct((ROWS + 1, blocks, LANES), jnp.float32),
        in_specs=[hbm, hbm],
        out_specs=pl.BlockSpec(memory_space=pltpu.VMEM),
        scratch_shapes=[
            pltpu.SMEM(shift_table.shape, jnp.int32),
            pltpu.VMEM(filterbank.shape, filterbank.dtype),
            pltpu.VMEM((channels, stride, LANES), jnp.float32),
            pltpu.VMEM((channels // 2, stride, LANES), jnp.float32),
            pltpu.VMEM((channels // 4, stride, LANES), jnp.float32),
            pltpu.SemaphoreType.DMA,
            pltpu.SemaphoreType.DMA((channels // 16,)),
        ],
        compiler_params=pltpu.CompilerParams(vmem_limit_bytes=32 << 20),
        name="local_tree",
    )(shift_table, filterbank)


def mean_path(mean, table_ref, scratch, blocks, lane, channels, row):
    bands = channels
    value = mean
    step = 0
    while bands > 1:
        bands //= 2
        trials = max(1, channels // bands * ROWS // channels)
        shift = table_ref[trials - 1 + (row >> (ROWS // trials).bit_length() - 1)]
        scratch[step, pl.ds(0, blocks), :] = value
        value = value + later(scratch, step, blocks, lane, shift)
        step += 1
    return value


def cross_tree(me, mean, table_ref, first, second, spare, blocks, lane, channels):
    row = reverse4(me & 15)
    clear_tail(spare, ROWS, blocks)
    clear_tail(first, ROWS, blocks)
    clear_tail(second, ROWS, blocks)
    mean = mean_path(mean, table_ref, spare, blocks, lane, channels, row)
    spare[ROWS - 1, pl.ds(0, blocks), :] = mean
    bands, trials = ROWS, 1
    source, target = first, second
    while bands > 1:
        fresh = 2 * trials
        base = ROWS * fresh - 1 + row * fresh

        def shift_of(trial):
            return table_ref[base + trial]

        taken = None
        if bands == ROWS:
            taken = [mean + later(spare, ROWS - 1, blocks, lane, shift_of(trial)) for trial in range(fresh)]
        tree_section(source, target, blocks, lane, bands, trials, fresh, shift_of, taken)
        source, target = target, source
        bands, trials = bands // 2, fresh
    return source


def finish(rows, width_ref, out_ref, peaks_ref, prefix, split):
    stride = rows.shape[1]
    blocks = stride - PAD
    length = blocks * LANES
    lane = lax.broadcasted_iota(jnp.int32, (ROWS, LANES), 1)
    flat = rows.reshape(ROWS * stride, LANES)

    total = jnp.zeros((ROWS, LANES), jnp.float32)
    for block in range(blocks):
        value = jnp.concatenate(
            [flat[pl.ds(block + 8 * half * stride, 8, stride=stride), :] for half in range(2)], axis=0
        )
        prefix[2 + block] = value
        total = total + value
    centre = jnp.sum(total, axis=1, keepdims=True) / length
    centre = jnp.broadcast_to(centre, (ROWS, LANES))
    total = jnp.zeros((ROWS, LANES), jnp.float32)
    for block in range(blocks):
        total = total + jnp.square(prefix[2 + block] - centre)
    spread = jnp.sum(total, axis=1, keepdims=True) / length
    gain = jnp.broadcast_to(lax.rsqrt(spread + epsilon), (ROWS, LANES))
    for block in range(blocks):
        value = (prefix[2 + block] - centre) * gain
        rounded = value.astype(jnp.bfloat16)
        out_ref[:, pl.ds(block * LANES, LANES)] = rounded
        split[pl.ds(block * ROWS, ROWS), pl.ds(0, LANES)] = rounded
        rest = value - rounded.astype(jnp.float32)
        split[pl.ds(block * ROWS, ROWS), pl.ds(LANES, LANES)] = rest.astype(jnp.bfloat16)

    above = lax.broadcasted_iota(jnp.int32, (2 * LANES, 2 * LANES), 0) & 127
    across = lax.broadcasted_iota(jnp.int32, (2 * LANES, 2 * LANES), 1)
    weights = jnp.where(above <= across, 1.0, 0.0).astype(jnp.bfloat16)
    sums = jnp.dot(split[...], weights, preferred_element_type=jnp.float32)
    carry = jnp.zeros((ROWS, LANES), jnp.float32)
    prefix[0] = carry
    prefix[1] = carry
    for block in range(blocks):
        part = sums[block * ROWS : (block + 1) * ROWS]
        prefix[2 + block] = part[:, :LANES] + carry
        carry = carry + part[:, LANES:]

    widths = peaks_ref.shape[0]
    peaks = jnp.zeros((ROWS, LANES), jnp.float32)
    for index in range(widths):
        width = width_ref[index]
        back = 2 * LANES - width
        whole, part = back >> 7, back & 127
        turn = (LANES - part) & 127
        keep = lane < LANES - part
        best = None
        here = pltpu.roll(prefix[whole], turn, axis=1)
        for block in range(blocks):
            beyond = pltpu.roll(prefix[whole + block + 1], turn, axis=1)
            gap = prefix[2 + block] - jnp.where(keep, here, beyond)
            best = gap if best is None else jnp.maximum(best, gap)
            here = beyond
        best = jnp.max(best, axis=1, keepdims=True)
        scale = lax.rsqrt(jnp.full((ROWS, LANES), width, jnp.int32).astype(jnp.float32))
        peaks = jnp.where(lane == index, best * scale, peaks)
    peaks_ref[...] = jnp.transpose(peaks)[:widths]


def cross_kernel(
    channels, count, finishing, table_ref, width_ref,
    own_ref, core_ref, x_ref, z1_ref, z2_ref, z3_ref, mean_ref,
    *rest,
):
    blocks = own_ref.shape[1]
    lane = lane_index(blocks)
    if finishing:
        out_ref, peaks_ref, first, second, spare, prefix, split = rest
    else:
        series_ref, first, second, spare = rest
    me = lax.axis_index("chan")
    here = me & 15

    def place(offset, value):
        first[here ^ offset, pl.ds(0, blocks), :] = value

    place(0, own_ref[0])
    place(1, core_ref[0])
    place(2, x_ref[0])
    place(3, x_ref[4])
    for step, ref in ((1, z1_ref), (2, z2_ref), (3, z3_ref)):
        for inner in range(4):
            place(4 * step + inner, ref[inner])
    mean = mean_ref[0]
    if finishing:
        mean = mean + z1_ref[4] + z2_ref[4] + z3_ref[4]
    mean = mean / (channels * count)
    rows = cross_tree(me, mean, table_ref, first, second, spare, blocks, lane, channels)
    if finishing:
        finish(rows, width_ref, out_ref, peaks_ref, prefix, split)
    else:
        for trial in range(ROWS):
            series_ref[trial] = rows[trial, pl.ds(0, blocks), :]


def finish_kernel(width_ref, series_ref, out_ref, peaks_ref, rows, prefix, split):
    blocks = series_ref.shape[1]
    for trial in range(ROWS):
        rows[trial, pl.ds(0, blocks), :] = series_ref[trial]
    finish(rows, width_ref, out_ref, peaks_ref, prefix, split)


def row_scratch(blocks):
    return pltpu.VMEM((ROWS, blocks + PAD, LANES), jnp.float32)


def finish_scratch(blocks):
    return [
        pltpu.VMEM((blocks + 2, ROWS, LANES), jnp.float32),
        pltpu.VMEM((blocks * ROWS, 2 * LANES), jnp.bfloat16),
    ]


def final_shapes(blocks, widths):
    return (
        jax.ShapeDtypeStruct((ROWS, blocks * LANES), jnp.bfloat16),
        jax.ShapeDtypeStruct((widths, ROWS), jnp.float32),
    )


def swapped(block, distance):
    count = lax.axis_size("chan")
    return lax.ppermute(block, "chan", [(device, device ^ distance) for device in range(count)])


def advance(rows_in, shifts, start):
    count, length = rows_in.shape
    padded = jnp.concatenate([rows_in, jnp.zeros_like(rows_in)], axis=1)
    moved = lax.dynamic_slice_in_dim(padded, jnp.minimum(2 * start, length), length, 1)
    moved = jnp.concatenate([moved, jnp.zeros((count, 2 * count), moved.dtype)], axis=1)
    width = length + 2 * count
    flat = jnp.concatenate([moved.reshape(-1), jnp.zeros((2 * count,), moved.dtype)])
    skewed = flat.reshape(count, width + 2)[:, :length]
    odd = jnp.concatenate([skewed[:, 1:], jnp.zeros((count, 1), moved.dtype)], axis=1)
    parity = shifts - 2 * (start + jnp.arange(count, dtype=jnp.int32))
    return jnp.where((parity == 1)[:, None], odd, skewed)


def wider_sections(current, shift_table, me, section_count):
    half = ROWS // 2
    position = reverse4(me % 16)
    for bit in range(4, section_count):
        side = me >> bit & 1
        trials_now = 2 * ROWS << bit
        theirs = lax.dynamic_slice_in_dim(current, (1 - side) * half, half, 0)
        ours = lax.dynamic_slice_in_dim(current, side * half, half, 0)
        arrived = swapped(theirs, 1 << bit)
        lower = jnp.where(side == 0, ours, arrived)
        upper = jnp.where(side == 0, arrived, ours)
        first_trial = 2 * (position * ROWS + side * half)
        shifts = lax.dynamic_slice_in_dim(shift_table, trials_now - 1 + first_trial, ROWS)
        current = jnp.repeat(lower, 2, axis=0) + advance(jnp.repeat(upper, 2, axis=0), shifts, first_trial)
        position = 2 * position + side
    return current


def shards(filterbank, shift_table, box_widths):
    channels, length = filterbank.shape
    blocks = length // LANES
    widths = box_widths.shape[0]
    count = lax.axis_size("chan")
    section_count = count.bit_length() - 1
    rows = local_rows(filterbank, shift_table)
    small = section_count == 4

    core = swapped(rows[8:], 1)
    mean = rows[ROWS:] + core[8:]
    across = swapped(jnp.concatenate([rows[4:8], core[4:8], mean], axis=0), 2)
    mean = mean + across[8:]
    arrived = []
    for step in (1, 2, 3):
        low = (0, 2, 1, 3)[step]
        parts = [part[low : low + 1] for part in (rows, core, across, across[4:8])]
        if small:
            parts.append(mean)
        arrived.append(swapped(jnp.concatenate(parts, axis=0), 4 * step))
    if not small:
        mean = lax.psum(rows[ROWS:], "chan")

    smem = pl.BlockSpec(memory_space=pltpu.SMEM)
    vmem = pl.BlockSpec(memory_space=pltpu.VMEM)
    params = pltpu.CompilerParams(vmem_limit_bytes=32 << 20)
    call = pl.pallas_call(
        functools.partial(cross_kernel, channels, count, small),
        out_shape=final_shapes(blocks, widths)
        if small
        else jax.ShapeDtypeStruct((ROWS, blocks, LANES), jnp.float32),
        in_specs=[smem] * 2 + [vmem] * 7,
        out_specs=(vmem, vmem) if small else vmem,
        scratch_shapes=[row_scratch(blocks)] * 3 + (finish_scratch(blocks) if small else []),
        compiler_params=params,
        name="cross_tree",
    )
    result = call(shift_table, box_widths, rows, core, across, *arrived, mean)
    if small:
        return tuple(result)
    me = lax.axis_index("chan")
    current = wider_sections(result.reshape(ROWS, length), shift_table, me, section_count)
    return tuple(
        pl.pallas_call(
            finish_kernel,
            out_shape=final_shapes(blocks, widths),
            in_specs=[smem, vmem],
            out_specs=(vmem, vmem),
            scratch_shapes=[row_scratch(blocks)] + finish_scratch(blocks),
            compiler_params=params,
            name="finish",
        )(box_widths, current.reshape(ROWS, blocks, LANES))
    )


def solution(mesh):
    placed = (P(("beam", "chan"), None), P(), P())
    return jax.shard_map(
        shards,
        mesh=mesh,
        in_specs=placed,
        out_specs=(P(("beam", "chan"), None), P("beam", "chan")),
        check_vma=False,
    )
```

```python
import functools

import jax
import jax.numpy as jnp
from jax import lax
from jax.experimental import pallas as pl
from jax.experimental.pallas import tpu as pltpu
from jax.sharding import PartitionSpec as P

ROWS = 16
LANES = 128
PAD = 8

epsilon = 1e-05


def reverse4(value):
    return (value & 1) << 3 | (value & 2) << 1 | (value & 4) >> 1 | (value & 8) >> 3


def lane_index(blocks):
    return lax.broadcasted_iota(jnp.int32, (blocks, LANES), 1)


def later(ref, row, blocks, lane, shift):
    whole, part = shift >> 7, shift & 127
    here = ref[row, pl.ds(whole, blocks), :]
    beyond = ref[row, pl.ds(whole + 1, blocks), :]
    return pltpu.roll(jnp.where(lane >= part, here, beyond), (LANES - part) & 127, axis=1)


def clear_tail(ref, count, blocks):
    for row in range(count):
        ref[row, pl.ds(blocks, PAD), :] = jnp.zeros((PAD, LANES), jnp.float32)


def tree_section(source, target, blocks, lane, subbands, trials_in, trials_out, shift_of, taken=None):
    for trial in range(trials_out):
        shift = shift_of(trial)
        old = trial * trials_in // trials_out
        for band in range(subbands // 2):
            low = source[2 * band * trials_in + old, pl.ds(0, blocks), :]
            high = later(source, (2 * band + 1) * trials_in + old, blocks, lane, shift)
            value = low + high
            if taken is not None:
                value = value - taken[trial]
            target[band * trials_out + trial, pl.ds(0, blocks), :] = value


def local_kernel(table_hbm, x_hbm, rows_ref, table_ref, x_ref, normal, first, second, table_sem, x_sem):
    channels, length = x_ref.shape
    blocks = length // LANES
    stride = blocks + PAD
    groups = channels // 16
    table_copy = pltpu.make_async_copy(table_hbm, table_ref, table_sem)
    copies = [
        pltpu.make_async_copy(x_hbm.at[pl.ds(16 * group, 16)], x_ref.at[pl.ds(16 * group, 16)], x_sem.at[group])
        for group in range(groups)
    ]
    for copy in copies:
        copy.start()
    table_copy.start()
    lane = lane_index(blocks)
    flat = normal.reshape(channels * stride, LANES)
    clear_tail(normal, channels, blocks)
    clear_tail(first, channels // 2, blocks)
    clear_tail(second, channels // 4, blocks)
    for group in range(groups):
        rows = pl.ds(16 * group, 16)

        def piece(block):
            return x_ref[rows, pl.ds(block * LANES, LANES)].astype(jnp.float32)

        copies[group].wait()
        total = piece(0)
        for block in range(1, blocks):
            total = total + piece(block)
        centre = jnp.sum(total, axis=1, keepdims=True) / length
        centre = jnp.broadcast_to(centre, (16, LANES))
        total = jnp.square(piece(0) - centre)
        for block in range(1, blocks):
            total = total + jnp.square(piece(block) - centre)
        spread = jnp.sum(total, axis=1, keepdims=True) / length
        gain = jnp.broadcast_to(lax.rsqrt(spread + epsilon), (16, LANES))
        for block in range(blocks):
            value = (piece(block) - centre) * gain
            for half in range(2):
                start = (16 * group + 8 * half) * stride + block
                flat[pl.ds(start, 8, stride=stride), :] = value[8 * half : 8 * half + 8]

    partial = normal[0, pl.ds(0, blocks), :]
    for channel in range(1, channels):
        partial = partial + normal[channel, pl.ds(0, blocks), :]
    for row in (3, 7, 11, 15, 20):
        rows_ref[row] = partial
    table_copy.wait()

    bands, trials = channels, 1
    source = normal
    buffers = (first, second)
    step = 0
    while bands > 2:
        fresh = max(1, 2 * channels // bands * ROWS // channels)
        target = buffers[step % 2]
        tree_section(
            source, target, blocks, lane, bands, trials, fresh, lambda trial: table_ref[fresh - 1 + trial]
        )
        source = target
        bands, trials = bands // 2, fresh
        step += 1
    mine = reverse4(lax.axis_index("chan") & 15)
    for trial in range(ROWS):
        shift = table_ref[ROWS - 1 + trial]
        old = trial * trials // ROWS
        high = later(source, trials + old, blocks, lane, shift)
        place = mine ^ trial
        group, low = place >> 2, place & 3
        rows_ref[jnp.where(low == 1, ROWS + group, place - (low > 0))] = source[old, pl.ds(0, blocks), :] + high


def local_rows(filterbank, shift_table):
    channels, length = filterbank.shape
    blocks = length // LANES
    stride = blocks + PAD
    hbm = pl.BlockSpec(memory_space=pltpu.HBM)
    return pl.pallas_call(
        local_kernel,
        out_shape=jax.ShapeDtypeStruct((ROWS + 5, blocks, LANES), jnp.float32),
        in_specs=[hbm, hbm],
        out_specs=pl.BlockSpec(memory_space=pltpu.VMEM),
        scratch_shapes=[
            pltpu.SMEM(shift_table.shape, jnp.int32),
            pltpu.VMEM(filterbank.shape, filterbank.dtype),
            pltpu.VMEM((channels, stride, LANES), jnp.float32),
            pltpu.VMEM((channels // 2, stride, LANES), jnp.float32),
            pltpu.VMEM((channels // 4, stride, LANES), jnp.float32),
            pltpu.SemaphoreType.DMA,
            pltpu.SemaphoreType.DMA((channels // 16,)),
        ],
        compiler_params=pltpu.CompilerParams(vmem_limit_bytes=32 << 20),
        name="local_tree",
    )(pltpu.with_memory_space_constraint(shift_table, pltpu.HBM), pltpu.with_memory_space_constraint(filterbank, pltpu.HBM))


def mean_path(mean, table_ref, scratch, blocks, lane, channels, row):
    bands = channels
    value = mean
    step = 0
    while bands > 1:
        bands //= 2
        trials = max(1, channels // bands * ROWS // channels)
        shift = table_ref[trials - 1 + (row >> (ROWS // trials).bit_length() - 1)]
        scratch[step, pl.ds(0, blocks), :] = value
        value = value + later(scratch, step, blocks, lane, shift)
        step += 1
    return value


def cross_tree(me, mean, table_ref, first, second, spare, blocks, lane, channels):
    row = reverse4(me & 15)
    clear_tail(spare, ROWS, blocks)
    clear_tail(first, ROWS, blocks)
    clear_tail(second, ROWS, blocks)
    mean = mean_path(mean, table_ref, spare, blocks, lane, channels, row)
    spare[ROWS - 1, pl.ds(0, blocks), :] = mean
    bands, trials = ROWS, 1
    source, target = first, second
    while bands > 1:
        fresh = 2 * trials
        base = ROWS * fresh - 1 + row * fresh

        def shift_of(trial):
            return table_ref[base + trial]

        taken = None
        if bands == ROWS:
            taken = [mean + later(spare, ROWS - 1, blocks, lane, shift_of(trial)) for trial in range(fresh)]
        tree_section(source, target, blocks, lane, bands, trials, fresh, shift_of, taken)
        source, target = target, source
        bands, trials = bands // 2, fresh
    return source


def finish(rows, width_ref, out_ref, peaks_ref, prefix, split):
    stride = rows.shape[1]
    blocks = stride - PAD
    length = blocks * LANES
    lane = lax.broadcasted_iota(jnp.int32, (ROWS, LANES), 1)
    flat = rows.reshape(ROWS * stride, LANES)

    total = jnp.zeros((ROWS, LANES), jnp.float32)
    for block in range(blocks):
        value = jnp.concatenate(
            [flat[pl.ds(block + 8 * half * stride, 8, stride=stride), :] for half in range(2)], axis=0
        )
        prefix[2 + block] = value
        total = total + value
    centre = jnp.sum(total, axis=1, keepdims=True) / length
    centre = jnp.broadcast_to(centre, (ROWS, LANES))
    total = jnp.zeros((ROWS, LANES), jnp.float32)
    for block in range(blocks):
        total = total + jnp.square(prefix[2 + block] - centre)
    spread = jnp.sum(total, axis=1, keepdims=True) / length
    gain = jnp.broadcast_to(lax.rsqrt(spread + epsilon), (ROWS, LANES))
    for block in range(blocks):
        value = (prefix[2 + block] - centre) * gain
        rounded = value.astype(jnp.bfloat16)
        out_ref[:, pl.ds(block * LANES, LANES)] = rounded
        split[pl.ds(block * ROWS, ROWS), pl.ds(0, LANES)] = rounded
        rest = value - rounded.astype(jnp.float32)
        split[pl.ds(block * ROWS, ROWS), pl.ds(LANES, LANES)] = rest.astype(jnp.bfloat16)

    above = lax.broadcasted_iota(jnp.int32, (2 * LANES, 2 * LANES), 0) & 127
    across = lax.broadcasted_iota(jnp.int32, (2 * LANES, 2 * LANES), 1)
    weights = jnp.where(above <= across, 1.0, 0.0).astype(jnp.bfloat16)
    sums = jnp.dot(split[...], weights, preferred_element_type=jnp.float32)
    carry = jnp.zeros((ROWS, LANES), jnp.float32)
    prefix[0] = carry
    prefix[1] = carry
    for block in range(blocks):
        part = sums[block * ROWS : (block + 1) * ROWS]
        prefix[2 + block] = part[:, :LANES] + carry
        carry = carry + part[:, LANES:]

    widths = peaks_ref.shape[0]
    peaks = jnp.zeros((ROWS, LANES), jnp.float32)
    for index in range(widths):
        width = width_ref[index]
        back = 2 * LANES - width
        whole, part = back >> 7, back & 127
        turn = (LANES - part) & 127
        keep = lane < LANES - part
        best = None
        here = pltpu.roll(prefix[whole], turn, axis=1)
        for block in range(blocks):
            beyond = pltpu.roll(prefix[whole + block + 1], turn, axis=1)
            gap = prefix[2 + block] - jnp.where(keep, here, beyond)
            best = gap if best is None else jnp.maximum(best, gap)
            here = beyond
        best = jnp.max(best, axis=1, keepdims=True)
        scale = lax.rsqrt(jnp.full((ROWS, LANES), width, jnp.int32).astype(jnp.float32))
        peaks = jnp.where(lane == index, best * scale, peaks)
    peaks_ref[...] = jnp.transpose(peaks)[:widths]


def cross_kernel(
    channels, count, finishing, table_ref, width_ref,
    own_ref, core_ref, x_ref, both_ref, z1_ref, z3_ref, z2_ref, pc_ref, px_ref, pb_ref, mean_ref,
    *rest,
):
    blocks = own_ref.shape[1]
    lane = lane_index(blocks)
    if finishing:
        out_ref, peaks_ref, first, second, spare, prefix, split = rest
    else:
        series_ref, first, second, spare = rest
    me = lax.axis_index("chan")
    here = me & 15

    def place(offset, value):
        first[here ^ offset, pl.ds(0, blocks), :] = value

    place(0, own_ref[0])
    place(1, core_ref[0])
    place(2, x_ref[0])
    place(3, both_ref[0])
    for step, ref in ((1, z1_ref), (3, z3_ref)):
        for inner in range(4):
            place(4 * step + inner, ref[inner])
    for inner, ref in enumerate((z2_ref, pc_ref, px_ref, pb_ref)):
        place(8 + inner, ref[0])
    mean = mean_ref[0]
    if finishing:
        mean = mean + z1_ref[4] + z3_ref[4] + pc_ref[1] + px_ref[1] + pb_ref[1]
    mean = mean / (channels * count)
    rows = cross_tree(me, mean, table_ref, first, second, spare, blocks, lane, channels)
    if finishing:
        finish(rows, width_ref, out_ref, peaks_ref, prefix, split)
    else:
        for trial in range(ROWS):
            series_ref[trial] = rows[trial, pl.ds(0, blocks), :]


def finish_kernel(width_ref, series_ref, out_ref, peaks_ref, rows, prefix, split):
    blocks = series_ref.shape[1]
    for trial in range(ROWS):
        rows[trial, pl.ds(0, blocks), :] = series_ref[trial]
    finish(rows, width_ref, out_ref, peaks_ref, prefix, split)


def row_scratch(blocks):
    return pltpu.VMEM((ROWS, blocks + PAD, LANES), jnp.float32)


def finish_scratch(blocks):
    return [
        pltpu.VMEM((blocks + 2, ROWS, LANES), jnp.float32),
        pltpu.VMEM((blocks * ROWS, 2 * LANES), jnp.bfloat16),
    ]


def final_shapes(blocks, widths):
    return (
        jax.ShapeDtypeStruct((ROWS, blocks * LANES), jnp.bfloat16),
        jax.ShapeDtypeStruct((widths, ROWS), jnp.float32),
    )


def swapped(block, distance):
    count = lax.axis_size("chan")
    return lax.ppermute(block, "chan", [(device, device ^ distance) for device in range(count)])


def advance(rows_in, shifts, start):
    count, length = rows_in.shape
    padded = jnp.concatenate([rows_in, jnp.zeros_like(rows_in)], axis=1)
    moved = lax.dynamic_slice_in_dim(padded, jnp.minimum(2 * start, length), length, 1)
    moved = jnp.concatenate([moved, jnp.zeros((count, 2 * count), moved.dtype)], axis=1)
    width = length + 2 * count
    flat = jnp.concatenate([moved.reshape(-1), jnp.zeros((2 * count,), moved.dtype)])
    skewed = flat.reshape(count, width + 2)[:, :length]
    odd = jnp.concatenate([skewed[:, 1:], jnp.zeros((count, 1), moved.dtype)], axis=1)
    parity = shifts - 2 * (start + jnp.arange(count, dtype=jnp.int32))
    return jnp.where((parity == 1)[:, None], odd, skewed)


def wider_sections(current, shift_table, me, section_count):
    half = ROWS // 2
    position = reverse4(me % 16)
    for bit in range(4, section_count):
        side = me >> bit & 1
        trials_now = 2 * ROWS << bit
        theirs = lax.dynamic_slice_in_dim(current, (1 - side) * half, half, 0)
        ours = lax.dynamic_slice_in_dim(current, side * half, half, 0)
        arrived = swapped(theirs, 1 << bit)
        lower = jnp.where(side == 0, ours, arrived)
        upper = jnp.where(side == 0, arrived, ours)
        first_trial = 2 * (position * ROWS + side * half)
        shifts = lax.dynamic_slice_in_dim(shift_table, trials_now - 1 + first_trial, ROWS)
        current = jnp.repeat(lower, 2, axis=0) + advance(jnp.repeat(upper, 2, axis=0), shifts, first_trial)
        position = 2 * position + side
    return current


def shards(filterbank, shift_table, box_widths):
    channels, length = filterbank.shape
    blocks = length // LANES
    widths = box_widths.shape[0]
    count = lax.axis_size("chan")
    section_count = count.bit_length() - 1
    rows = local_rows(filterbank, shift_table)
    small = section_count == 4

    across = swapped(rows[4:8], 2)
    both = swapped(rows[12:16], 3)
    core = swapped(rows[8:12], 1)
    z2 = swapped(rows[16:], 8)
    plane = (rows, core, across, both)
    mean = sum(part[3:4] for part in plane)
    z1 = swapped(jnp.concatenate([part[1:2] for part in plane] + [mean], axis=0), 4)
    z3 = swapped(jnp.concatenate([part[2:3] for part in plane] + [mean], axis=0), 12)
    passed = [
        swapped(jnp.concatenate([z2[place : place + 1], z2[4:]], axis=0), offset)
        for offset, place in ((1, 2), (2, 1), (3, 3))
    ]
    mean = mean + z2[4:]
    arrived = [z1, z3, z2, *passed]
    if not small:
        mean = lax.psum(rows[3:4], "chan")

    smem = pl.BlockSpec(memory_space=pltpu.SMEM)
    vmem = pl.BlockSpec(memory_space=pltpu.VMEM)
    params = pltpu.CompilerParams(vmem_limit_bytes=32 << 20)
    call = pl.pallas_call(
        functools.partial(cross_kernel, channels, count, small),
        out_shape=final_shapes(blocks, widths)
        if small
        else jax.ShapeDtypeStruct((ROWS, blocks, LANES), jnp.float32),
        in_specs=[smem] * 2 + [vmem] * 11,
        out_specs=(vmem, vmem) if small else vmem,
        scratch_shapes=[row_scratch(blocks)] * 3 + (finish_scratch(blocks) if small else []),
        compiler_params=params,
        name="cross_tree",
    )
    result = call(shift_table, box_widths, *plane, *arrived, mean)
    if small:
        return tuple(result)
    me = lax.axis_index("chan")
    current = wider_sections(result.reshape(ROWS, length), shift_table, me, section_count)
    return tuple(
        pl.pallas_call(
            finish_kernel,
            out_shape=final_shapes(blocks, widths),
            in_specs=[smem, vmem],
            out_specs=(vmem, vmem),
            scratch_shapes=[row_scratch(blocks)] + finish_scratch(blocks),
            compiler_params=params,
            name="finish",
        )(box_widths, current.reshape(ROWS, blocks, LANES))
    )


def solution(mesh):
    placed = (P(("beam", "chan"), None), P(), P())
    return jax.shard_map(
        shards,
        mesh=mesh,
        in_specs=placed,
        out_specs=(P(("beam", "chan"), None), P("beam", "chan")),
        check_vma=False,
    )
```

```python
import functools

import jax
import jax.numpy as jnp
from jax import lax
from jax.experimental import pallas as pl
from jax.experimental.pallas import tpu as pltpu
from jax.sharding import PartitionSpec as P

ROWS = 16
LANES = 128
PAD = 8
WIDTHS = 8
PATH = ((1, 0), (1, 1), (2, 2), (4, 3), (8, 4), (16, 5))

epsilon = 1e-05


def reverse4(value):
    return (value & 1) << 3 | (value & 2) << 1 | (value & 4) >> 1 | (value & 8) >> 3


def lane_index(blocks):
    return lax.broadcasted_iota(jnp.int32, (blocks, LANES), 1)


def moved(here, beyond, lane, part):
    return pltpu.roll(jnp.where(lane >= part, here, beyond), (LANES - part) & 127, axis=1)


def later(ref, row, blocks, lane, shift):
    whole = shift >> 7
    here = ref[row, pl.ds(whole, blocks), :]
    beyond = ref[row, pl.ds(whole + 1, blocks), :]
    return moved(here, beyond, lane, shift & 127)


def clear_tail(ref, rows, blocks):
    for row in rows:
        ref[row, blocks : blocks + PAD, :] = jnp.zeros((PAD, LANES), jnp.float32)


def spread_sum(terms):
    strands = [None] * 4
    for index, term in enumerate(terms):
        strand = strands[index % 4]
        strands[index % 4] = term if strand is None else strand + term
    return (strands[0] + strands[1]) + (strands[2] + strands[3])


def packed_words(table_ref, width_ref, row):
    path, cross = jnp.int32(0), jnp.int32(0)
    spot = 0
    for trials, _ in PATH:
        index = row >> (ROWS // trials).bit_length() - 1
        path = path | (table_ref[trials - 1 + index] - 2 * index) << spot
        spot += 1
    spot = 0
    for fresh in (2, 4, 8, 16):
        for trial in range(fresh):
            index = row * fresh + trial
            cross = cross | (table_ref[ROWS * fresh - 1 + index] - 2 * index) << spot
            spot += 1
    words = [path, cross]
    for start in range(0, WIDTHS, 4):
        word = jnp.int32(0)
        for place in range(4):
            word = word | width_ref[start + place] << 8 * place
        words.append(word)
    return words


def local_kernel(
    table_hbm, width_hbm, x_hbm, rows_ref, words_ref,
    table_ref, width_ref, x_ref, normal, inner, quads, eights, sixteens, halves, small_sem, x_sem,
):
    channels, length = x_ref.shape
    blocks = length // LANES
    stride = blocks + PAD
    groups = channels // 16
    copies = [
        pltpu.make_async_copy(x_hbm.at[pl.ds(16 * group, 16)], x_ref.at[pl.ds(16 * group, 16)], x_sem.at[group])
        for group in range(groups)
    ]
    for copy in copies:
        copy.start()
    table_copy = pltpu.make_async_copy(table_hbm, table_ref, small_sem.at[0])
    width_copy = pltpu.make_async_copy(width_hbm, width_ref, small_sem.at[1])
    table_copy.start()
    width_copy.start()
    lane = lane_index(blocks)
    flat = normal.reshape(channels * stride, LANES)
    clear_tail(normal, range(3, channels, 4), blocks)
    clear_tail(inner, range(ROWS), blocks)
    for ref in (quads, eights, sixteens, halves):
        clear_tail(ref, range(ROWS), blocks)

    def row_of(ref, row):
        return ref[row, 0:blocks, :]

    for group in range(groups):
        rows = slice(16 * group, 16 * group + 16)

        def piece(block):
            return x_ref[rows, block * LANES : (block + 1) * LANES].astype(jnp.float32)

        copies[group].wait()
        total = spread_sum(piece(block) for block in range(blocks))
        centre = jnp.sum(total, axis=1, keepdims=True) / length
        centre = jnp.broadcast_to(centre, (16, LANES))
        total = spread_sum(jnp.square(piece(block) - centre) for block in range(blocks))
        spread = jnp.sum(total, axis=1, keepdims=True) / length
        gain = jnp.broadcast_to(lax.rsqrt(spread + epsilon), (16, LANES))
        for block in range(blocks):
            value = (piece(block) - centre) * gain
            for half in range(2):
                start = (16 * group + 8 * half) * stride + block
                flat[pl.ds(start, 8, stride=stride), :] = value[8 * half : 8 * half + 8]
    table_copy.wait()
    width_copy.wait()

    shift = table_ref[0]
    partial = []
    for quad in range(ROWS):
        pair = row_of(normal, 4 * quad + 1) + row_of(normal, 4 * quad + 2)
        inner[quad, 0:blocks, :] = pair + later(normal, 4 * quad + 3, blocks, lane, shift)
        partial.append(pair + (row_of(normal, 4 * quad) + row_of(normal, 4 * quad + 3)))
    partial = spread_sum(partial)
    for row in (3, 7, 11, 15, 20):
        rows_ref[row] = partial
    for quad in range(ROWS):
        quads[quad, 0:blocks, :] = row_of(normal, 4 * quad) + later(inner, quad, blocks, lane, shift)
    bands, trials = ROWS, 1
    for source, target in ((quads, eights), (eights, sixteens), (sixteens, halves)):
        fresh = 2 * trials
        for trial in range(fresh):
            shift = table_ref[fresh - 1 + trial]
            for band in range(bands // 2):
                high = later(source, (2 * band + 1) * trials + trial // 2, blocks, lane, shift)
                value = row_of(source, 2 * band * trials + trial // 2) + high
                target[band * fresh + trial, 0:blocks, :] = value
        bands, trials = bands // 2, fresh
    mine = reverse4(lax.axis_index("chan") & 15)
    for trial in range(ROWS):
        high = later(halves, 8 + trial // 2, blocks, lane, table_ref[ROWS - 1 + trial])
        place = mine ^ trial
        group, low = place >> 2, place & 3
        spot = jnp.where(low == 1, ROWS + group, place - (low > 0))
        rows_ref[spot] = row_of(halves, trial // 2) + high
    small_lane = lax.broadcasted_iota(jnp.int32, words_ref.shape, 1)
    words = jnp.zeros(words_ref.shape, jnp.int32)
    for index, word in enumerate(packed_words(table_ref, width_ref, mine)):
        words = jnp.where(small_lane == index, word, words)
    words_ref[...] = words


def local_rows(filterbank, shift_table, box_widths):
    channels, length = filterbank.shape
    blocks = length // LANES
    hbm = pl.BlockSpec(memory_space=pltpu.HBM)
    vmem = pl.BlockSpec(memory_space=pltpu.VMEM)
    inputs = [pltpu.with_memory_space_constraint(value, pltpu.HBM) for value in (shift_table, box_widths, filterbank)]
    return pl.pallas_call(
        local_kernel,
        out_shape=(
            jax.ShapeDtypeStruct((ROWS + 5, blocks, LANES), jnp.float32),
            jax.ShapeDtypeStruct((8, LANES), jnp.int32),
        ),
        in_specs=[hbm] * 3,
        out_specs=(vmem, vmem),
        scratch_shapes=[
            pltpu.SMEM(shift_table.shape, jnp.int32),
            pltpu.SMEM(box_widths.shape, jnp.int32),
            pltpu.VMEM(filterbank.shape, filterbank.dtype),
            pltpu.VMEM((channels, blocks + PAD, LANES), jnp.float32),
            *[row_scratch(blocks)] * 5,
            pltpu.SemaphoreType.DMA((2,)),
            pltpu.SemaphoreType.DMA((channels // 16,)),
        ],
        compiler_params=pltpu.CompilerParams(vmem_limit_bytes=32 << 20),
        name="local_tree",
    )(*inputs)


def mean_path(mean, word, scratch, blocks, lane, row):
    value = mean
    for step in range(0, len(PATH), 2):
        shifts = []
        for trials, spot in PATH[step : step + 2]:
            index = row >> (ROWS // trials).bit_length() - 1
            shifts.append(2 * index + (word >> spot & 1))
        scratch[step, 0:blocks, :] = value
        near, far = shifts
        value = (value + later(scratch, step, blocks, lane, near)) + (
            later(scratch, step, blocks, lane, far) + later(scratch, step, blocks, lane, near + far)
        )
    return value


def cross_tree(me, mean, words, buffers, spare, blocks, lane):
    row = reverse4(me & 15)
    path, cross = words[0], words[1]
    mean = mean_path(mean, path, spare, blocks, lane, row)
    spare[ROWS - 1, 0:blocks, :] = mean
    bands, trials = ROWS, 1
    spot = 0
    for source, target in zip(buffers[:-1], buffers[1:]):
        fresh = 2 * trials
        for trial in range(fresh):
            shift = 2 * (row * fresh + trial) + (cross >> spot & 1)
            spot += 1
            old = trial // 2
            if bands == ROWS:
                taken = mean + later(spare, ROWS - 1, blocks, lane, shift)
            for band in range(bands // 2):
                high = later(source, (2 * band + 1) * trials + old, blocks, lane, shift)
                value = source[2 * band * trials + old, 0:blocks, :] + high
                if bands == ROWS:
                    value = value - taken
                target[band * fresh + trial, 0:blocks, :] = value
        bands, trials = bands // 2, fresh
    return buffers[-1]


def finish(rows, widths, out_ref, peaks_ref, prefix, split):
    stride = rows.shape[1]
    blocks = stride - PAD
    length = blocks * LANES
    lane = lax.broadcasted_iota(jnp.int32, (ROWS, LANES), 1)
    flat = rows.reshape(ROWS * stride, LANES)

    total = jnp.zeros((ROWS, LANES), jnp.float32)
    for block in range(blocks):
        value = jnp.concatenate(
            [flat[pl.ds(block + 8 * half * stride, 8, stride=stride), :] for half in range(2)], axis=0
        )
        prefix[2 + block] = value
        total = total + value
    centre = jnp.sum(total, axis=1, keepdims=True) / length
    centre = jnp.broadcast_to(centre, (ROWS, LANES))
    total = jnp.zeros((ROWS, LANES), jnp.float32)
    for block in range(blocks):
        total = total + jnp.square(prefix[2 + block] - centre)
    spread = jnp.sum(total, axis=1, keepdims=True) / length
    gain = jnp.broadcast_to(lax.rsqrt(spread + epsilon), (ROWS, LANES))
    for block in range(blocks):
        value = (prefix[2 + block] - centre) * gain
        rounded = value.astype(jnp.bfloat16)
        out_ref[:, pl.ds(block * LANES, LANES)] = rounded
        split[pl.ds(block * ROWS, ROWS), pl.ds(0, LANES)] = rounded
        rest = value - rounded.astype(jnp.float32)
        split[pl.ds(block * ROWS, ROWS), pl.ds(LANES, LANES)] = rest.astype(jnp.bfloat16)

    above = lax.broadcasted_iota(jnp.int32, (2 * LANES, 2 * LANES), 0) & 127
    across = lax.broadcasted_iota(jnp.int32, (2 * LANES, 2 * LANES), 1)
    weights = jnp.where(above <= across, 1.0, 0.0).astype(jnp.bfloat16)
    sums = jnp.dot(split[...], weights, preferred_element_type=jnp.float32)
    carry = jnp.zeros((ROWS, LANES), jnp.float32)
    prefix[0] = carry
    prefix[1] = carry
    for block in range(blocks):
        part = sums[block * ROWS : (block + 1) * ROWS]
        prefix[2 + block] = part[:, :LANES] + carry
        carry = carry + part[:, LANES:]

    peaks = jnp.zeros((ROWS, LANES), jnp.float32)
    backs = [2 * LANES - width for width in widths]
    heres = [prefix[back >> 7] for back in backs]
    best = [None] * len(widths)
    for block in range(blocks):
        now = prefix[2 + block]
        for index, back in enumerate(backs):
            beyond = prefix[(back >> 7) + block + 1]
            gap = now - moved(heres[index], beyond, lane, back & 127)
            best[index] = gap if best[index] is None else jnp.maximum(best[index], gap)
            heres[index] = beyond
    for index, width in enumerate(widths):
        peak = jnp.max(best[index], axis=1, keepdims=True)
        scale = lax.rsqrt(jnp.full((ROWS, LANES), width, jnp.int32).astype(jnp.float32))
        peaks = jnp.where(lane == index, peak * scale, peaks)
    peaks_ref[...] = jnp.transpose(peaks)[: len(widths)]


def cross_kernel(
    channels, count, finishing, words_ref,
    own_ref, core_ref, x_ref, both_ref, z1_ref, z3_ref, z2_ref, pc_ref, px_ref, pb_ref, mean_ref,
    *rest,
):
    blocks = own_ref.shape[1]
    lane = lane_index(blocks)
    if finishing:
        out_ref, peaks_ref, spare, *buffers, prefix, split = rest
    else:
        series_ref, spare, *buffers = rest
    words = [words_ref[0, index] for index in range(2 + WIDTHS // 4)]
    for ref in (spare, *buffers):
        clear_tail(ref, range(ROWS), blocks)
    first = buffers[0]
    me = lax.axis_index("chan")
    here = me & 15

    def place(offset, value):
        first[here ^ offset, pl.ds(0, blocks), :] = value

    place(0, own_ref[0])
    place(1, core_ref[0])
    place(2, x_ref[0])
    place(3, both_ref[0])
    for step, ref in ((1, z1_ref), (3, z3_ref)):
        for inner in range(4):
            place(4 * step + inner, ref[inner])
    for inner, ref in enumerate((z2_ref, pc_ref, px_ref, pb_ref)):
        place(8 + inner, ref[0])
    mean = mean_ref[0]
    if finishing:
        mean = mean + z1_ref[4] + z3_ref[4] + pc_ref[1] + px_ref[1] + pb_ref[1]
    mean = mean / (channels * count)
    rows = cross_tree(me, mean, words, buffers, spare, blocks, lane)
    if finishing:
        finish(rows, unpacked_widths(words), out_ref, peaks_ref, prefix, split)
    else:
        for trial in range(ROWS):
            series_ref[trial] = rows[trial, pl.ds(0, blocks), :]


def unpacked_widths(words):
    return [words[2 + index // 4] >> 8 * (index % 4) & 255 for index in range(WIDTHS)]


def finish_kernel(words_ref, series_ref, out_ref, peaks_ref, rows, *scratch):
    blocks = series_ref.shape[1]
    words = [words_ref[0, index] for index in range(2 + WIDTHS // 4)]
    for trial in range(ROWS):
        rows[trial, pl.ds(0, blocks), :] = series_ref[trial]
    finish(rows, unpacked_widths(words), out_ref, peaks_ref, *scratch)


def row_scratch(blocks):
    return pltpu.VMEM((ROWS, blocks + PAD, LANES), jnp.float32)


def finish_scratch(blocks):
    return [
        pltpu.VMEM((blocks + 2, ROWS, LANES), jnp.float32),
        pltpu.VMEM((blocks * ROWS, 2 * LANES), jnp.bfloat16),
    ]


def final_shapes(blocks):
    return (
        jax.ShapeDtypeStruct((ROWS, blocks * LANES), jnp.bfloat16),
        jax.ShapeDtypeStruct((WIDTHS, ROWS), jnp.float32),
    )


def swapped(block, distance):
    count = lax.axis_size("chan")
    return lax.ppermute(block, "chan", [(device, device ^ distance) for device in range(count)])


def advance(rows_in, shifts, start):
    count, length = rows_in.shape
    padded = jnp.concatenate([rows_in, jnp.zeros_like(rows_in)], axis=1)
    moved = lax.dynamic_slice_in_dim(padded, jnp.minimum(2 * start, length), length, 1)
    moved = jnp.concatenate([moved, jnp.zeros((count, 2 * count), moved.dtype)], axis=1)
    width = length + 2 * count
    flat = jnp.concatenate([moved.reshape(-1), jnp.zeros((2 * count,), moved.dtype)])
    skewed = flat.reshape(count, width + 2)[:, :length]
    odd = jnp.concatenate([skewed[:, 1:], jnp.zeros((count, 1), moved.dtype)], axis=1)
    parity = shifts - 2 * (start + jnp.arange(count, dtype=jnp.int32))
    return jnp.where((parity == 1)[:, None], odd, skewed)


def wider_sections(current, shift_table, me, section_count):
    half = ROWS // 2
    position = reverse4(me % 16)
    for bit in range(4, section_count):
        side = me >> bit & 1
        trials_now = 2 * ROWS << bit
        theirs = lax.dynamic_slice_in_dim(current, (1 - side) * half, half, 0)
        ours = lax.dynamic_slice_in_dim(current, side * half, half, 0)
        arrived = swapped(theirs, 1 << bit)
        lower = jnp.where(side == 0, ours, arrived)
        upper = jnp.where(side == 0, arrived, ours)
        first_trial = 2 * (position * ROWS + side * half)
        shifts = lax.dynamic_slice_in_dim(shift_table, trials_now - 1 + first_trial, ROWS)
        current = jnp.repeat(lower, 2, axis=0) + advance(jnp.repeat(upper, 2, axis=0), shifts, first_trial)
        position = 2 * position + side
    return current


def shards(filterbank, shift_table, box_widths):
    channels, length = filterbank.shape
    blocks = length // LANES
    count = lax.axis_size("chan")
    section_count = count.bit_length() - 1
    rows, words = local_rows(filterbank, shift_table, box_widths)
    small = section_count == 4

    across = swapped(rows[4:8], 2)
    both = swapped(rows[12:16], 3)
    core = swapped(rows[8:12], 1)
    z2 = swapped(rows[16:], 8)
    plane = (rows, core, across, both)
    mean = sum(part[3:4] for part in plane)
    z1 = swapped(jnp.concatenate([part[1:2] for part in plane] + [mean], axis=0), 4)
    z3 = swapped(jnp.concatenate([part[2:3] for part in plane] + [mean], axis=0), 12)
    passed = [
        swapped(jnp.concatenate([z2[place : place + 1], z2[4:]], axis=0), offset)
        for offset, place in ((1, 2), (2, 1), (3, 3))
    ]
    mean = mean + z2[4:]
    arrived = [z1, z3, z2, *passed]
    if not small:
        mean = lax.psum(rows[3:4], "chan")

    vmem = pl.BlockSpec(memory_space=pltpu.VMEM)
    params = pltpu.CompilerParams(vmem_limit_bytes=32 << 20)
    call = pl.pallas_call(
        functools.partial(cross_kernel, channels, count, small),
        out_shape=final_shapes(blocks)
        if small
        else jax.ShapeDtypeStruct((ROWS, blocks, LANES), jnp.float32),
        in_specs=[vmem] * 12,
        out_specs=(vmem, vmem) if small else vmem,
        scratch_shapes=[
            *[row_scratch(blocks)] * 6,
            *(finish_scratch(blocks) if small else []),
        ],
        compiler_params=params,
        name="cross_tree",
    )
    result = call(words, *plane, *arrived, mean)
    if small:
        return tuple(result)
    me = lax.axis_index("chan")
    current = wider_sections(result.reshape(ROWS, length), shift_table, me, section_count)
    return tuple(
        pl.pallas_call(
            finish_kernel,
            out_shape=final_shapes(blocks),
            in_specs=[vmem, vmem],
            out_specs=(vmem, vmem),
            scratch_shapes=[row_scratch(blocks)] + finish_scratch(blocks),
            compiler_params=params,
            name="finish",
        )(words, current.reshape(ROWS, blocks, LANES))
    )


def solution(mesh):
    placed = (P(("beam", "chan"), None), P(), P())
    return jax.shard_map(
        shards,
        mesh=mesh,
        in_specs=placed,
        out_specs=(P(("beam", "chan"), None), P("beam", "chan")),
        check_vma=False,
    )
```

```python
import functools

import jax
import jax.numpy as jnp
from jax import lax
from jax.experimental import pallas as pl
from jax.experimental.pallas import tpu as pltpu
from jax.sharding import PartitionSpec as P

ROWS = 16
LANES = 128
PAD = 8
WIDTHS = 8
EARLY = (4, 12)
LATE = tuple(step for step in (4, 8, 12) if step not in EARLY)
SPAN = len(LATE) + 2
LOW = {4: 2, 8: 1, 12: 3}
SPOTS = {LOW[step]: (1 + index, SPAN) for index, step in enumerate(LATE)}
SPOTS.update({LOW[step]: (4 * SPAN + 5 * index, 1) for index, step in enumerate(EARLY)})
MEAN_ROWS = [SPAN * group + SPAN - 1 for group in range(4)] + [4 * SPAN + 5 * index + 4 for index in range(len(EARLY))]
PATH = ((1, 0), (1, 1), (2, 2), (4, 3), (8, 4), (16, 5))

epsilon = 1e-05


def reverse4(value):
    return (value & 1) << 3 | (value & 2) << 1 | (value & 4) >> 1 | (value & 8) >> 3


def lane_index(blocks):
    return lax.broadcasted_iota(jnp.int32, (blocks, LANES), 1)


def moved(here, beyond, lane, part):
    return pltpu.roll(jnp.where(lane >= part, here, beyond), (LANES - part) & 127, axis=1)


def later(ref, row, blocks, lane, shift):
    whole = shift >> 7
    here = ref[row, pl.ds(whole, blocks), :]
    beyond = ref[row, pl.ds(whole + 1, blocks), :]
    return moved(here, beyond, lane, shift & 127)


def clear_tail(ref, rows, blocks):
    for row in rows:
        ref[row, blocks : blocks + PAD, :] = jnp.zeros((PAD, LANES), jnp.float32)


def spread_sum(terms):
    strands = [None] * 4
    for index, term in enumerate(terms):
        strand = strands[index % 4]
        strands[index % 4] = term if strand is None else strand + term
    return (strands[0] + strands[1]) + (strands[2] + strands[3])


def packed_words(table_ref, width_ref, row):
    path, cross = jnp.int32(0), jnp.int32(0)
    spot = 0
    for trials, _ in PATH:
        index = row >> (ROWS // trials).bit_length() - 1
        path = path | (table_ref[trials - 1 + index] - 2 * index) << spot
        spot += 1
    spot = 0
    for fresh in (2, 4, 8, 16):
        for trial in range(fresh):
            index = row * fresh + trial
            cross = cross | (table_ref[ROWS * fresh - 1 + index] - 2 * index) << spot
            spot += 1
    words = [path, cross]
    for start in range(0, WIDTHS, 4):
        word = jnp.int32(0)
        for place in range(4):
            word = word | width_ref[start + place] << 8 * place
        words.append(word)
    return words


def local_kernel(
    table_hbm, width_hbm, x_hbm, rows_ref, words_ref,
    table_ref, width_ref, x_ref, normal, inner, quads, eights, sixteens, halves, small_sem, x_sem,
):
    channels, length = x_ref.shape
    blocks = length // LANES
    stride = blocks + PAD
    groups = channels // 16
    copies = [
        pltpu.make_async_copy(x_hbm.at[pl.ds(16 * group, 16)], x_ref.at[pl.ds(16 * group, 16)], x_sem.at[group])
        for group in range(groups)
    ]
    for copy in copies:
        copy.start()
    table_copy = pltpu.make_async_copy(table_hbm, table_ref, small_sem.at[0])
    width_copy = pltpu.make_async_copy(width_hbm, width_ref, small_sem.at[1])
    table_copy.start()
    width_copy.start()
    lane = lane_index(blocks)
    flat = normal.reshape(channels * stride, LANES)
    clear_tail(normal, range(3, channels, 4), blocks)
    clear_tail(inner, range(ROWS), blocks)
    for ref in (quads, eights, sixteens, halves):
        clear_tail(ref, range(ROWS), blocks)

    def row_of(ref, row):
        return ref[row, 0:blocks, :]

    for group in range(groups):
        rows = slice(16 * group, 16 * group + 16)

        def piece(block):
            return x_ref[rows, block * LANES : (block + 1) * LANES].astype(jnp.float32)

        copies[group].wait()
        total = spread_sum(piece(block) for block in range(blocks))
        centre = jnp.sum(total, axis=1, keepdims=True) / length
        centre = jnp.broadcast_to(centre, (16, LANES))
        total = spread_sum(jnp.square(piece(block) - centre) for block in range(blocks))
        spread = jnp.sum(total, axis=1, keepdims=True) / length
        gain = jnp.broadcast_to(lax.rsqrt(spread + epsilon), (16, LANES))
        for block in range(blocks):
            value = (piece(block) - centre) * gain
            for half in range(2):
                start = (16 * group + 8 * half) * stride + block
                flat[pl.ds(start, 8, stride=stride), :] = value[8 * half : 8 * half + 8]
    table_copy.wait()
    width_copy.wait()

    shift = table_ref[0]
    partial = []
    for quad in range(ROWS):
        pair = row_of(normal, 4 * quad + 1) + row_of(normal, 4 * quad + 2)
        inner[quad, 0:blocks, :] = pair + later(normal, 4 * quad + 3, blocks, lane, shift)
        partial.append(pair + (row_of(normal, 4 * quad) + row_of(normal, 4 * quad + 3)))
    partial = spread_sum(partial)
    for row in MEAN_ROWS:
        rows_ref[row] = partial
    for quad in range(ROWS):
        quads[quad, 0:blocks, :] = row_of(normal, 4 * quad) + later(inner, quad, blocks, lane, shift)
    bands, trials = ROWS, 1
    for source, target in ((quads, eights), (eights, sixteens), (sixteens, halves)):
        fresh = 2 * trials
        for trial in range(fresh):
            shift = table_ref[fresh - 1 + trial]
            for band in range(bands // 2):
                high = later(source, (2 * band + 1) * trials + trial // 2, blocks, lane, shift)
                value = row_of(source, 2 * band * trials + trial // 2) + high
                target[band * fresh + trial, 0:blocks, :] = value
        bands, trials = bands // 2, fresh
    mine = reverse4(lax.axis_index("chan") & 15)
    for trial in range(ROWS):
        high = later(halves, 8 + trial // 2, blocks, lane, table_ref[ROWS - 1 + trial])
        place = mine ^ trial
        group, low = place >> 2, place & 3
        spot = group * SPAN
        for other, (base, scale) in SPOTS.items():
            spot = jnp.where(low == other, base + scale * group, spot)
        rows_ref[spot] = row_of(halves, trial // 2) + high
    small_lane = lax.broadcasted_iota(jnp.int32, words_ref.shape, 1)
    words = jnp.zeros(words_ref.shape, jnp.int32)
    for index, word in enumerate(packed_words(table_ref, width_ref, mine)):
        words = jnp.where(small_lane == index, word, words)
    words_ref[...] = words


def local_rows(filterbank, shift_table, box_widths):
    channels, length = filterbank.shape
    blocks = length // LANES
    hbm = pl.BlockSpec(memory_space=pltpu.HBM)
    vmem = pl.BlockSpec(memory_space=pltpu.VMEM)
    inputs = [pltpu.with_memory_space_constraint(value, pltpu.HBM) for value in (shift_table, box_widths, filterbank)]
    return pl.pallas_call(
        local_kernel,
        out_shape=(
            jax.ShapeDtypeStruct((4 * SPAN + 5 * len(EARLY), blocks, LANES), jnp.float32),
            jax.ShapeDtypeStruct((8, LANES), jnp.int32),
        ),
        in_specs=[hbm] * 3,
        out_specs=(vmem, vmem),
        scratch_shapes=[
            pltpu.SMEM(shift_table.shape, jnp.int32),
            pltpu.SMEM(box_widths.shape, jnp.int32),
            pltpu.VMEM(filterbank.shape, filterbank.dtype),
            pltpu.VMEM((channels, blocks + PAD, LANES), jnp.float32),
            *[row_scratch(blocks)] * 5,
            pltpu.SemaphoreType.DMA((2,)),
            pltpu.SemaphoreType.DMA((channels // 16,)),
        ],
        compiler_params=pltpu.CompilerParams(vmem_limit_bytes=32 << 20),
        name="local_tree",
    )(*inputs)


def mean_path(mean, word, scratch, blocks, lane, row):
    value = mean
    for step in range(0, len(PATH), 2):
        shifts = []
        for trials, spot in PATH[step : step + 2]:
            index = row >> (ROWS // trials).bit_length() - 1
            shifts.append(2 * index + (word >> spot & 1))
        scratch[step, 0:blocks, :] = value
        near, far = shifts
        value = (value + later(scratch, step, blocks, lane, near)) + (
            later(scratch, step, blocks, lane, far) + later(scratch, step, blocks, lane, near + far)
        )
    return value


def cross_tree(me, mean, words, buffers, spare, blocks, lane):
    row = reverse4(me & 15)
    path, cross = words[0], words[1]
    mean = mean_path(mean, path, spare, blocks, lane, row)
    spare[ROWS - 1, 0:blocks, :] = mean
    bands, trials = ROWS, 1
    spot = 0
    for source, target in zip(buffers[:-1], buffers[1:]):
        fresh = 2 * trials
        for trial in range(fresh):
            shift = 2 * (row * fresh + trial) + (cross >> spot & 1)
            spot += 1
            old = trial // 2
            if bands == ROWS:
                taken = mean + later(spare, ROWS - 1, blocks, lane, shift)
            for band in range(bands // 2):
                high = later(source, (2 * band + 1) * trials + old, blocks, lane, shift)
                value = source[2 * band * trials + old, 0:blocks, :] + high
                if bands == ROWS:
                    value = value - taken
                target[band * fresh + trial, 0:blocks, :] = value
        bands, trials = bands // 2, fresh
    return buffers[-1]


def finish(rows, widths, out_ref, peaks_ref, prefix, split):
    stride = rows.shape[1]
    blocks = stride - PAD
    length = blocks * LANES
    lane = lax.broadcasted_iota(jnp.int32, (ROWS, LANES), 1)
    flat = rows.reshape(ROWS * stride, LANES)

    total = jnp.zeros((ROWS, LANES), jnp.float32)
    for block in range(blocks):
        value = jnp.concatenate(
            [flat[pl.ds(block + 8 * half * stride, 8, stride=stride), :] for half in range(2)], axis=0
        )
        prefix[2 + block] = value
        total = total + value
    centre = jnp.sum(total, axis=1, keepdims=True) / length
    centre = jnp.broadcast_to(centre, (ROWS, LANES))
    total = jnp.zeros((ROWS, LANES), jnp.float32)
    for block in range(blocks):
        total = total + jnp.square(prefix[2 + block] - centre)
    spread = jnp.sum(total, axis=1, keepdims=True) / length
    gain = jnp.broadcast_to(lax.rsqrt(spread + epsilon), (ROWS, LANES))
    for block in range(blocks):
        value = (prefix[2 + block] - centre) * gain
        rounded = value.astype(jnp.bfloat16)
        out_ref[:, pl.ds(block * LANES, LANES)] = rounded
        split[pl.ds(block * ROWS, ROWS), pl.ds(0, LANES)] = rounded
        rest = value - rounded.astype(jnp.float32)
        split[pl.ds(block * ROWS, ROWS), pl.ds(LANES, LANES)] = rest.astype(jnp.bfloat16)

    above = lax.broadcasted_iota(jnp.int32, (2 * LANES, 2 * LANES), 0) & 127
    across = lax.broadcasted_iota(jnp.int32, (2 * LANES, 2 * LANES), 1)
    weights = jnp.where(above <= across, 1.0, 0.0).astype(jnp.bfloat16)
    sums = jnp.dot(split[...], weights, preferred_element_type=jnp.float32)
    carry = jnp.zeros((ROWS, LANES), jnp.float32)
    prefix[0] = carry
    prefix[1] = carry
    for block in range(blocks):
        part = sums[block * ROWS : (block + 1) * ROWS]
        prefix[2 + block] = part[:, :LANES] + carry
        carry = carry + part[:, LANES:]

    peaks = jnp.zeros((ROWS, LANES), jnp.float32)
    backs = [2 * LANES - width for width in widths]
    heres = [prefix[back >> 7] for back in backs]
    best = [None] * len(widths)
    for block in range(blocks):
        now = prefix[2 + block]
        for index, back in enumerate(backs):
            beyond = prefix[(back >> 7) + block + 1]
            gap = now - moved(heres[index], beyond, lane, back & 127)
            best[index] = gap if best[index] is None else jnp.maximum(best[index], gap)
            heres[index] = beyond
    for index, width in enumerate(widths):
        peak = jnp.max(best[index], axis=1, keepdims=True)
        scale = lax.rsqrt(jnp.full((ROWS, LANES), width, jnp.int32).astype(jnp.float32))
        peaks = jnp.where(lane == index, peak * scale, peaks)
    peaks_ref[...] = jnp.transpose(peaks)[: len(widths)]


def cross_kernel(
    channels, count, finishing, words_ref, *rest,
):
    plane, rest = rest[:4], rest[4:]
    early, rest = rest[: len(EARLY)], rest[len(EARLY) :]
    late, rest = rest[: len(LATE)], rest[len(LATE) :]
    passed, (mean_ref, *rest) = rest[:3], rest[3:]
    blocks = mean_ref.shape[1]
    lane = lane_index(blocks)
    if finishing:
        out_ref, peaks_ref, spare, *buffers, prefix, split = rest
    else:
        series_ref, spare, *buffers = rest
    words = [words_ref[0, index] for index in range(2 + WIDTHS // 4)]
    for ref in (spare, *buffers):
        clear_tail(ref, range(ROWS), blocks)
    first = buffers[0]
    me = lax.axis_index("chan")
    here = me & 15

    def place(offset, value):
        first[here ^ offset, pl.ds(0, blocks), :] = value

    offsets = (0, 2, 1, 3)
    for group, offset in enumerate(offsets):
        place(offset, plane[group][0])
        for index, step in enumerate(LATE):
            place(step + offset, late[index][group])
        for index, step in enumerate(EARLY):
            place(step + offset, passed[group - 1][index] if group else early[index][0])
    mean = mean_ref[0]
    if finishing:
        for ref in late:
            mean = mean + ref[4]
        for ref in passed:
            mean = mean + ref[len(EARLY)]
    mean = mean / (channels * count)
    rows = cross_tree(me, mean, words, buffers, spare, blocks, lane)
    if finishing:
        finish(rows, unpacked_widths(words), out_ref, peaks_ref, prefix, split)
    else:
        for trial in range(ROWS):
            series_ref[trial] = rows[trial, pl.ds(0, blocks), :]


def unpacked_widths(words):
    return [words[2 + index // 4] >> 8 * (index % 4) & 255 for index in range(WIDTHS)]


def finish_kernel(words_ref, series_ref, out_ref, peaks_ref, rows, *scratch):
    blocks = series_ref.shape[1]
    words = [words_ref[0, index] for index in range(2 + WIDTHS // 4)]
    for trial in range(ROWS):
        rows[trial, pl.ds(0, blocks), :] = series_ref[trial]
    finish(rows, unpacked_widths(words), out_ref, peaks_ref, *scratch)


def row_scratch(blocks):
    return pltpu.VMEM((ROWS, blocks + PAD, LANES), jnp.float32)


def finish_scratch(blocks):
    return [
        pltpu.VMEM((blocks + 2, ROWS, LANES), jnp.float32),
        pltpu.VMEM((blocks * ROWS, 2 * LANES), jnp.bfloat16),
    ]


def final_shapes(blocks):
    return (
        jax.ShapeDtypeStruct((ROWS, blocks * LANES), jnp.bfloat16),
        jax.ShapeDtypeStruct((WIDTHS, ROWS), jnp.float32),
    )


def swapped(block, distance):
    count = lax.axis_size("chan")
    return lax.ppermute(block, "chan", [(device, device ^ distance) for device in range(count)])


def advance(rows_in, shifts, start):
    count, length = rows_in.shape
    padded = jnp.concatenate([rows_in, jnp.zeros_like(rows_in)], axis=1)
    moved = lax.dynamic_slice_in_dim(padded, jnp.minimum(2 * start, length), length, 1)
    moved = jnp.concatenate([moved, jnp.zeros((count, 2 * count), moved.dtype)], axis=1)
    width = length + 2 * count
    flat = jnp.concatenate([moved.reshape(-1), jnp.zeros((2 * count,), moved.dtype)])
    skewed = flat.reshape(count, width + 2)[:, :length]
    odd = jnp.concatenate([skewed[:, 1:], jnp.zeros((count, 1), moved.dtype)], axis=1)
    parity = shifts - 2 * (start + jnp.arange(count, dtype=jnp.int32))
    return jnp.where((parity == 1)[:, None], odd, skewed)


def wider_sections(current, shift_table, me, section_count):
    half = ROWS // 2
    position = reverse4(me % 16)
    for bit in range(4, section_count):
        side = me >> bit & 1
        trials_now = 2 * ROWS << bit
        theirs = lax.dynamic_slice_in_dim(current, (1 - side) * half, half, 0)
        ours = lax.dynamic_slice_in_dim(current, side * half, half, 0)
        arrived = swapped(theirs, 1 << bit)
        lower = jnp.where(side == 0, ours, arrived)
        upper = jnp.where(side == 0, arrived, ours)
        first_trial = 2 * (position * ROWS + side * half)
        shifts = lax.dynamic_slice_in_dim(shift_table, trials_now - 1 + first_trial, ROWS)
        current = jnp.repeat(lower, 2, axis=0) + advance(jnp.repeat(upper, 2, axis=0), shifts, first_trial)
        position = 2 * position + side
    return current


def shards(filterbank, shift_table, box_widths):
    channels, length = filterbank.shape
    blocks = length // LANES
    count = lax.axis_size("chan")
    section_count = count.bit_length() - 1
    rows, words = local_rows(filterbank, shift_table, box_widths)
    small = section_count == 4

    early = [swapped(rows[4 * SPAN + 5 * index : 4 * SPAN + 5 * index + 5], step) for index, step in enumerate(EARLY)]
    plane = [rows] + [
        swapped(rows[SPAN * group : SPAN * (group + 1)], offset) for group, offset in ((1, 2), (2, 1), (3, 3))
    ]
    mean = sum(part[SPAN - 1 : SPAN] for part in plane)
    late = [
        swapped(jnp.concatenate([part[1 + index : 2 + index] for part in plane] + [mean], axis=0), step)
        for index, step in enumerate(LATE)
    ]
    column = sum(part[4:] for part in early)
    passed = [
        swapped(jnp.concatenate([part[group : group + 1] for part in early] + [column], axis=0), offset)
        for group, offset in ((1, 2), (2, 1), (3, 3))
    ]
    mean = mean + column
    arrived = [*plane, *early, *late, *passed]
    if not small:
        mean = lax.psum(rows[SPAN - 1 : SPAN], "chan")

    vmem = pl.BlockSpec(memory_space=pltpu.VMEM)
    params = pltpu.CompilerParams(vmem_limit_bytes=32 << 20)
    call = pl.pallas_call(
        functools.partial(cross_kernel, channels, count, small),
        out_shape=final_shapes(blocks)
        if small
        else jax.ShapeDtypeStruct((ROWS, blocks, LANES), jnp.float32),
        in_specs=[vmem] * (len(arrived) + 2),
        out_specs=(vmem, vmem) if small else vmem,
        scratch_shapes=[
            *[row_scratch(blocks)] * 6,
            *(finish_scratch(blocks) if small else []),
        ],
        compiler_params=params,
        name="cross_tree",
    )
    result = call(words, *arrived, mean)
    if small:
        return tuple(result)
    me = lax.axis_index("chan")
    current = wider_sections(result.reshape(ROWS, length), shift_table, me, section_count)
    return tuple(
        pl.pallas_call(
            finish_kernel,
            out_shape=final_shapes(blocks),
            in_specs=[vmem, vmem],
            out_specs=(vmem, vmem),
            scratch_shapes=[row_scratch(blocks)] + finish_scratch(blocks),
            compiler_params=params,
            name="finish",
        )(words, current.reshape(ROWS, blocks, LANES))
    )


def solution(mesh):
    placed = (P(("beam", "chan"), None), P(), P())
    return jax.shard_map(
        shards,
        mesh=mesh,
        in_specs=placed,
        out_specs=(P(("beam", "chan"), None), P("beam", "chan")),
        check_vma=False,
    )
```

```python
import functools

import jax
import jax.numpy as jnp
from jax import lax
from jax.experimental import pallas as pl
from jax.experimental.pallas import tpu as pltpu
from jax.sharding import PartitionSpec as P

ROWS = 16
LANES = 128
PAD = 8
WIDTHS = 8
EARLY = (4, 12)
LATE = tuple(step for step in (4, 8, 12) if step not in EARLY)
SPAN = len(LATE) + 2
LOW = {4: 2, 8: 1, 12: 3}
SPOTS = {LOW[step]: (1 + index, SPAN) for index, step in enumerate(LATE)}
SPOTS.update({LOW[step]: (4 * SPAN + 5 * index, 1) for index, step in enumerate(EARLY)})
MEAN_ROWS = [SPAN * group + SPAN - 1 for group in range(4)] + [4 * SPAN + 5 * index + 4 for index in range(len(EARLY))]
PATH = ((1, 0), (1, 1), (2, 2), (4, 3), (8, 4), (16, 5))

epsilon = 1e-05


def reverse4(value):
    return (value & 1) << 3 | (value & 2) << 1 | (value & 4) >> 1 | (value & 8) >> 3


def lane_index(blocks):
    return lax.broadcasted_iota(jnp.int32, (blocks, LANES), 1)


def moved(here, beyond, lane, part):
    return pltpu.roll(jnp.where(lane >= part, here, beyond), (LANES - part) & 127, axis=1)


def later(ref, row, blocks, lane, shift):
    whole = shift >> 7
    here = ref[row, pl.ds(whole, blocks), :]
    beyond = ref[row, pl.ds(whole + 1, blocks), :]
    return moved(here, beyond, lane, shift & 127)


def clear_tail(ref, rows, blocks):
    for row in rows:
        ref[row, blocks : blocks + PAD, :] = jnp.zeros((PAD, LANES), jnp.float32)


def spread_sum(terms):
    strands = [None] * 4
    for index, term in enumerate(terms):
        strand = strands[index % 4]
        strands[index % 4] = term if strand is None else strand + term
    return (strands[0] + strands[1]) + (strands[2] + strands[3])


def packed_words(table_ref, width_ref, row):
    path, cross = jnp.int32(0), jnp.int32(0)
    spot = 0
    for trials, _ in PATH:
        index = row >> (ROWS // trials).bit_length() - 1
        path = path | (table_ref[trials - 1 + index] - 2 * index) << spot
        spot += 1
    spot = 0
    for fresh in (2, 4, 8, 16):
        for trial in range(fresh):
            index = row * fresh + trial
            cross = cross | (table_ref[ROWS * fresh - 1 + index] - 2 * index) << spot
            spot += 1
    words = [path, cross]
    for start in range(0, WIDTHS, 4):
        word = jnp.int32(0)
        for place in range(4):
            word = word | width_ref[start + place] << 8 * place
        words.append(word)
    return words


def local_kernel(
    table_hbm, width_hbm, x_hbm, rows_ref, words_ref,
    table_ref, width_ref, x_ref, normal, inner, quads, eights, sixteens, halves, small_sem, x_sem,
):
    channels, length = x_ref.shape
    blocks = length // LANES
    stride = blocks + PAD
    groups = channels // 16
    copies = [
        pltpu.make_async_copy(x_hbm.at[pl.ds(16 * group, 16)], x_ref.at[pl.ds(16 * group, 16)], x_sem.at[group])
        for group in range(groups)
    ]
    for copy in copies:
        copy.start()
    table_copy = pltpu.make_async_copy(table_hbm, table_ref, small_sem.at[0])
    width_copy = pltpu.make_async_copy(width_hbm, width_ref, small_sem.at[1])
    table_copy.start()
    width_copy.start()
    lane = lane_index(blocks)
    flat = normal.reshape(channels * stride, LANES)
    clear_tail(normal, range(3, channels, 4), blocks)
    clear_tail(inner, range(ROWS), blocks)
    for ref in (quads, eights, sixteens, halves):
        clear_tail(ref, range(ROWS), blocks)

    def row_of(ref, row):
        return ref[row, 0:blocks, :]

    for group in range(groups):
        rows = slice(16 * group, 16 * group + 16)

        def piece(block):
            return x_ref[rows, block * LANES : (block + 1) * LANES].astype(jnp.float32)

        copies[group].wait()
        total = spread_sum(piece(block) for block in range(blocks))
        centre = jnp.sum(total, axis=1, keepdims=True) / length
        centre = jnp.broadcast_to(centre, (16, LANES))
        total = spread_sum(jnp.square(piece(block) - centre) for block in range(blocks))
        spread = jnp.sum(total, axis=1, keepdims=True) / length
        gain = jnp.broadcast_to(lax.rsqrt(spread + epsilon), (16, LANES))
        for block in range(blocks):
            value = (piece(block) - centre) * gain
            for half in range(2):
                start = (16 * group + 8 * half) * stride + block
                flat[pl.ds(start, 8, stride=stride), :] = value[8 * half : 8 * half + 8]
    table_copy.wait()
    width_copy.wait()

    shift = table_ref[0]
    partial = []
    for quad in range(ROWS):
        pair = row_of(normal, 4 * quad + 1) + row_of(normal, 4 * quad + 2)
        inner[quad, 0:blocks, :] = pair + later(normal, 4 * quad + 3, blocks, lane, shift)
        partial.append(pair + (row_of(normal, 4 * quad) + row_of(normal, 4 * quad + 3)))
    partial = spread_sum(partial)
    for row in MEAN_ROWS:
        rows_ref[row] = partial
    for quad in range(ROWS):
        quads[quad, 0:blocks, :] = row_of(normal, 4 * quad) + later(inner, quad, blocks, lane, shift)
    bands, trials = ROWS, 1
    for source, target in ((quads, eights), (eights, sixteens), (sixteens, halves)):
        fresh = 2 * trials
        for trial in range(fresh):
            shift = table_ref[fresh - 1 + trial]
            for band in range(bands // 2):
                high = later(source, (2 * band + 1) * trials + trial // 2, blocks, lane, shift)
                value = row_of(source, 2 * band * trials + trial // 2) + high
                target[band * fresh + trial, 0:blocks, :] = value
        bands, trials = bands // 2, fresh
    mine = reverse4(lax.axis_index("chan") & 15)
    for trial in range(ROWS):
        high = later(halves, 8 + trial // 2, blocks, lane, table_ref[ROWS - 1 + trial])
        place = mine ^ trial
        group, low = place >> 2, place & 3
        spot = group * SPAN
        for other, (base, scale) in SPOTS.items():
            spot = jnp.where(low == other, base + scale * group, spot)
        rows_ref[spot] = row_of(halves, trial // 2) + high
    small_lane = lax.broadcasted_iota(jnp.int32, words_ref.shape, 1)
    words = jnp.zeros(words_ref.shape, jnp.int32)
    for index, word in enumerate(packed_words(table_ref, width_ref, mine)):
        words = jnp.where(small_lane == index, word, words)
    words_ref[...] = words


def local_rows(filterbank, shift_table, box_widths):
    channels, length = filterbank.shape
    blocks = length // LANES
    hbm = pl.BlockSpec(memory_space=pltpu.HBM)
    vmem = pl.BlockSpec(memory_space=pltpu.VMEM)
    inputs = [pltpu.with_memory_space_constraint(value, pltpu.HBM) for value in (shift_table, box_widths, filterbank)]
    return pl.pallas_call(
        local_kernel,
        out_shape=(
            jax.ShapeDtypeStruct((4 * SPAN + 5 * len(EARLY), blocks, LANES), jnp.float32),
            jax.ShapeDtypeStruct((8, LANES), jnp.int32),
        ),
        in_specs=[hbm] * 3,
        out_specs=(vmem, vmem),
        scratch_shapes=[
            pltpu.SMEM(shift_table.shape, jnp.int32),
            pltpu.SMEM(box_widths.shape, jnp.int32),
            pltpu.VMEM(filterbank.shape, filterbank.dtype),
            pltpu.VMEM((channels, blocks + PAD, LANES), jnp.float32),
            *[row_scratch(blocks)] * 5,
            pltpu.SemaphoreType.DMA((2,)),
            pltpu.SemaphoreType.DMA((channels // 16,)),
        ],
        compiler_params=pltpu.CompilerParams(vmem_limit_bytes=32 << 20),
        name="local_tree",
    )(*inputs)


def mean_path(mean, word, scratch, blocks, lane, row):
    value = mean
    for step in range(0, len(PATH), 2):
        shifts = []
        for trials, spot in PATH[step : step + 2]:
            index = row >> (ROWS // trials).bit_length() - 1
            shifts.append(2 * index + (word >> spot & 1))
        scratch[step, 0:blocks, :] = value
        near, far = shifts
        value = (value + later(scratch, step, blocks, lane, near)) + (
            later(scratch, step, blocks, lane, far) + later(scratch, step, blocks, lane, near + far)
        )
    return value


def cross_tree(me, mean, words, buffers, spare, blocks, lane):
    row = reverse4(me & 15)
    path, cross = words[0], words[1]
    mean = mean_path(mean, path, spare, blocks, lane, row)
    spare[ROWS - 1, 0:blocks, :] = mean
    bands, trials = ROWS, 1
    spot = 0
    for source, target in zip(buffers[:-1], buffers[1:]):
        fresh = 2 * trials
        for trial in range(fresh):
            shift = 2 * (row * fresh + trial) + (cross >> spot & 1)
            spot += 1
            old = trial // 2
            if bands == ROWS:
                taken = mean + later(spare, ROWS - 1, blocks, lane, shift)
            for band in range(bands // 2):
                high = later(source, (2 * band + 1) * trials + old, blocks, lane, shift)
                value = source[2 * band * trials + old, 0:blocks, :] + high
                if bands == ROWS:
                    value = value - taken
                target[band * fresh + trial, 0:blocks, :] = value
        bands, trials = bands // 2, fresh
    return buffers[-1]


def finish(rows, widths, out_ref, peaks_ref, values, prefix, split):
    stride = rows.shape[1]
    blocks = stride - PAD
    length = blocks * LANES
    lane = lax.broadcasted_iota(jnp.int32, (ROWS, LANES), 1)
    flat = rows.reshape(ROWS * stride, LANES)

    total = []
    for block in range(blocks):
        value = jnp.concatenate(
            [flat[pl.ds(block + 8 * half * stride, 8, stride=stride), :] for half in range(2)], axis=0
        )
        values[block] = value
        high = value.astype(jnp.bfloat16)
        rest = (value - high.astype(jnp.float32)).astype(jnp.bfloat16)
        split[pl.ds(block * ROWS, ROWS), pl.ds(0, LANES)] = high
        split[pl.ds(block * ROWS, ROWS), pl.ds(LANES, LANES)] = rest
        total.append(value)
    centre = jnp.sum(spread_sum(total), axis=1, keepdims=True) / length
    centre = jnp.broadcast_to(centre, (ROWS, LANES))
    above = lax.broadcasted_iota(jnp.int32, (2 * LANES, 2 * LANES), 0) & 127
    across = lax.broadcasted_iota(jnp.int32, (2 * LANES, 2 * LANES), 1)
    weights = jnp.where(above <= across, 1.0, 0.0).astype(jnp.bfloat16)
    sums = jnp.dot(split[...], weights, preferred_element_type=jnp.float32)
    carry = jnp.zeros((ROWS, LANES), jnp.float32)
    prefix[0] = carry
    prefix[1] = carry
    ramp = centre * (lane + 1).astype(jnp.float32)
    drop = centre * LANES
    for block in range(blocks):
        part = sums[block * ROWS : (block + 1) * ROWS]
        prefix[2 + block] = (part[:, :LANES] - ramp) + carry
        carry = carry + (part[:, LANES:] - drop)

    spread = spread_sum(jnp.square(values[block] - centre) for block in range(blocks))
    spread = jnp.sum(spread, axis=1, keepdims=True) / length
    gain = jnp.broadcast_to(lax.rsqrt(spread + epsilon), (ROWS, LANES))
    for block in range(blocks):
        out_ref[:, pl.ds(block * LANES, LANES)] = ((values[block] - centre) * gain).astype(jnp.bfloat16)

    peaks = jnp.zeros((ROWS, LANES), jnp.float32)
    backs = [2 * LANES - width for width in widths]
    heres = [prefix[back >> 7] for back in backs]
    best = [None] * len(widths)
    for block in range(blocks):
        now = prefix[2 + block]
        for index, back in enumerate(backs):
            beyond = prefix[(back >> 7) + block + 1]
            gap = now - moved(heres[index], beyond, lane, back & 127)
            best[index] = gap if best[index] is None else jnp.maximum(best[index], gap)
            heres[index] = beyond
    for index, width in enumerate(widths):
        peak = jnp.max(best[index], axis=1, keepdims=True)
        scale = gain * lax.rsqrt(jnp.full((ROWS, LANES), width, jnp.int32).astype(jnp.float32))
        peaks = jnp.where(lane == index, peak * scale, peaks)
    peaks_ref[...] = jnp.transpose(peaks)[: len(widths)]


def cross_kernel(
    channels, count, finishing, words_ref, *rest,
):
    plane, rest = rest[:4], rest[4:]
    early, rest = rest[: len(EARLY)], rest[len(EARLY) :]
    late, rest = rest[: len(LATE)], rest[len(LATE) :]
    passed, (mean_ref, *rest) = rest[:3], rest[3:]
    blocks = mean_ref.shape[1]
    lane = lane_index(blocks)
    if finishing:
        out_ref, peaks_ref, spare, *buffers, values, prefix, split = rest
    else:
        series_ref, spare, *buffers = rest
    words = [words_ref[0, index] for index in range(2 + WIDTHS // 4)]
    for ref in (spare, *buffers):
        clear_tail(ref, range(ROWS), blocks)
    first = buffers[0]
    me = lax.axis_index("chan")
    here = me & 15

    def place(offset, value):
        first[here ^ offset, pl.ds(0, blocks), :] = value

    offsets = (0, 2, 1, 3)
    for group, offset in enumerate(offsets):
        place(offset, plane[group][0])
        for index, step in enumerate(LATE):
            place(step + offset, late[index][group])
        for index, step in enumerate(EARLY):
            place(step + offset, passed[group - 1][index] if group else early[index][0])
    mean = mean_ref[0]
    if finishing:
        for ref in late:
            mean = mean + ref[4]
        for ref in passed:
            mean = mean + ref[len(EARLY)]
    mean = mean / (channels * count)
    rows = cross_tree(me, mean, words, buffers, spare, blocks, lane)
    if finishing:
        finish(rows, unpacked_widths(words), out_ref, peaks_ref, values, prefix, split)
    else:
        for trial in range(ROWS):
            series_ref[trial] = rows[trial, pl.ds(0, blocks), :]


def unpacked_widths(words):
    return [words[2 + index // 4] >> 8 * (index % 4) & 255 for index in range(WIDTHS)]


def finish_kernel(words_ref, series_ref, out_ref, peaks_ref, rows, *scratch):
    blocks = series_ref.shape[1]
    words = [words_ref[0, index] for index in range(2 + WIDTHS // 4)]
    for trial in range(ROWS):
        rows[trial, pl.ds(0, blocks), :] = series_ref[trial]
    finish(rows, unpacked_widths(words), out_ref, peaks_ref, *scratch)


def row_scratch(blocks):
    return pltpu.VMEM((ROWS, blocks + PAD, LANES), jnp.float32)


def finish_scratch(blocks):
    return [
        pltpu.VMEM((blocks, ROWS, LANES), jnp.float32),
        pltpu.VMEM((blocks + 2, ROWS, LANES), jnp.float32),
        pltpu.VMEM((blocks * ROWS, 2 * LANES), jnp.bfloat16),
    ]


def final_shapes(blocks):
    return (
        jax.ShapeDtypeStruct((ROWS, blocks * LANES), jnp.bfloat16),
        jax.ShapeDtypeStruct((WIDTHS, ROWS), jnp.float32),
    )


def swapped(block, distance):
    count = lax.axis_size("chan")
    return lax.ppermute(block, "chan", [(device, device ^ distance) for device in range(count)])


def advance(rows_in, shifts, start):
    count, length = rows_in.shape
    padded = jnp.concatenate([rows_in, jnp.zeros_like(rows_in)], axis=1)
    moved = lax.dynamic_slice_in_dim(padded, jnp.minimum(2 * start, length), length, 1)
    moved = jnp.concatenate([moved, jnp.zeros((count, 2 * count), moved.dtype)], axis=1)
    width = length + 2 * count
    flat = jnp.concatenate([moved.reshape(-1), jnp.zeros((2 * count,), moved.dtype)])
    skewed = flat.reshape(count, width + 2)[:, :length]
    odd = jnp.concatenate([skewed[:, 1:], jnp.zeros((count, 1), moved.dtype)], axis=1)
    parity = shifts - 2 * (start + jnp.arange(count, dtype=jnp.int32))
    return jnp.where((parity == 1)[:, None], odd, skewed)


def wider_sections(current, shift_table, me, section_count):
    half = ROWS // 2
    position = reverse4(me % 16)
    for bit in range(4, section_count):
        side = me >> bit & 1
        trials_now = 2 * ROWS << bit
        theirs = lax.dynamic_slice_in_dim(current, (1 - side) * half, half, 0)
        ours = lax.dynamic_slice_in_dim(current, side * half, half, 0)
        arrived = swapped(theirs, 1 << bit)
        lower = jnp.where(side == 0, ours, arrived)
        upper = jnp.where(side == 0, arrived, ours)
        first_trial = 2 * (position * ROWS + side * half)
        shifts = lax.dynamic_slice_in_dim(shift_table, trials_now - 1 + first_trial, ROWS)
        current = jnp.repeat(lower, 2, axis=0) + advance(jnp.repeat(upper, 2, axis=0), shifts, first_trial)
        position = 2 * position + side
    return current


def shards(filterbank, shift_table, box_widths):
    channels, length = filterbank.shape
    blocks = length // LANES
    count = lax.axis_size("chan")
    section_count = count.bit_length() - 1
    rows, words = local_rows(filterbank, shift_table, box_widths)
    small = section_count == 4

    early = [swapped(rows[4 * SPAN + 5 * index : 4 * SPAN + 5 * index + 5], step) for index, step in enumerate(EARLY)]
    plane = [rows] + [
        swapped(rows[SPAN * group : SPAN * (group + 1)], offset) for group, offset in ((1, 2), (2, 1), (3, 3))
    ]
    mean = sum(part[SPAN - 1 : SPAN] for part in plane)
    late = [
        swapped(jnp.concatenate([part[1 + index : 2 + index] for part in plane] + [mean], axis=0), step)
        for index, step in enumerate(LATE)
    ]
    column = sum(part[4:] for part in early)
    passed = [
        swapped(jnp.concatenate([part[group : group + 1] for part in early] + [column], axis=0), offset)
        for group, offset in ((1, 2), (2, 1), (3, 3))
    ]
    mean = mean + column
    arrived = [*plane, *early, *late, *passed]
    if not small:
        mean = lax.psum(rows[SPAN - 1 : SPAN], "chan")

    vmem = pl.BlockSpec(memory_space=pltpu.VMEM)
    params = pltpu.CompilerParams(vmem_limit_bytes=32 << 20)
    call = pl.pallas_call(
        functools.partial(cross_kernel, channels, count, small),
        out_shape=final_shapes(blocks)
        if small
        else jax.ShapeDtypeStruct((ROWS, blocks, LANES), jnp.float32),
        in_specs=[vmem] * (len(arrived) + 2),
        out_specs=(vmem, vmem) if small else vmem,
        scratch_shapes=[
            *[row_scratch(blocks)] * 6,
            *(finish_scratch(blocks) if small else []),
        ],
        compiler_params=params,
        name="cross_tree",
    )
    result = call(words, *arrived, mean)
    if small:
        return tuple(result)
    me = lax.axis_index("chan")
    current = wider_sections(result.reshape(ROWS, length), shift_table, me, section_count)
    return tuple(
        pl.pallas_call(
            finish_kernel,
            out_shape=final_shapes(blocks),
            in_specs=[vmem, vmem],
            out_specs=(vmem, vmem),
            scratch_shapes=[row_scratch(blocks)] + finish_scratch(blocks),
            compiler_params=params,
            name="finish",
        )(words, current.reshape(ROWS, blocks, LANES))
    )


def solution(mesh):
    placed = (P(("beam", "chan"), None), P(), P())
    return jax.shard_map(
        shards,
        mesh=mesh,
        in_specs=placed,
        out_specs=(P(("beam", "chan"), None), P("beam", "chan")),
        check_vma=False,
    )
```

```python
import functools

import jax
import jax.numpy as jnp
from jax import lax
from jax.experimental import pallas as pl
from jax.experimental.pallas import tpu as pltpu
from jax.sharding import PartitionSpec as P

ROWS = 16
LANES = 128
PAD = 8
WIDTHS = 8
EARLY = (4, 12)
LATE = tuple(step for step in (4, 8, 12) if step not in EARLY)
SPAN = len(LATE) + 2
LOW = {4: 2, 8: 1, 12: 3}
SPOTS = {LOW[step]: (1 + index, SPAN) for index, step in enumerate(LATE)}
SPOTS.update({LOW[step]: (4 * SPAN + 5 * index, 1) for index, step in enumerate(EARLY)})
MEAN_ROWS = [SPAN * group + SPAN - 1 for group in range(4)] + [4 * SPAN + 5 * index + 4 for index in range(len(EARLY))]
PATH = ((1, 0), (1, 1), (2, 2), (4, 3), (8, 4), (16, 5))

epsilon = 1e-05


def reverse4(value):
    return (value & 1) << 3 | (value & 2) << 1 | (value & 4) >> 1 | (value & 8) >> 3


def lane_index(blocks):
    return lax.broadcasted_iota(jnp.int32, (blocks, LANES), 1)


def moved(here, beyond, lane, part):
    return pltpu.roll(jnp.where(lane >= part, here, beyond), (LANES - part) & 127, axis=1)


def later(ref, blocks, lane, shift):
    whole = shift >> 7
    return moved(ref[pl.ds(whole, blocks), :], ref[pl.ds(whole + 1, blocks), :], lane, shift & 127)


def clear_tail(refs, blocks):
    for ref in refs:
        ref[blocks : blocks + PAD, :] = jnp.zeros((PAD, LANES), jnp.float32)


def rows_of(ref):
    return [ref.at[row] for row in range(ref.shape[0])]


def spread_sum(terms):
    strands = [None] * 4
    for index, term in enumerate(terms):
        strand = strands[index % 4]
        strands[index % 4] = term if strand is None else strand + term
    return (strands[0] + strands[1]) + (strands[2] + strands[3])


def packed_words(table_ref, width_ref, row):
    path, cross = jnp.int32(0), jnp.int32(0)
    spot = 0
    for trials, _ in PATH:
        index = row >> (ROWS // trials).bit_length() - 1
        path = path | (table_ref[trials - 1 + index] - 2 * index) << spot
        spot += 1
    spot = 0
    for fresh in (2, 4, 8, 16):
        for trial in range(fresh):
            index = row * fresh + trial
            cross = cross | (table_ref[ROWS * fresh - 1 + index] - 2 * index) << spot
            spot += 1
    words = [path, cross]
    for start in range(0, WIDTHS, 4):
        word = jnp.int32(0)
        for place in range(4):
            word = word | width_ref[start + place] << 8 * place
        words.append(word)
    return words


def local_kernel(
    table_hbm, width_hbm, x_hbm, rows_ref, words_ref,
    table_ref, width_ref, x_ref, normal, small_sem, x_sem, *single,
):
    channels, length = x_ref.shape
    blocks = length // LANES
    stride = blocks + PAD
    groups = channels // 16
    copies = [
        pltpu.make_async_copy(x_hbm.at[pl.ds(16 * group, 16)], x_ref.at[pl.ds(16 * group, 16)], x_sem.at[group])
        for group in range(groups)
    ]
    for copy in copies:
        copy.start()
    table_copy = pltpu.make_async_copy(table_hbm, table_ref, small_sem.at[0])
    width_copy = pltpu.make_async_copy(width_hbm, width_ref, small_sem.at[1])
    table_copy.start()
    width_copy.start()
    lane = lane_index(blocks)
    flat = normal.reshape(channels * stride, LANES)
    channel = rows_of(normal)
    inner, quads, eights, sixteens, halves = [single[ROWS * level : ROWS * (level + 1)] for level in range(5)]
    clear_tail(channel[3::4] + list(single), blocks)

    def row_of(refs, row):
        return refs[row][0:blocks, :]

    for group in range(groups):
        rows = slice(16 * group, 16 * group + 16)

        def piece(block):
            return x_ref[rows, block * LANES : (block + 1) * LANES].astype(jnp.float32)

        copies[group].wait()
        total = spread_sum(piece(block) for block in range(blocks))
        centre = jnp.sum(total, axis=1, keepdims=True) / length
        centre = jnp.broadcast_to(centre, (16, LANES))
        total = spread_sum(jnp.square(piece(block) - centre) for block in range(blocks))
        spread = jnp.sum(total, axis=1, keepdims=True) / length
        gain = jnp.broadcast_to(lax.rsqrt(spread + epsilon), (16, LANES))
        for block in range(blocks):
            value = (piece(block) - centre) * gain
            for half in range(2):
                start = (16 * group + 8 * half) * stride + block
                flat[pl.ds(start, 8, stride=stride), :] = value[8 * half : 8 * half + 8]
    table_copy.wait()
    width_copy.wait()

    shift = table_ref[0]
    partial = []
    for quad in range(ROWS):
        pair = row_of(channel, 4 * quad + 1) + row_of(channel, 4 * quad + 2)
        inner[quad][0:blocks, :] = pair + later(channel[4 * quad + 3], blocks, lane, shift)
        partial.append(pair + (row_of(channel, 4 * quad) + row_of(channel, 4 * quad + 3)))
    partial = spread_sum(partial)
    for row in MEAN_ROWS:
        rows_ref[row] = partial
    for quad in range(ROWS):
        quads[quad][0:blocks, :] = row_of(channel, 4 * quad) + later(inner[quad], blocks, lane, shift)
    bands, trials = ROWS, 1
    for source, target in ((quads, eights), (eights, sixteens), (sixteens, halves)):
        fresh = 2 * trials
        for trial in range(fresh):
            shift = table_ref[fresh - 1 + trial]
            for band in range(bands // 2):
                high = later(source[(2 * band + 1) * trials + trial // 2], blocks, lane, shift)
                value = row_of(source, 2 * band * trials + trial // 2) + high
                target[band * fresh + trial][0:blocks, :] = value
        bands, trials = bands // 2, fresh
    mine = reverse4(lax.axis_index("chan") & 15)
    for trial in range(ROWS):
        high = later(halves[8 + trial // 2], blocks, lane, table_ref[ROWS - 1 + trial])
        place = mine ^ trial
        group, low = place >> 2, place & 3
        spot = group * SPAN
        for other, (base, scale) in SPOTS.items():
            spot = jnp.where(low == other, base + scale * group, spot)
        rows_ref[spot] = row_of(halves, trial // 2) + high
    small_lane = lax.broadcasted_iota(jnp.int32, words_ref.shape, 1)
    words = jnp.zeros(words_ref.shape, jnp.int32)
    for index, word in enumerate(packed_words(table_ref, width_ref, mine)):
        words = jnp.where(small_lane == index, word, words)
    words_ref[...] = words


def local_rows(filterbank, shift_table, box_widths):
    channels, length = filterbank.shape
    blocks = length // LANES
    hbm = pl.BlockSpec(memory_space=pltpu.HBM)
    vmem = pl.BlockSpec(memory_space=pltpu.VMEM)
    inputs = [pltpu.with_memory_space_constraint(value, pltpu.HBM) for value in (shift_table, box_widths, filterbank)]
    return pl.pallas_call(
        local_kernel,
        out_shape=(
            jax.ShapeDtypeStruct((4 * SPAN + 5 * len(EARLY), blocks, LANES), jnp.float32),
            jax.ShapeDtypeStruct((8, LANES), jnp.int32),
        ),
        in_specs=[hbm] * 3,
        out_specs=(vmem, vmem),
        scratch_shapes=[
            pltpu.SMEM(shift_table.shape, jnp.int32),
            pltpu.SMEM(box_widths.shape, jnp.int32),
            pltpu.VMEM(filterbank.shape, filterbank.dtype),
            pltpu.VMEM((channels, blocks + PAD, LANES), jnp.float32),
            pltpu.SemaphoreType.DMA((2,)),
            pltpu.SemaphoreType.DMA((channels // 16,)),
            *[pltpu.VMEM((blocks + PAD, LANES), jnp.float32)] * 5 * ROWS,
        ],
        compiler_params=pltpu.CompilerParams(vmem_limit_bytes=32 << 20),
        name="local_tree",
    )(*inputs)


def mean_path(mean, word, scratch, blocks, lane, row):
    value = mean
    for step in range(0, len(PATH), 2):
        shifts = []
        for trials, spot in PATH[step : step + 2]:
            index = row >> (ROWS // trials).bit_length() - 1
            shifts.append(2 * index + (word >> spot & 1))
        ref = scratch[step // 2]
        ref[0:blocks, :] = value
        near, far = shifts
        value = (value + later(ref, blocks, lane, near)) + (
            later(ref, blocks, lane, far) + later(ref, blocks, lane, near + far)
        )
    return value


def cross_tree(me, mean, words, buffers, spare, blocks, lane):
    row = reverse4(me & 15)
    path, cross = words[0], words[1]
    mean = mean_path(mean, path, spare, blocks, lane, row)
    spare[3][0:blocks, :] = mean
    bands, trials = ROWS, 1
    spot = 0
    for source, target in zip(buffers[:-1], buffers[1:]):
        fresh = 2 * trials
        for trial in range(fresh):
            shift = 2 * (row * fresh + trial) + (cross >> spot & 1)
            spot += 1
            old = trial // 2
            if bands == ROWS:
                taken = mean + later(spare[3], blocks, lane, shift)
            for band in range(bands // 2):
                high = later(source[(2 * band + 1) * trials + old], blocks, lane, shift)
                value = source[2 * band * trials + old][0:blocks, :] + high
                if bands == ROWS:
                    value = value - taken
                target[band * fresh + trial][0:blocks, :] = value
        bands, trials = bands // 2, fresh


def finish(rows, widths, out_ref, peaks_ref, values, prefix, split):
    stride = rows.shape[1]
    blocks = stride - PAD
    length = blocks * LANES
    lane = lax.broadcasted_iota(jnp.int32, (ROWS, LANES), 1)
    flat = rows.reshape(ROWS * stride, LANES)

    total = []
    for block in range(blocks):
        value = jnp.concatenate(
            [flat[pl.ds(block + 8 * half * stride, 8, stride=stride), :] for half in range(2)], axis=0
        )
        values[block] = value
        high = value.astype(jnp.bfloat16)
        rest = (value - high.astype(jnp.float32)).astype(jnp.bfloat16)
        split[pl.ds(block * ROWS, ROWS), pl.ds(0, LANES)] = high
        split[pl.ds(block * ROWS, ROWS), pl.ds(LANES, LANES)] = rest
        total.append(value)
    centre = jnp.sum(spread_sum(total), axis=1, keepdims=True) / length
    centre = jnp.broadcast_to(centre, (ROWS, LANES))
    above = lax.broadcasted_iota(jnp.int32, (2 * LANES, 2 * LANES), 0) & 127
    across = lax.broadcasted_iota(jnp.int32, (2 * LANES, 2 * LANES), 1)
    weights = jnp.where(above <= across, 1.0, 0.0).astype(jnp.bfloat16)
    sums = jnp.dot(split[...], weights, preferred_element_type=jnp.float32)
    carry = jnp.zeros((ROWS, LANES), jnp.float32)
    prefix[0] = carry
    prefix[1] = carry
    ramp = centre * (lane + 1).astype(jnp.float32)
    drop = centre * LANES
    for block in range(blocks):
        part = sums[block * ROWS : (block + 1) * ROWS]
        prefix[2 + block] = (part[:, :LANES] - ramp) + carry
        carry = carry + (part[:, LANES:] - drop)

    spread = spread_sum(jnp.square(values[block] - centre) for block in range(blocks))
    spread = jnp.sum(spread, axis=1, keepdims=True) / length
    gain = jnp.broadcast_to(lax.rsqrt(spread + epsilon), (ROWS, LANES))
    for block in range(blocks):
        out_ref[:, pl.ds(block * LANES, LANES)] = ((values[block] - centre) * gain).astype(jnp.bfloat16)

    peaks = jnp.zeros((ROWS, LANES), jnp.float32)
    backs = [2 * LANES - width for width in widths]
    heres = [prefix[back >> 7] for back in backs]
    best = [None] * len(widths)
    for block in range(blocks):
        now = prefix[2 + block]
        for index, back in enumerate(backs):
            beyond = prefix[(back >> 7) + block + 1]
            gap = now - moved(heres[index], beyond, lane, back & 127)
            best[index] = gap if best[index] is None else jnp.maximum(best[index], gap)
            heres[index] = beyond
    for index, width in enumerate(widths):
        peak = jnp.max(best[index], axis=1, keepdims=True)
        scale = gain * lax.rsqrt(jnp.full((ROWS, LANES), width, jnp.int32).astype(jnp.float32))
        peaks = jnp.where(lane == index, peak * scale, peaks)
    peaks_ref[...] = jnp.transpose(peaks)[: len(widths)]


def cross_kernel(
    channels, count, finishing, words_ref, *rest,
):
    plane, rest = rest[:4], rest[4:]
    early, rest = rest[: len(EARLY)], rest[len(EARLY) :]
    late, rest = rest[: len(LATE)], rest[len(LATE) :]
    passed, (mean_ref, *rest) = rest[:3], rest[3:]
    blocks = mean_ref.shape[1]
    lane = lane_index(blocks)
    if finishing:
        out_ref, peaks_ref, first, final, *single, values, prefix, split = rest
    else:
        series_ref, first, final, *single = rest
    words = [words_ref[0, index] for index in range(2 + WIDTHS // 4)]
    spare, single = single[:4], single[4:]
    buffers = [rows_of(first), single[:ROWS], single[ROWS : 2 * ROWS], single[2 * ROWS :], rows_of(final)]
    clear_tail([*spare, *buffers[0], *single], blocks)
    me = lax.axis_index("chan")
    here = me & 15

    def place(offset, value):
        first[here ^ offset, pl.ds(0, blocks), :] = value

    offsets = (0, 2, 1, 3)
    for group, offset in enumerate(offsets):
        place(offset, plane[group][0])
        for index, step in enumerate(LATE):
            place(step + offset, late[index][group])
        for index, step in enumerate(EARLY):
            place(step + offset, passed[group - 1][index] if group else early[index][0])
    mean = mean_ref[0]
    if finishing:
        for ref in late:
            mean = mean + ref[4]
        for ref in passed:
            mean = mean + ref[len(EARLY)]
    mean = mean / (channels * count)
    cross_tree(me, mean, words, buffers, spare, blocks, lane)
    if finishing:
        finish(final, unpacked_widths(words), out_ref, peaks_ref, values, prefix, split)
    else:
        for trial in range(ROWS):
            series_ref[trial] = final[trial, pl.ds(0, blocks), :]


def unpacked_widths(words):
    return [words[2 + index // 4] >> 8 * (index % 4) & 255 for index in range(WIDTHS)]


def finish_kernel(words_ref, series_ref, out_ref, peaks_ref, rows, *scratch):
    blocks = series_ref.shape[1]
    words = [words_ref[0, index] for index in range(2 + WIDTHS // 4)]
    for trial in range(ROWS):
        rows[trial, pl.ds(0, blocks), :] = series_ref[trial]
    finish(rows, unpacked_widths(words), out_ref, peaks_ref, *scratch)


def row_scratch(blocks):
    return pltpu.VMEM((ROWS, blocks + PAD, LANES), jnp.float32)


def finish_scratch(blocks):
    return [
        pltpu.VMEM((blocks, ROWS, LANES), jnp.float32),
        pltpu.VMEM((blocks + 2, ROWS, LANES), jnp.float32),
        pltpu.VMEM((blocks * ROWS, 2 * LANES), jnp.bfloat16),
    ]


def final_shapes(blocks):
    return (
        jax.ShapeDtypeStruct((ROWS, blocks * LANES), jnp.bfloat16),
        jax.ShapeDtypeStruct((WIDTHS, ROWS), jnp.float32),
    )


def swapped(block, distance):
    count = lax.axis_size("chan")
    return lax.ppermute(block, "chan", [(device, device ^ distance) for device in range(count)])


def advance(rows_in, shifts, start):
    count, length = rows_in.shape
    padded = jnp.concatenate([rows_in, jnp.zeros_like(rows_in)], axis=1)
    moved = lax.dynamic_slice_in_dim(padded, jnp.minimum(2 * start, length), length, 1)
    moved = jnp.concatenate([moved, jnp.zeros((count, 2 * count), moved.dtype)], axis=1)
    width = length + 2 * count
    flat = jnp.concatenate([moved.reshape(-1), jnp.zeros((2 * count,), moved.dtype)])
    skewed = flat.reshape(count, width + 2)[:, :length]
    odd = jnp.concatenate([skewed[:, 1:], jnp.zeros((count, 1), moved.dtype)], axis=1)
    parity = shifts - 2 * (start + jnp.arange(count, dtype=jnp.int32))
    return jnp.where((parity == 1)[:, None], odd, skewed)


def wider_sections(current, shift_table, me, section_count):
    half = ROWS // 2
    position = reverse4(me % 16)
    for bit in range(4, section_count):
        side = me >> bit & 1
        trials_now = 2 * ROWS << bit
        theirs = lax.dynamic_slice_in_dim(current, (1 - side) * half, half, 0)
        ours = lax.dynamic_slice_in_dim(current, side * half, half, 0)
        arrived = swapped(theirs, 1 << bit)
        lower = jnp.where(side == 0, ours, arrived)
        upper = jnp.where(side == 0, arrived, ours)
        first_trial = 2 * (position * ROWS + side * half)
        shifts = lax.dynamic_slice_in_dim(shift_table, trials_now - 1 + first_trial, ROWS)
        current = jnp.repeat(lower, 2, axis=0) + advance(jnp.repeat(upper, 2, axis=0), shifts, first_trial)
        position = 2 * position + side
    return current


def shards(filterbank, shift_table, box_widths):
    channels, length = filterbank.shape
    blocks = length // LANES
    count = lax.axis_size("chan")
    section_count = count.bit_length() - 1
    rows, words = local_rows(filterbank, shift_table, box_widths)
    small = section_count == 4

    early = [swapped(rows[4 * SPAN + 5 * index : 4 * SPAN + 5 * index + 5], step) for index, step in enumerate(EARLY)]
    plane = [rows] + [
        swapped(rows[SPAN * group : SPAN * (group + 1)], offset) for group, offset in ((1, 2), (2, 1), (3, 3))
    ]
    mean = sum(part[SPAN - 1 : SPAN] for part in plane)
    late = [
        swapped(jnp.concatenate([part[1 + index : 2 + index] for part in plane] + [mean], axis=0), step)
        for index, step in enumerate(LATE)
    ]
    column = sum(part[4:] for part in early)
    passed = [
        swapped(jnp.concatenate([part[group : group + 1] for part in early] + [column], axis=0), offset)
        for group, offset in ((1, 2), (2, 1), (3, 3))
    ]
    mean = mean + column
    arrived = [*plane, *early, *late, *passed]
    if not small:
        mean = lax.psum(rows[SPAN - 1 : SPAN], "chan")

    vmem = pl.BlockSpec(memory_space=pltpu.VMEM)
    params = pltpu.CompilerParams(vmem_limit_bytes=32 << 20)
    call = pl.pallas_call(
        functools.partial(cross_kernel, channels, count, small),
        out_shape=final_shapes(blocks)
        if small
        else jax.ShapeDtypeStruct((ROWS, blocks, LANES), jnp.float32),
        in_specs=[vmem] * (len(arrived) + 2),
        out_specs=(vmem, vmem) if small else vmem,
        scratch_shapes=[
            *[row_scratch(blocks)] * 2,
            *[pltpu.VMEM((blocks + PAD, LANES), jnp.float32)] * (4 + 3 * ROWS),
            *(finish_scratch(blocks) if small else []),
        ],
        compiler_params=params,
        name="cross_tree",
    )
    result = call(words, *arrived, mean)
    if small:
        return tuple(result)
    me = lax.axis_index("chan")
    current = wider_sections(result.reshape(ROWS, length), shift_table, me, section_count)
    return tuple(
        pl.pallas_call(
            finish_kernel,
            out_shape=final_shapes(blocks),
            in_specs=[vmem, vmem],
            out_specs=(vmem, vmem),
            scratch_shapes=[row_scratch(blocks)] + finish_scratch(blocks),
            compiler_params=params,
            name="finish",
        )(words, current.reshape(ROWS, blocks, LANES))
    )


def solution(mesh):
    placed = (P(("beam", "chan"), None), P(), P())
    return jax.shard_map(
        shards,
        mesh=mesh,
        in_specs=placed,
        out_specs=(P(("beam", "chan"), None), P("beam", "chan")),
        check_vma=False,
    )
```

```python
import functools

import jax
import jax.numpy as jnp
from jax import lax
from jax.experimental import pallas as pl
from jax.experimental.pallas import tpu as pltpu
from jax.sharding import PartitionSpec as P

ROWS = 16
LANES = 128
PAD = 8
WIDTHS = 8
EARLY = (4, 12)
LATE = tuple(step for step in (4, 8, 12) if step not in EARLY)
SPAN = len(LATE) + 2
LOW = {4: 2, 8: 1, 12: 3}
SPOTS = {LOW[step]: (1 + index, SPAN) for index, step in enumerate(LATE)}
SPOTS.update({LOW[step]: (4 * SPAN + 5 * index, 1) for index, step in enumerate(EARLY)})
MEAN_ROWS = [SPAN * group + SPAN - 1 for group in range(4)] + [4 * SPAN + 5 * index + 4 for index in range(len(EARLY))]
PATH = ((1, 0), (1, 1), (2, 2), (4, 3), (8, 4), (16, 5))

epsilon = 1e-05


def reverse4(value):
    return (value & 1) << 3 | (value & 2) << 1 | (value & 4) >> 1 | (value & 8) >> 3


def lane_index(blocks):
    return lax.broadcasted_iota(jnp.int32, (blocks, LANES), 1)


def moved(here, beyond, lane, part):
    return pltpu.roll(jnp.where(lane >= part, here, beyond), (LANES - part) & 127, axis=1)


def later(ref, blocks, lane, shift):
    whole = shift >> 7
    return moved(ref[pl.ds(whole, blocks), :], ref[pl.ds(whole + 1, blocks), :], lane, shift & 127)


def clear_tail(refs, blocks):
    for ref in refs:
        ref[blocks : blocks + PAD, :] = jnp.zeros((PAD, LANES), jnp.float32)


def rows_of(ref):
    return [ref.at[row] for row in range(ref.shape[0])]


def spread_sum(terms):
    strands = [None] * 4
    for index, term in enumerate(terms):
        strand = strands[index % 4]
        strands[index % 4] = term if strand is None else strand + term
    return (strands[0] + strands[1]) + (strands[2] + strands[3])


def packed_words(table_ref, width_ref, row):
    path, cross = jnp.int32(0), jnp.int32(0)
    spot = 0
    for trials, _ in PATH:
        index = row >> (ROWS // trials).bit_length() - 1
        path = path | (table_ref[trials - 1 + index] - 2 * index) << spot
        spot += 1
    spot = 0
    for fresh in (2, 4, 8, 16):
        for trial in range(fresh):
            index = row * fresh + trial
            cross = cross | (table_ref[ROWS * fresh - 1 + index] - 2 * index) << spot
            spot += 1
    words = [path, cross]
    for start in range(0, WIDTHS, 4):
        word = jnp.int32(0)
        for place in range(4):
            word = word | width_ref[start + place] << 8 * place
        words.append(word)
    return words


def local_kernel(
    table_hbm, width_hbm, x_hbm, rows_ref, words_ref,
    table_ref, width_ref, x_ref, normal, small_sem, x_sem, *single,
):
    channels, length = x_ref.shape
    blocks = length // LANES
    stride = blocks + PAD
    groups = channels // 16
    copies = [
        pltpu.make_async_copy(x_hbm, x_ref, x_sem),
        pltpu.make_async_copy(table_hbm, table_ref, small_sem.at[0]),
        pltpu.make_async_copy(width_hbm, width_ref, small_sem.at[1]),
    ]
    for copy in copies:
        copy.start()
    lane = lane_index(blocks)
    flat = normal.reshape(channels * stride, LANES)
    channel = rows_of(normal)
    inner, quads, eights, sixteens, halves = [single[ROWS * level : ROWS * (level + 1)] for level in range(5)]
    clear_tail(channel[3::4] + list(single), blocks)

    def row_of(refs, row):
        return refs[row][0:blocks, :]

    for copy in copies:
        copy.wait()
    for group in range(groups):
        rows = slice(16 * group, 16 * group + 16)

        def piece(block):
            return x_ref[rows, block * LANES : (block + 1) * LANES].astype(jnp.float32)

        total = spread_sum(piece(block) for block in range(blocks))
        centre = jnp.sum(total, axis=1, keepdims=True) / length
        centre = jnp.broadcast_to(centre, (16, LANES))
        total = spread_sum(jnp.square(piece(block) - centre) for block in range(blocks))
        spread = jnp.sum(total, axis=1, keepdims=True) / length
        gain = jnp.broadcast_to(lax.rsqrt(spread + epsilon), (16, LANES))
        for block in range(blocks):
            value = (piece(block) - centre) * gain
            for half in range(2):
                start = (16 * group + 8 * half) * stride + block
                flat[pl.ds(start, 8, stride=stride), :] = value[8 * half : 8 * half + 8]
    shift = table_ref[0]
    partial = []
    for quad in range(ROWS):
        pair = row_of(channel, 4 * quad + 1) + row_of(channel, 4 * quad + 2)
        inner[quad][0:blocks, :] = pair + later(channel[4 * quad + 3], blocks, lane, shift)
        partial.append(pair + (row_of(channel, 4 * quad) + row_of(channel, 4 * quad + 3)))
    partial = spread_sum(partial)
    for row in MEAN_ROWS:
        rows_ref[row] = partial
    for quad in range(ROWS):
        quads[quad][0:blocks, :] = row_of(channel, 4 * quad) + later(inner[quad], blocks, lane, shift)
    bands, trials = ROWS, 1
    for source, target in ((quads, eights), (eights, sixteens), (sixteens, halves)):
        fresh = 2 * trials
        for trial in range(fresh):
            shift = table_ref[fresh - 1 + trial]
            for band in range(bands // 2):
                high = later(source[(2 * band + 1) * trials + trial // 2], blocks, lane, shift)
                value = row_of(source, 2 * band * trials + trial // 2) + high
                target[band * fresh + trial][0:blocks, :] = value
        bands, trials = bands // 2, fresh
    mine = reverse4(lax.axis_index("chan") & 15)
    for trial in range(ROWS):
        high = later(halves[8 + trial // 2], blocks, lane, table_ref[ROWS - 1 + trial])
        place = mine ^ trial
        group, low = place >> 2, place & 3
        spot = group * SPAN
        for other, (base, scale) in SPOTS.items():
            spot = jnp.where(low == other, base + scale * group, spot)
        rows_ref[spot] = row_of(halves, trial // 2) + high
    small_lane = lax.broadcasted_iota(jnp.int32, words_ref.shape, 1)
    words = jnp.zeros(words_ref.shape, jnp.int32)
    for index, word in enumerate(packed_words(table_ref, width_ref, mine)):
        words = jnp.where(small_lane == index, word, words)
    words_ref[...] = words


def local_rows(filterbank, shift_table, box_widths):
    channels, length = filterbank.shape
    blocks = length // LANES
    hbm = pl.BlockSpec(memory_space=pltpu.HBM)
    vmem = pl.BlockSpec(memory_space=pltpu.VMEM)
    inputs = [pltpu.with_memory_space_constraint(value, pltpu.HBM) for value in (shift_table, box_widths, filterbank)]
    return pl.pallas_call(
        local_kernel,
        out_shape=(
            jax.ShapeDtypeStruct((4 * SPAN + 5 * len(EARLY), blocks, LANES), jnp.float32),
            jax.ShapeDtypeStruct((8, LANES), jnp.int32),
        ),
        in_specs=[hbm] * 3,
        out_specs=(vmem, vmem),
        scratch_shapes=[
            pltpu.SMEM(shift_table.shape, jnp.int32),
            pltpu.SMEM(box_widths.shape, jnp.int32),
            pltpu.VMEM(filterbank.shape, filterbank.dtype),
            pltpu.VMEM((channels, blocks + PAD, LANES), jnp.float32),
            pltpu.SemaphoreType.DMA((2,)),
            pltpu.SemaphoreType.DMA,
            *[pltpu.VMEM((blocks + PAD, LANES), jnp.float32)] * 5 * ROWS,
        ],
        compiler_params=pltpu.CompilerParams(vmem_limit_bytes=32 << 20),
        name="local_tree",
    )(*inputs)


def mean_path(mean, word, scratch, blocks, lane, row):
    value = mean
    for step in range(0, len(PATH), 2):
        shifts = []
        for trials, spot in PATH[step : step + 2]:
            index = row >> (ROWS // trials).bit_length() - 1
            shifts.append(2 * index + (word >> spot & 1))
        ref = scratch[step // 2]
        ref[0:blocks, :] = value
        near, far = shifts
        value = (value + later(ref, blocks, lane, near)) + (
            later(ref, blocks, lane, far) + later(ref, blocks, lane, near + far)
        )
    return value


def cross_tree(me, mean, words, buffers, spare, blocks, lane):
    row = reverse4(me & 15)
    path, cross = words[0], words[1]
    mean = mean_path(mean, path, spare, blocks, lane, row)
    spare[3][0:blocks, :] = mean
    bands, trials = ROWS, 1
    spot = 0
    for source, target in zip(buffers[:-1], buffers[1:]):
        fresh = 2 * trials
        for trial in range(fresh):
            shift = 2 * (row * fresh + trial) + (cross >> spot & 1)
            spot += 1
            old = trial // 2
            if bands == ROWS:
                taken = mean + later(spare[3], blocks, lane, shift)
            for band in range(bands // 2):
                high = later(source[(2 * band + 1) * trials + old], blocks, lane, shift)
                value = source[2 * band * trials + old][0:blocks, :] + high
                if bands == ROWS:
                    value = value - taken
                target[band * fresh + trial][0:blocks, :] = value
        bands, trials = bands // 2, fresh


def finish(rows, widths, out_ref, peaks_ref, values, prefix, split):
    stride = rows.shape[1]
    blocks = stride - PAD
    length = blocks * LANES
    lane = lax.broadcasted_iota(jnp.int32, (ROWS, LANES), 1)
    flat = rows.reshape(ROWS * stride, LANES)

    total = []
    for block in range(blocks):
        value = jnp.concatenate(
            [flat[pl.ds(block + 8 * half * stride, 8, stride=stride), :] for half in range(2)], axis=0
        )
        values[block] = value
        high = value.astype(jnp.bfloat16)
        rest = (value - high.astype(jnp.float32)).astype(jnp.bfloat16)
        split[pl.ds(block * ROWS, ROWS), pl.ds(0, LANES)] = high
        split[pl.ds(block * ROWS, ROWS), pl.ds(LANES, LANES)] = rest
        total.append(value)
    centre = jnp.sum(spread_sum(total), axis=1, keepdims=True) / length
    centre = jnp.broadcast_to(centre, (ROWS, LANES))
    above = lax.broadcasted_iota(jnp.int32, (2 * LANES, 2 * LANES), 0) & 127
    across = lax.broadcasted_iota(jnp.int32, (2 * LANES, 2 * LANES), 1)
    weights = jnp.where(above <= across, 1.0, 0.0).astype(jnp.bfloat16)
    sums = jnp.dot(split[...], weights, preferred_element_type=jnp.float32)
    carry = jnp.zeros((ROWS, LANES), jnp.float32)
    prefix[0] = carry
    prefix[1] = carry
    ramp = centre * (lane + 1).astype(jnp.float32)
    drop = centre * LANES
    for block in range(blocks):
        part = sums[block * ROWS : (block + 1) * ROWS]
        prefix[2 + block] = (part[:, :LANES] - ramp) + carry
        carry = carry + (part[:, LANES:] - drop)

    spread = spread_sum(jnp.square(values[block] - centre) for block in range(blocks))
    spread = jnp.sum(spread, axis=1, keepdims=True) / length
    gain = jnp.broadcast_to(lax.rsqrt(spread + epsilon), (ROWS, LANES))
    for block in range(blocks):
        out_ref[:, pl.ds(block * LANES, LANES)] = ((values[block] - centre) * gain).astype(jnp.bfloat16)

    peaks = jnp.zeros((ROWS, LANES), jnp.float32)
    backs = [2 * LANES - width for width in widths]
    heres = [prefix[back >> 7] for back in backs]
    best = [None] * len(widths)
    for block in range(blocks):
        now = prefix[2 + block]
        for index, back in enumerate(backs):
            beyond = prefix[(back >> 7) + block + 1]
            gap = now - moved(heres[index], beyond, lane, back & 127)
            best[index] = gap if best[index] is None else jnp.maximum(best[index], gap)
            heres[index] = beyond
    for index, width in enumerate(widths):
        peak = jnp.max(best[index], axis=1, keepdims=True)
        scale = gain * lax.rsqrt(jnp.full((ROWS, LANES), width, jnp.int32).astype(jnp.float32))
        peaks = jnp.where(lane == index, peak * scale, peaks)
    peaks_ref[...] = jnp.transpose(peaks)[: len(widths)]


def cross_kernel(
    channels, count, finishing, words_ref, *rest,
):
    plane, rest = rest[:4], rest[4:]
    early, rest = rest[: len(EARLY)], rest[len(EARLY) :]
    late, rest = rest[: len(LATE)], rest[len(LATE) :]
    passed, (mean_ref, *rest) = rest[:3], rest[3:]
    blocks = mean_ref.shape[1]
    lane = lane_index(blocks)
    if finishing:
        out_ref, peaks_ref, first, final, *single, values, prefix, split = rest
    else:
        series_ref, first, final, *single = rest
    words = [words_ref[0, index] for index in range(2 + WIDTHS // 4)]
    spare, single = single[:4], single[4:]
    buffers = [rows_of(first), single[:ROWS], single[ROWS : 2 * ROWS], single[2 * ROWS :], rows_of(final)]
    clear_tail([*spare, *buffers[0], *single], blocks)
    me = lax.axis_index("chan")
    here = me & 15

    def place(offset, value):
        first[here ^ offset, pl.ds(0, blocks), :] = value

    offsets = (0, 2, 1, 3)
    for group, offset in enumerate(offsets):
        place(offset, plane[group][0])
        for index, step in enumerate(LATE):
            place(step + offset, late[index][group])
        for index, step in enumerate(EARLY):
            place(step + offset, passed[group - 1][index] if group else early[index][0])
    mean = mean_ref[0]
    if finishing:
        for ref in late:
            mean = mean + ref[4]
        for ref in passed:
            mean = mean + ref[len(EARLY)]
    mean = mean / (channels * count)
    cross_tree(me, mean, words, buffers, spare, blocks, lane)
    if finishing:
        finish(final, unpacked_widths(words), out_ref, peaks_ref, values, prefix, split)
    else:
        for trial in range(ROWS):
            series_ref[trial] = final[trial, pl.ds(0, blocks), :]


def unpacked_widths(words):
    return [words[2 + index // 4] >> 8 * (index % 4) & 255 for index in range(WIDTHS)]


def finish_kernel(words_ref, series_ref, out_ref, peaks_ref, rows, *scratch):
    blocks = series_ref.shape[1]
    words = [words_ref[0, index] for index in range(2 + WIDTHS // 4)]
    for trial in range(ROWS):
        rows[trial, pl.ds(0, blocks), :] = series_ref[trial]
    finish(rows, unpacked_widths(words), out_ref, peaks_ref, *scratch)


def row_scratch(blocks):
    return pltpu.VMEM((ROWS, blocks + PAD, LANES), jnp.float32)


def finish_scratch(blocks):
    return [
        pltpu.VMEM((blocks, ROWS, LANES), jnp.float32),
        pltpu.VMEM((blocks + 2, ROWS, LANES), jnp.float32),
        pltpu.VMEM((blocks * ROWS, 2 * LANES), jnp.bfloat16),
    ]


def final_shapes(blocks):
    return (
        jax.ShapeDtypeStruct((ROWS, blocks * LANES), jnp.bfloat16),
        jax.ShapeDtypeStruct((WIDTHS, ROWS), jnp.float32),
    )


def swapped(block, distance):
    count = lax.axis_size("chan")
    return lax.ppermute(block, "chan", [(device, device ^ distance) for device in range(count)])


def advance(rows_in, shifts, start):
    count, length = rows_in.shape
    padded = jnp.concatenate([rows_in, jnp.zeros_like(rows_in)], axis=1)
    moved = lax.dynamic_slice_in_dim(padded, jnp.minimum(2 * start, length), length, 1)
    moved = jnp.concatenate([moved, jnp.zeros((count, 2 * count), moved.dtype)], axis=1)
    width = length + 2 * count
    flat = jnp.concatenate([moved.reshape(-1), jnp.zeros((2 * count,), moved.dtype)])
    skewed = flat.reshape(count, width + 2)[:, :length]
    odd = jnp.concatenate([skewed[:, 1:], jnp.zeros((count, 1), moved.dtype)], axis=1)
    parity = shifts - 2 * (start + jnp.arange(count, dtype=jnp.int32))
    return jnp.where((parity == 1)[:, None], odd, skewed)


def wider_sections(current, shift_table, me, section_count):
    half = ROWS // 2
    position = reverse4(me % 16)
    for bit in range(4, section_count):
        side = me >> bit & 1
        trials_now = 2 * ROWS << bit
        theirs = lax.dynamic_slice_in_dim(current, (1 - side) * half, half, 0)
        ours = lax.dynamic_slice_in_dim(current, side * half, half, 0)
        arrived = swapped(theirs, 1 << bit)
        lower = jnp.where(side == 0, ours, arrived)
        upper = jnp.where(side == 0, arrived, ours)
        first_trial = 2 * (position * ROWS + side * half)
        shifts = lax.dynamic_slice_in_dim(shift_table, trials_now - 1 + first_trial, ROWS)
        current = jnp.repeat(lower, 2, axis=0) + advance(jnp.repeat(upper, 2, axis=0), shifts, first_trial)
        position = 2 * position + side
    return current


def shards(filterbank, shift_table, box_widths):
    channels, length = filterbank.shape
    blocks = length // LANES
    count = lax.axis_size("chan")
    section_count = count.bit_length() - 1
    rows, words = local_rows(filterbank, shift_table, box_widths)
    small = section_count == 4

    early = [swapped(rows[4 * SPAN + 5 * index : 4 * SPAN + 5 * index + 5], step) for index, step in enumerate(EARLY)]
    plane = [rows] + [
        swapped(rows[SPAN * group : SPAN * (group + 1)], offset) for group, offset in ((1, 2), (2, 1), (3, 3))
    ]
    mean = sum(part[SPAN - 1 : SPAN] for part in plane)
    late = [
        swapped(jnp.concatenate([part[1 + index : 2 + index] for part in plane] + [mean], axis=0), step)
        for index, step in enumerate(LATE)
    ]
    column = sum(part[4:] for part in early)
    passed = [
        swapped(jnp.concatenate([part[group : group + 1] for part in early] + [column], axis=0), offset)
        for group, offset in ((1, 2), (2, 1), (3, 3))
    ]
    mean = mean + column
    arrived = [*plane, *early, *late, *passed]
    if not small:
        mean = lax.psum(rows[SPAN - 1 : SPAN], "chan")

    vmem = pl.BlockSpec(memory_space=pltpu.VMEM)
    params = pltpu.CompilerParams(vmem_limit_bytes=32 << 20)
    call = pl.pallas_call(
        functools.partial(cross_kernel, channels, count, small),
        out_shape=final_shapes(blocks)
        if small
        else jax.ShapeDtypeStruct((ROWS, blocks, LANES), jnp.float32),
        in_specs=[vmem] * (len(arrived) + 2),
        out_specs=(vmem, vmem) if small else vmem,
        scratch_shapes=[
            *[row_scratch(blocks)] * 2,
            *[pltpu.VMEM((blocks + PAD, LANES), jnp.float32)] * (4 + 3 * ROWS),
            *(finish_scratch(blocks) if small else []),
        ],
        compiler_params=params,
        name="cross_tree",
    )
    result = call(words, *arrived, mean)
    if small:
        return tuple(result)
    me = lax.axis_index("chan")
    current = wider_sections(result.reshape(ROWS, length), shift_table, me, section_count)
    return tuple(
        pl.pallas_call(
            finish_kernel,
            out_shape=final_shapes(blocks),
            in_specs=[vmem, vmem],
            out_specs=(vmem, vmem),
            scratch_shapes=[row_scratch(blocks)] + finish_scratch(blocks),
            compiler_params=params,
            name="finish",
        )(words, current.reshape(ROWS, blocks, LANES))
    )


def solution(mesh):
    placed = (P(("beam", "chan"), None), P(), P())
    return jax.shard_map(
        shards,
        mesh=mesh,
        in_specs=placed,
        out_specs=(P(("beam", "chan"), None), P("beam", "chan")),
        check_vma=False,
    )
```

```python
import functools

import jax
import jax.numpy as jnp
from jax import lax
from jax.experimental import pallas as pl
from jax.experimental.pallas import tpu as pltpu
from jax.sharding import PartitionSpec as P

ROWS = 16
LANES = 128
PAD = 8
WIDTHS = 8
EARLY = (4, 12)
LATE = tuple(step for step in (4, 8, 12) if step not in EARLY)
SPAN = len(LATE) + 2
LOW = {4: 2, 8: 1, 12: 3}
SPOTS = {LOW[step]: (1 + index, SPAN) for index, step in enumerate(LATE)}
SPOTS.update({LOW[step]: (4 * SPAN + 5 * index, 1) for index, step in enumerate(EARLY)})
MEAN_ROWS = [SPAN * group + SPAN - 1 for group in range(4)] + [4 * SPAN + 5 * index + 4 for index in range(len(EARLY))]
PATH = ((1, 0), (1, 1), (2, 2), (4, 3), (8, 4), (16, 5))

epsilon = 1e-05


def reverse4(value):
    return (value & 1) << 3 | (value & 2) << 1 | (value & 4) >> 1 | (value & 8) >> 3


def lane_index(blocks):
    return lax.broadcasted_iota(jnp.int32, (blocks, LANES), 1)


def moved(here, beyond, lane, part):
    return pltpu.roll(jnp.where(lane >= part, here, beyond), (LANES - part) & 127, axis=1)


def later(ref, blocks, lane, shift):
    whole = shift >> 7
    return moved(ref[pl.ds(whole, blocks), :], ref[pl.ds(whole + 1, blocks), :], lane, shift & 127)


def clear_tail(refs, blocks):
    for ref in refs:
        ref[blocks : blocks + PAD, :] = jnp.zeros((PAD, LANES), jnp.float32)


def uppers(refs, trials):
    return [ref for row, ref in enumerate(refs) if row // trials % 2]


def rows_of(ref):
    return [ref.at[row] for row in range(ref.shape[0])]


def spread_sum(terms):
    strands = [None] * 4
    for index, term in enumerate(terms):
        strand = strands[index % 4]
        strands[index % 4] = term if strand is None else strand + term
    return (strands[0] + strands[1]) + (strands[2] + strands[3])


def packed_words(table_ref, width_ref, row):
    path, cross = jnp.int32(0), jnp.int32(0)
    spot = 0
    for trials, _ in PATH:
        index = row >> (ROWS // trials).bit_length() - 1
        path = path | (table_ref[trials - 1 + index] - 2 * index) << spot
        spot += 1
    spot = 0
    for fresh in (2, 4, 8, 16):
        for trial in range(fresh):
            index = row * fresh + trial
            cross = cross | (table_ref[ROWS * fresh - 1 + index] - 2 * index) << spot
            spot += 1
    words = [path, cross]
    for start in range(0, WIDTHS, 4):
        word = jnp.int32(0)
        for place in range(4):
            word = word | width_ref[start + place] << 8 * place
        words.append(word)
    return words


def local_kernel(
    table_hbm, width_hbm, x_hbm, rows_ref, words_ref,
    table_ref, width_ref, x_ref, small_sem, x_sem, *single,
):
    channels, length = x_ref.shape
    blocks = length // LANES
    stride = blocks + PAD
    groups = channels // 16
    copies = [
        pltpu.make_async_copy(x_hbm, x_ref, x_sem),
        pltpu.make_async_copy(table_hbm, table_ref, small_sem.at[0]),
        pltpu.make_async_copy(width_hbm, width_ref, small_sem.at[1]),
    ]
    for copy in copies:
        copy.start()
    lane = lane_index(blocks)
    normal, single = single[:groups], single[groups:]
    channel = [ref.at[pl.ds(row * stride, stride), :] for ref in normal for row in range(16)]
    inner, quads, eights, sixteens, halves = [single[ROWS * level : ROWS * (level + 1)] for level in range(5)]
    clear_tail(channel[3::4] + list(inner), blocks)
    for level, refs in enumerate((quads, eights, sixteens, halves)):
        clear_tail(uppers(refs, 1 << level), blocks)

    def row_of(refs, row):
        return refs[row][0:blocks, :]

    for copy in copies:
        copy.wait()
    for group in range(groups):
        rows = slice(16 * group, 16 * group + 16)

        def piece(block):
            return x_ref[rows, block * LANES : (block + 1) * LANES].astype(jnp.float32)

        total = spread_sum(piece(block) for block in range(blocks))
        centre = jnp.sum(total, axis=1, keepdims=True) / length
        centre = jnp.broadcast_to(centre, (16, LANES))
        total = spread_sum(jnp.square(piece(block) - centre) for block in range(blocks))
        spread = jnp.sum(total, axis=1, keepdims=True) / length
        gain = jnp.broadcast_to(lax.rsqrt(spread + epsilon), (16, LANES))
        for block in range(blocks):
            value = (piece(block) - centre) * gain
            for half in range(2):
                start = 8 * half * stride + block
                normal[group][pl.ds(start, 8, stride=stride), :] = value[8 * half : 8 * half + 8]
    shift = table_ref[0]
    partial = []
    for quad in range(ROWS):
        pair = row_of(channel, 4 * quad + 1) + row_of(channel, 4 * quad + 2)
        inner[quad][0:blocks, :] = pair + later(channel[4 * quad + 3], blocks, lane, shift)
        partial.append(pair + (row_of(channel, 4 * quad) + row_of(channel, 4 * quad + 3)))
    partial = spread_sum(partial)
    for row in MEAN_ROWS:
        rows_ref[row] = partial
    for quad in range(ROWS):
        quads[quad][0:blocks, :] = row_of(channel, 4 * quad) + later(inner[quad], blocks, lane, shift)
    bands, trials = ROWS, 1
    for source, target in ((quads, eights), (eights, sixteens), (sixteens, halves)):
        fresh = 2 * trials
        for trial in range(fresh):
            shift = table_ref[fresh - 1 + trial]
            for band in range(bands // 2):
                high = later(source[(2 * band + 1) * trials + trial // 2], blocks, lane, shift)
                value = row_of(source, 2 * band * trials + trial // 2) + high
                target[band * fresh + trial][0:blocks, :] = value
        bands, trials = bands // 2, fresh
    mine = reverse4(lax.axis_index("chan") & 15)
    for trial in range(ROWS):
        high = later(halves[8 + trial // 2], blocks, lane, table_ref[ROWS - 1 + trial])
        place = mine ^ trial
        group, low = place >> 2, place & 3
        spot = group * SPAN
        for other, (base, scale) in SPOTS.items():
            spot = jnp.where(low == other, base + scale * group, spot)
        rows_ref[spot] = row_of(halves, trial // 2) + high
    small_lane = lax.broadcasted_iota(jnp.int32, words_ref.shape, 1)
    words = jnp.zeros(words_ref.shape, jnp.int32)
    for index, word in enumerate(packed_words(table_ref, width_ref, mine)):
        words = jnp.where(small_lane == index, word, words)
    words_ref[...] = words


def local_rows(filterbank, shift_table, box_widths):
    channels, length = filterbank.shape
    blocks = length // LANES
    hbm = pl.BlockSpec(memory_space=pltpu.HBM)
    vmem = pl.BlockSpec(memory_space=pltpu.VMEM)
    inputs = [pltpu.with_memory_space_constraint(value, pltpu.HBM) for value in (shift_table, box_widths, filterbank)]
    return pl.pallas_call(
        local_kernel,
        out_shape=(
            jax.ShapeDtypeStruct((4 * SPAN + 5 * len(EARLY), blocks, LANES), jnp.float32),
            jax.ShapeDtypeStruct((8, LANES), jnp.int32),
        ),
        in_specs=[hbm] * 3,
        out_specs=(vmem, vmem),
        scratch_shapes=[
            pltpu.SMEM(shift_table.shape, jnp.int32),
            pltpu.SMEM(box_widths.shape, jnp.int32),
            pltpu.VMEM(filterbank.shape, filterbank.dtype),
            pltpu.SemaphoreType.DMA((2,)),
            pltpu.SemaphoreType.DMA,
            *[pltpu.VMEM((16 * (blocks + PAD), LANES), jnp.float32)] * (channels // 16),
            *[pltpu.VMEM((blocks + PAD, LANES), jnp.float32)] * 5 * ROWS,
        ],
        compiler_params=pltpu.CompilerParams(vmem_limit_bytes=32 << 20),
        name="local_tree",
    )(*inputs)


def mean_path(mean, word, scratch, blocks, lane, row):
    value = mean
    for step in range(0, len(PATH), 2):
        shifts = []
        for trials, spot in PATH[step : step + 2]:
            index = row >> (ROWS // trials).bit_length() - 1
            shifts.append(2 * index + (word >> spot & 1))
        ref = scratch[step // 2]
        ref[0:blocks, :] = value
        near, far = shifts
        value = (value + later(ref, blocks, lane, near)) + (
            later(ref, blocks, lane, far) + later(ref, blocks, lane, near + far)
        )
    return value


def cross_tree(me, mean, words, buffers, spare, blocks, lane):
    row = reverse4(me & 15)
    path, cross = words[0], words[1]
    mean = mean_path(mean, path, spare, blocks, lane, row)
    spare[3][0:blocks, :] = mean
    bands, trials = ROWS, 1
    spot = 0
    for source, target in zip(buffers[:-1], buffers[1:]):
        fresh = 2 * trials
        for trial in range(fresh):
            shift = 2 * (row * fresh + trial) + (cross >> spot & 1)
            spot += 1
            old = trial // 2
            if bands == ROWS:
                taken = mean + later(spare[3], blocks, lane, shift)
            for band in range(bands // 2):
                high = later(source[(2 * band + 1) * trials + old], blocks, lane, shift)
                value = source[2 * band * trials + old][0:blocks, :] + high
                if bands == ROWS:
                    value = value - taken
                target[band * fresh + trial][0:blocks, :] = value
        bands, trials = bands // 2, fresh


def finish(rows, widths, out_ref, peaks_ref, values, prefix, split):
    stride = rows.shape[1]
    blocks = stride - PAD
    length = blocks * LANES
    lane = lax.broadcasted_iota(jnp.int32, (ROWS, LANES), 1)
    flat = rows.reshape(ROWS * stride, LANES)

    total = []
    for block in range(blocks):
        value = jnp.concatenate(
            [flat[pl.ds(block + 8 * half * stride, 8, stride=stride), :] for half in range(2)], axis=0
        )
        values[block] = value
        high = value.astype(jnp.bfloat16)
        rest = (value - high.astype(jnp.float32)).astype(jnp.bfloat16)
        split[pl.ds(block * ROWS, ROWS), pl.ds(0, LANES)] = high
        split[pl.ds(block * ROWS, ROWS), pl.ds(LANES, LANES)] = rest
        total.append(value)
    centre = jnp.sum(spread_sum(total), axis=1, keepdims=True) / length
    centre = jnp.broadcast_to(centre, (ROWS, LANES))
    above = lax.broadcasted_iota(jnp.int32, (2 * LANES, 2 * LANES), 0) & 127
    across = lax.broadcasted_iota(jnp.int32, (2 * LANES, 2 * LANES), 1)
    weights = jnp.where(above <= across, 1.0, 0.0).astype(jnp.bfloat16)
    sums = jnp.dot(split[...], weights, preferred_element_type=jnp.float32)
    carry = jnp.zeros((ROWS, LANES), jnp.float32)
    prefix[0] = carry
    prefix[1] = carry
    ramp = centre * (lane + 1).astype(jnp.float32)
    drop = centre * LANES
    for block in range(blocks):
        part = sums[block * ROWS : (block + 1) * ROWS]
        prefix[2 + block] = (part[:, :LANES] - ramp) + carry
        carry = carry + (part[:, LANES:] - drop)

    spread = spread_sum(jnp.square(values[block] - centre) for block in range(blocks))
    spread = jnp.sum(spread, axis=1, keepdims=True) / length
    gain = jnp.broadcast_to(lax.rsqrt(spread + epsilon), (ROWS, LANES))
    for block in range(blocks):
        out_ref[:, pl.ds(block * LANES, LANES)] = ((values[block] - centre) * gain).astype(jnp.bfloat16)

    peaks = jnp.zeros((ROWS, LANES), jnp.float32)
    backs = [2 * LANES - width for width in widths]
    heres = [prefix[back >> 7] for back in backs]
    best = [None] * len(widths)
    for block in range(blocks):
        now = prefix[2 + block]
        for index, back in enumerate(backs):
            beyond = prefix[(back >> 7) + block + 1]
            gap = now - moved(heres[index], beyond, lane, back & 127)
            best[index] = gap if best[index] is None else jnp.maximum(best[index], gap)
            heres[index] = beyond
    for index, width in enumerate(widths):
        peak = jnp.max(best[index], axis=1, keepdims=True)
        scale = gain * lax.rsqrt(jnp.full((ROWS, LANES), width, jnp.int32).astype(jnp.float32))
        peaks = jnp.where(lane == index, peak * scale, peaks)
    peaks_ref[...] = jnp.transpose(peaks)[: len(widths)]


def cross_kernel(
    channels, count, finishing, words_ref, *rest,
):
    plane, rest = rest[:4], rest[4:]
    early, rest = rest[: len(EARLY)], rest[len(EARLY) :]
    late, rest = rest[: len(LATE)], rest[len(LATE) :]
    passed, (mean_ref, *rest) = rest[:3], rest[3:]
    blocks = mean_ref.shape[1]
    lane = lane_index(blocks)
    if finishing:
        out_ref, peaks_ref, first, final, *single, values, prefix, split = rest
    else:
        series_ref, first, final, *single = rest
    words = [words_ref[0, index] for index in range(2 + WIDTHS // 4)]
    spare, single = single[:4], single[4:]
    buffers = [rows_of(first), single[:ROWS], single[ROWS : 2 * ROWS], single[2 * ROWS :], rows_of(final)]
    clear_tail(spare, blocks)
    for level, refs in enumerate(buffers[:4]):
        clear_tail(uppers(refs, 1 << level), blocks)
    me = lax.axis_index("chan")
    here = me & 15

    def place(offset, value):
        first[here ^ offset, pl.ds(0, blocks), :] = value

    offsets = (0, 2, 1, 3)
    for group, offset in enumerate(offsets):
        place(offset, plane[group][0])
        for index, step in enumerate(LATE):
            place(step + offset, late[index][group])
        for index, step in enumerate(EARLY):
            place(step + offset, passed[group - 1][index] if group else early[index][0])
    mean = mean_ref[0]
    if finishing:
        for ref in late:
            mean = mean + ref[4]
        for ref in passed:
            mean = mean + ref[len(EARLY)]
    mean = mean / (channels * count)
    cross_tree(me, mean, words, buffers, spare, blocks, lane)
    if finishing:
        finish(final, unpacked_widths(words), out_ref, peaks_ref, values, prefix, split)
    else:
        for trial in range(ROWS):
            series_ref[trial] = final[trial, pl.ds(0, blocks), :]


def unpacked_widths(words):
    return [words[2 + index // 4] >> 8 * (index % 4) & 255 for index in range(WIDTHS)]


def finish_kernel(words_ref, series_ref, out_ref, peaks_ref, rows, *scratch):
    blocks = series_ref.shape[1]
    words = [words_ref[0, index] for index in range(2 + WIDTHS // 4)]
    for trial in range(ROWS):
        rows[trial, pl.ds(0, blocks), :] = series_ref[trial]
    finish(rows, unpacked_widths(words), out_ref, peaks_ref, *scratch)


def row_scratch(blocks):
    return pltpu.VMEM((ROWS, blocks + PAD, LANES), jnp.float32)


def finish_scratch(blocks):
    return [
        pltpu.VMEM((blocks, ROWS, LANES), jnp.float32),
        pltpu.VMEM((blocks + 2, ROWS, LANES), jnp.float32),
        pltpu.VMEM((blocks * ROWS, 2 * LANES), jnp.bfloat16),
    ]


def final_shapes(blocks):
    return (
        jax.ShapeDtypeStruct((ROWS, blocks * LANES), jnp.bfloat16),
        jax.ShapeDtypeStruct((WIDTHS, ROWS), jnp.float32),
    )


def swapped(block, distance):
    count = lax.axis_size("chan")
    return lax.ppermute(block, "chan", [(device, device ^ distance) for device in range(count)])


def advance(rows_in, shifts, start):
    count, length = rows_in.shape
    padded = jnp.concatenate([rows_in, jnp.zeros_like(rows_in)], axis=1)
    moved = lax.dynamic_slice_in_dim(padded, jnp.minimum(2 * start, length), length, 1)
    moved = jnp.concatenate([moved, jnp.zeros((count, 2 * count), moved.dtype)], axis=1)
    width = length + 2 * count
    flat = jnp.concatenate([moved.reshape(-1), jnp.zeros((2 * count,), moved.dtype)])
    skewed = flat.reshape(count, width + 2)[:, :length]
    odd = jnp.concatenate([skewed[:, 1:], jnp.zeros((count, 1), moved.dtype)], axis=1)
    parity = shifts - 2 * (start + jnp.arange(count, dtype=jnp.int32))
    return jnp.where((parity == 1)[:, None], odd, skewed)


def wider_sections(current, shift_table, me, section_count):
    half = ROWS // 2
    position = reverse4(me % 16)
    for bit in range(4, section_count):
        side = me >> bit & 1
        trials_now = 2 * ROWS << bit
        theirs = lax.dynamic_slice_in_dim(current, (1 - side) * half, half, 0)
        ours = lax.dynamic_slice_in_dim(current, side * half, half, 0)
        arrived = swapped(theirs, 1 << bit)
        lower = jnp.where(side == 0, ours, arrived)
        upper = jnp.where(side == 0, arrived, ours)
        first_trial = 2 * (position * ROWS + side * half)
        shifts = lax.dynamic_slice_in_dim(shift_table, trials_now - 1 + first_trial, ROWS)
        current = jnp.repeat(lower, 2, axis=0) + advance(jnp.repeat(upper, 2, axis=0), shifts, first_trial)
        position = 2 * position + side
    return current


def shards(filterbank, shift_table, box_widths):
    channels, length = filterbank.shape
    blocks = length // LANES
    count = lax.axis_size("chan")
    section_count = count.bit_length() - 1
    rows, words = local_rows(filterbank, shift_table, box_widths)
    small = section_count == 4

    early = [swapped(rows[4 * SPAN + 5 * index : 4 * SPAN + 5 * index + 5], step) for index, step in enumerate(EARLY)]
    plane = [rows] + [
        swapped(rows[SPAN * group : SPAN * (group + 1)], offset) for group, offset in ((1, 2), (2, 1), (3, 3))
    ]
    mean = sum(part[SPAN - 1 : SPAN] for part in plane)
    late = [
        swapped(jnp.concatenate([part[1 + index : 2 + index] for part in plane] + [mean], axis=0), step)
        for index, step in enumerate(LATE)
    ]
    column = sum(part[4:] for part in early)
    passed = [
        swapped(jnp.concatenate([part[group : group + 1] for part in early] + [column], axis=0), offset)
        for group, offset in ((1, 2), (2, 1), (3, 3))
    ]
    mean = mean + column
    arrived = [*plane, *early, *late, *passed]
    if not small:
        mean = lax.psum(rows[SPAN - 1 : SPAN], "chan")

    vmem = pl.BlockSpec(memory_space=pltpu.VMEM)
    params = pltpu.CompilerParams(vmem_limit_bytes=32 << 20)
    call = pl.pallas_call(
        functools.partial(cross_kernel, channels, count, small),
        out_shape=final_shapes(blocks)
        if small
        else jax.ShapeDtypeStruct((ROWS, blocks, LANES), jnp.float32),
        in_specs=[vmem] * (len(arrived) + 2),
        out_specs=(vmem, vmem) if small else vmem,
        scratch_shapes=[
            *[row_scratch(blocks)] * 2,
            *[pltpu.VMEM((blocks + PAD, LANES), jnp.float32)] * (4 + 3 * ROWS),
            *(finish_scratch(blocks) if small else []),
        ],
        compiler_params=params,
        name="cross_tree",
    )
    result = call(words, *arrived, mean)
    if small:
        return tuple(result)
    me = lax.axis_index("chan")
    current = wider_sections(result.reshape(ROWS, length), shift_table, me, section_count)
    return tuple(
        pl.pallas_call(
            finish_kernel,
            out_shape=final_shapes(blocks),
            in_specs=[vmem, vmem],
            out_specs=(vmem, vmem),
            scratch_shapes=[row_scratch(blocks)] + finish_scratch(blocks),
            compiler_params=params,
            name="finish",
        )(words, current.reshape(ROWS, blocks, LANES))
    )


def solution(mesh):
    placed = (P(("beam", "chan"), None), P(), P())
    return jax.shard_map(
        shards,
        mesh=mesh,
        in_specs=placed,
        out_specs=(P(("beam", "chan"), None), P("beam", "chan")),
        check_vma=False,
    )
```

```python
import functools

import jax
import jax.numpy as jnp
from jax import lax
from jax.experimental import pallas as pl
from jax.experimental.pallas import tpu as pltpu
from jax.sharding import PartitionSpec as P

ROWS = 16
LANES = 128
PAD = 8
WIDTHS = 8
EARLY = (4, 12)
LATE = tuple(step for step in (4, 8, 12) if step not in EARLY)
SPAN = len(LATE) + 2
LOW = {4: 2, 8: 1, 12: 3}
SPOTS = {LOW[step]: (1 + index, SPAN) for index, step in enumerate(LATE)}
SPOTS.update({LOW[step]: (4 * SPAN + 5 * index, 1) for index, step in enumerate(EARLY)})
MEAN_ROWS = [SPAN * group + SPAN - 1 for group in range(4)] + [4 * SPAN + 5 * index + 4 for index in range(len(EARLY))]
PATH = ((1, 0), (1, 1), (2, 2), (4, 3), (8, 4), (16, 5))

epsilon = 1e-05


def reverse4(value):
    return (value & 1) << 3 | (value & 2) << 1 | (value & 4) >> 1 | (value & 8) >> 3


def lane_index(blocks):
    return lax.broadcasted_iota(jnp.int32, (blocks, LANES), 1)


def moved(here, beyond, lane, part):
    return pltpu.roll(jnp.where(lane >= part, here, beyond), (LANES - part) & 127, axis=1)


def later(ref, blocks, lane, shift):
    whole = shift >> 7
    return moved(ref[pl.ds(whole, blocks), :], ref[pl.ds(whole + 1, blocks), :], lane, shift & 127)


def clear_tail(refs, blocks):
    for ref in refs:
        ref[blocks : blocks + PAD, :] = jnp.zeros((PAD, LANES), jnp.float32)


def uppers(refs, trials):
    return [ref for row, ref in enumerate(refs) if row // trials % 2]


def rows_of(ref):
    return [ref.at[row] for row in range(ref.shape[0])]


def spread_sum(terms):
    strands = [None] * 4
    for index, term in enumerate(terms):
        strand = strands[index % 4]
        strands[index % 4] = term if strand is None else strand + term
    return (strands[0] + strands[1]) + (strands[2] + strands[3])


def packed_words(table_ref, width_ref, row):
    path, cross = jnp.int32(0), jnp.int32(0)
    spot = 0
    for trials, _ in PATH:
        index = row >> (ROWS // trials).bit_length() - 1
        path = path | (table_ref[trials - 1 + index] - 2 * index) << spot
        spot += 1
    spot = 0
    for fresh in (2, 4, 8, 16):
        for trial in range(fresh):
            index = row * fresh + trial
            cross = cross | (table_ref[ROWS * fresh - 1 + index] - 2 * index) << spot
            spot += 1
    words = [path, cross]
    for start in range(0, WIDTHS, 4):
        word = jnp.int32(0)
        for place in range(4):
            word = word | width_ref[start + place] << 8 * place
        words.append(word)
    return words


def local_kernel(
    table_hbm, width_hbm, x_hbm, rows_ref, words_ref,
    table_ref, width_ref, x_ref, small_sem, x_sem, *single,
):
    channels, length = x_ref.shape
    blocks = length // LANES
    stride = blocks + PAD
    groups = channels // 16
    copies = [
        pltpu.make_async_copy(x_hbm, x_ref, x_sem),
        pltpu.make_async_copy(table_hbm, table_ref, small_sem.at[0]),
        pltpu.make_async_copy(width_hbm, width_ref, small_sem.at[1]),
    ]
    for copy in copies:
        copy.start()
    lane = lane_index(blocks)
    normal, single = single[:groups], single[groups:]
    channel = [ref.at[pl.ds(row * stride, stride), :] for ref in normal for row in range(16)]
    inner, quads, eights, sixteens, halves = [single[ROWS * level : ROWS * (level + 1)] for level in range(5)]
    clear_tail(channel[3::4] + list(inner), blocks)
    for level, refs in enumerate((quads, eights, sixteens, halves)):
        clear_tail(uppers(refs, 1 << level), blocks)

    def row_of(refs, row):
        return refs[row][0:blocks, :]

    for copy in copies:
        copy.wait()
    for group in range(groups):
        rows = slice(16 * group, 16 * group + 16)

        def piece(block):
            return x_ref[rows, block * LANES : (block + 1) * LANES].astype(jnp.float32)

        total = spread_sum(piece(block) for block in range(blocks))
        centre = jnp.sum(total, axis=1, keepdims=True) / length
        centre = jnp.broadcast_to(centre, (16, LANES))
        total = spread_sum(jnp.square(piece(block) - centre) for block in range(blocks))
        spread = jnp.sum(total, axis=1, keepdims=True) / length
        gain = jnp.broadcast_to(lax.rsqrt(spread + epsilon), (16, LANES))
        for block in range(blocks):
            value = (piece(block) - centre) * gain
            for half in range(2):
                start = 8 * half * stride + block
                normal[group][pl.ds(start, 8, stride=stride), :] = value[8 * half : 8 * half + 8]
    shift = table_ref[0]
    partial = []
    for quad in range(ROWS):
        pair = row_of(channel, 4 * quad + 1) + row_of(channel, 4 * quad + 2)
        inner[quad][0:blocks, :] = pair + later(channel[4 * quad + 3], blocks, lane, shift)
        partial.append(pair + (row_of(channel, 4 * quad) + row_of(channel, 4 * quad + 3)))
    partial = spread_sum(partial)
    for row in MEAN_ROWS:
        rows_ref[row] = partial
    for quad in range(ROWS):
        quads[quad][0:blocks, :] = row_of(channel, 4 * quad) + later(inner[quad], blocks, lane, shift)
    bands, trials = ROWS, 1
    for source, target in ((quads, eights), (eights, sixteens), (sixteens, halves)):
        fresh = 2 * trials
        for trial in range(fresh):
            shift = table_ref[fresh - 1 + trial]
            for band in range(bands // 2):
                high = later(source[(2 * band + 1) * trials + trial // 2], blocks, lane, shift)
                value = row_of(source, 2 * band * trials + trial // 2) + high
                target[band * fresh + trial][0:blocks, :] = value
        bands, trials = bands // 2, fresh
    mine = reverse4(lax.axis_index("chan") & 15)
    for trial in range(ROWS):
        high = later(halves[8 + trial // 2], blocks, lane, table_ref[ROWS - 1 + trial])
        place = mine ^ trial
        group, low = place >> 2, place & 3
        spot = group * SPAN
        for other, (base, scale) in SPOTS.items():
            spot = jnp.where(low == other, base + scale * group, spot)
        rows_ref[spot] = row_of(halves, trial // 2) + high
    small_lane = lax.broadcasted_iota(jnp.int32, words_ref.shape, 1)
    words = jnp.zeros(words_ref.shape, jnp.int32)
    for index, word in enumerate(packed_words(table_ref, width_ref, mine)):
        words = jnp.where(small_lane == index, word, words)
    words_ref[...] = words


def local_rows(filterbank, shift_table, box_widths):
    channels, length = filterbank.shape
    blocks = length // LANES
    hbm = pl.BlockSpec(memory_space=pltpu.HBM)
    vmem = pl.BlockSpec(memory_space=pltpu.VMEM)
    inputs = [pltpu.with_memory_space_constraint(value, pltpu.HBM) for value in (shift_table, box_widths, filterbank)]
    return pl.pallas_call(
        local_kernel,
        out_shape=(
            jax.ShapeDtypeStruct((4 * SPAN + 5 * len(EARLY), blocks, LANES), jnp.float32),
            jax.ShapeDtypeStruct((8, LANES), jnp.int32),
        ),
        in_specs=[hbm] * 3,
        out_specs=(vmem, vmem),
        scratch_shapes=[
            pltpu.SMEM(shift_table.shape, jnp.int32),
            pltpu.SMEM(box_widths.shape, jnp.int32),
            pltpu.VMEM(filterbank.shape, filterbank.dtype),
            pltpu.SemaphoreType.DMA((2,)),
            pltpu.SemaphoreType.DMA,
            *[pltpu.VMEM((16 * (blocks + PAD), LANES), jnp.float32)] * (channels // 16),
            *[pltpu.VMEM((blocks + PAD, LANES), jnp.float32)] * 5 * ROWS,
        ],
        compiler_params=pltpu.CompilerParams(vmem_limit_bytes=32 << 20),
        name="local_tree",
    )(*inputs)


def mean_path(mean, word, scratch, blocks, lane, row):
    value = mean
    for step in range(0, len(PATH), 3):
        moves = []
        for trials, spot in PATH[step : step + 3]:
            index = row >> (ROWS // trials).bit_length() - 1
            shift = 2 * index + (word >> spot & 1)
            moves = moves + [shift] + [other + shift for other in moves]
        ref = scratch[step // 3]
        ref[0:blocks, :] = value
        value = value + spread_sum(later(ref, blocks, lane, move) for move in moves)
    return value


def cross_tree(me, mean, words, buffers, spare, blocks, lane):
    row = reverse4(me & 15)
    path, cross = words[0], words[1]
    mean = mean_path(mean, path, spare, blocks, lane, row)
    spare[3][0:blocks, :] = mean
    bands, trials = ROWS, 1
    spot = 0
    for source, target in zip(buffers[:-1], buffers[1:]):
        fresh = 2 * trials
        for trial in range(fresh):
            shift = 2 * (row * fresh + trial) + (cross >> spot & 1)
            spot += 1
            old = trial // 2
            if bands == ROWS:
                taken = mean + later(spare[3], blocks, lane, shift)
            for band in range(bands // 2):
                high = later(source[(2 * band + 1) * trials + old], blocks, lane, shift)
                value = source[2 * band * trials + old][0:blocks, :] + high
                if bands == ROWS:
                    value = value - taken
                target[band * fresh + trial][0:blocks, :] = value
        bands, trials = bands // 2, fresh


def finish(rows, widths, out_ref, peaks_ref, values, prefix, split):
    stride = rows.shape[1]
    blocks = stride - PAD
    length = blocks * LANES
    lane = lax.broadcasted_iota(jnp.int32, (ROWS, LANES), 1)
    flat = rows.reshape(ROWS * stride, LANES)

    total = []
    for block in range(blocks):
        value = jnp.concatenate(
            [flat[pl.ds(block + 8 * half * stride, 8, stride=stride), :] for half in range(2)], axis=0
        )
        values[block] = value
        high = value.astype(jnp.bfloat16)
        rest = (value - high.astype(jnp.float32)).astype(jnp.bfloat16)
        split[pl.ds(block * ROWS, ROWS), pl.ds(0, LANES)] = high
        split[pl.ds(block * ROWS, ROWS), pl.ds(LANES, LANES)] = rest
        total.append(value)
    centre = jnp.sum(spread_sum(total), axis=1, keepdims=True) / length
    centre = jnp.broadcast_to(centre, (ROWS, LANES))
    above = lax.broadcasted_iota(jnp.int32, (2 * LANES, 2 * LANES), 0) & 127
    across = lax.broadcasted_iota(jnp.int32, (2 * LANES, 2 * LANES), 1)
    weights = jnp.where(above <= across, 1.0, 0.0).astype(jnp.bfloat16)
    sums = jnp.dot(split[...], weights, preferred_element_type=jnp.float32)
    carry = jnp.zeros((ROWS, LANES), jnp.float32)
    prefix[0] = carry
    prefix[1] = carry
    ramp = centre * (lane + 1).astype(jnp.float32)
    drop = centre * LANES
    for block in range(blocks):
        part = sums[block * ROWS : (block + 1) * ROWS]
        prefix[2 + block] = (part[:, :LANES] - ramp) + carry
        carry = carry + (part[:, LANES:] - drop)

    spread = spread_sum(jnp.square(values[block] - centre) for block in range(blocks))
    spread = jnp.sum(spread, axis=1, keepdims=True) / length
    gain = jnp.broadcast_to(lax.rsqrt(spread + epsilon), (ROWS, LANES))
    for block in range(blocks):
        out_ref[:, pl.ds(block * LANES, LANES)] = ((values[block] - centre) * gain).astype(jnp.bfloat16)

    peaks = jnp.zeros((ROWS, LANES), jnp.float32)
    backs = [2 * LANES - width for width in widths]
    heres = [prefix[back >> 7] for back in backs]
    best = [None] * len(widths)
    for block in range(blocks):
        now = prefix[2 + block]
        for index, back in enumerate(backs):
            beyond = prefix[(back >> 7) + block + 1]
            gap = now - moved(heres[index], beyond, lane, back & 127)
            best[index] = gap if best[index] is None else jnp.maximum(best[index], gap)
            heres[index] = beyond
    for index, width in enumerate(widths):
        peak = jnp.max(best[index], axis=1, keepdims=True)
        scale = gain * lax.rsqrt(jnp.full((ROWS, LANES), width, jnp.int32).astype(jnp.float32))
        peaks = jnp.where(lane == index, peak * scale, peaks)
    peaks_ref[...] = jnp.transpose(peaks)[: len(widths)]


def cross_kernel(
    channels, count, finishing, words_ref, *rest,
):
    plane, rest = rest[:4], rest[4:]
    early, rest = rest[: len(EARLY)], rest[len(EARLY) :]
    late, rest = rest[: len(LATE)], rest[len(LATE) :]
    passed, (mean_ref, *rest) = rest[:3], rest[3:]
    blocks = mean_ref.shape[1]
    lane = lane_index(blocks)
    if finishing:
        out_ref, peaks_ref, first, final, *single, values, prefix, split = rest
    else:
        series_ref, first, final, *single = rest
    words = [words_ref[0, index] for index in range(2 + WIDTHS // 4)]
    spare, single = single[:4], single[4:]
    buffers = [rows_of(first), single[:ROWS], single[ROWS : 2 * ROWS], single[2 * ROWS :], rows_of(final)]
    clear_tail(spare, blocks)
    for level, refs in enumerate(buffers[:4]):
        clear_tail(uppers(refs, 1 << level), blocks)
    me = lax.axis_index("chan")
    here = me & 15

    def place(offset, value):
        first[here ^ offset, pl.ds(0, blocks), :] = value

    offsets = (0, 2, 1, 3)
    for group, offset in enumerate(offsets):
        place(offset, plane[group][0])
        for index, step in enumerate(LATE):
            place(step + offset, late[index][group])
        for index, step in enumerate(EARLY):
            place(step + offset, passed[group - 1][index] if group else early[index][0])
    mean = mean_ref[0]
    if finishing:
        for ref in late:
            mean = mean + ref[4]
        for ref in passed:
            mean = mean + ref[len(EARLY)]
    mean = mean / (channels * count)
    cross_tree(me, mean, words, buffers, spare, blocks, lane)
    if finishing:
        finish(final, unpacked_widths(words), out_ref, peaks_ref, values, prefix, split)
    else:
        for trial in range(ROWS):
            series_ref[trial] = final[trial, pl.ds(0, blocks), :]


def unpacked_widths(words):
    return [words[2 + index // 4] >> 8 * (index % 4) & 255 for index in range(WIDTHS)]


def finish_kernel(words_ref, series_ref, out_ref, peaks_ref, rows, *scratch):
    blocks = series_ref.shape[1]
    words = [words_ref[0, index] for index in range(2 + WIDTHS // 4)]
    for trial in range(ROWS):
        rows[trial, pl.ds(0, blocks), :] = series_ref[trial]
    finish(rows, unpacked_widths(words), out_ref, peaks_ref, *scratch)


def row_scratch(blocks):
    return pltpu.VMEM((ROWS, blocks + PAD, LANES), jnp.float32)


def finish_scratch(blocks):
    return [
        pltpu.VMEM((blocks, ROWS, LANES), jnp.float32),
        pltpu.VMEM((blocks + 2, ROWS, LANES), jnp.float32),
        pltpu.VMEM((blocks * ROWS, 2 * LANES), jnp.bfloat16),
    ]


def final_shapes(blocks):
    return (
        jax.ShapeDtypeStruct((ROWS, blocks * LANES), jnp.bfloat16),
        jax.ShapeDtypeStruct((WIDTHS, ROWS), jnp.float32),
    )


def swapped(block, distance):
    count = lax.axis_size("chan")
    return lax.ppermute(block, "chan", [(device, device ^ distance) for device in range(count)])


def advance(rows_in, shifts, start):
    count, length = rows_in.shape
    padded = jnp.concatenate([rows_in, jnp.zeros_like(rows_in)], axis=1)
    moved = lax.dynamic_slice_in_dim(padded, jnp.minimum(2 * start, length), length, 1)
    moved = jnp.concatenate([moved, jnp.zeros((count, 2 * count), moved.dtype)], axis=1)
    width = length + 2 * count
    flat = jnp.concatenate([moved.reshape(-1), jnp.zeros((2 * count,), moved.dtype)])
    skewed = flat.reshape(count, width + 2)[:, :length]
    odd = jnp.concatenate([skewed[:, 1:], jnp.zeros((count, 1), moved.dtype)], axis=1)
    parity = shifts - 2 * (start + jnp.arange(count, dtype=jnp.int32))
    return jnp.where((parity == 1)[:, None], odd, skewed)


def wider_sections(current, shift_table, me, section_count):
    half = ROWS // 2
    position = reverse4(me % 16)
    for bit in range(4, section_count):
        side = me >> bit & 1
        trials_now = 2 * ROWS << bit
        theirs = lax.dynamic_slice_in_dim(current, (1 - side) * half, half, 0)
        ours = lax.dynamic_slice_in_dim(current, side * half, half, 0)
        arrived = swapped(theirs, 1 << bit)
        lower = jnp.where(side == 0, ours, arrived)
        upper = jnp.where(side == 0, arrived, ours)
        first_trial = 2 * (position * ROWS + side * half)
        shifts = lax.dynamic_slice_in_dim(shift_table, trials_now - 1 + first_trial, ROWS)
        current = jnp.repeat(lower, 2, axis=0) + advance(jnp.repeat(upper, 2, axis=0), shifts, first_trial)
        position = 2 * position + side
    return current


def shards(filterbank, shift_table, box_widths):
    channels, length = filterbank.shape
    blocks = length // LANES
    count = lax.axis_size("chan")
    section_count = count.bit_length() - 1
    rows, words = local_rows(filterbank, shift_table, box_widths)
    small = section_count == 4

    early = [swapped(rows[4 * SPAN + 5 * index : 4 * SPAN + 5 * index + 5], step) for index, step in enumerate(EARLY)]
    plane = [rows] + [
        swapped(rows[SPAN * group : SPAN * (group + 1)], offset) for group, offset in ((1, 2), (2, 1), (3, 3))
    ]
    mean = sum(part[SPAN - 1 : SPAN] for part in plane)
    late = [
        swapped(jnp.concatenate([part[1 + index : 2 + index] for part in plane] + [mean], axis=0), step)
        for index, step in enumerate(LATE)
    ]
    column = sum(part[4:] for part in early)
    passed = [
        swapped(jnp.concatenate([part[group : group + 1] for part in early] + [column], axis=0), offset)
        for group, offset in ((1, 2), (2, 1), (3, 3))
    ]
    mean = mean + column
    arrived = [*plane, *early, *late, *passed]
    if not small:
        mean = lax.psum(rows[SPAN - 1 : SPAN], "chan")

    vmem = pl.BlockSpec(memory_space=pltpu.VMEM)
    params = pltpu.CompilerParams(vmem_limit_bytes=32 << 20)
    call = pl.pallas_call(
        functools.partial(cross_kernel, channels, count, small),
        out_shape=final_shapes(blocks)
        if small
        else jax.ShapeDtypeStruct((ROWS, blocks, LANES), jnp.float32),
        in_specs=[vmem] * (len(arrived) + 2),
        out_specs=(vmem, vmem) if small else vmem,
        scratch_shapes=[
            *[row_scratch(blocks)] * 2,
            *[pltpu.VMEM((blocks + PAD, LANES), jnp.float32)] * (4 + 3 * ROWS),
            *(finish_scratch(blocks) if small else []),
        ],
        compiler_params=params,
        name="cross_tree",
    )
    result = call(words, *arrived, mean)
    if small:
        return tuple(result)
    me = lax.axis_index("chan")
    current = wider_sections(result.reshape(ROWS, length), shift_table, me, section_count)
    return tuple(
        pl.pallas_call(
            finish_kernel,
            out_shape=final_shapes(blocks),
            in_specs=[vmem, vmem],
            out_specs=(vmem, vmem),
            scratch_shapes=[row_scratch(blocks)] + finish_scratch(blocks),
            compiler_params=params,
            name="finish",
        )(words, current.reshape(ROWS, blocks, LANES))
    )


def solution(mesh):
    placed = (P(("beam", "chan"), None), P(), P())
    return jax.shard_map(
        shards,
        mesh=mesh,
        in_specs=placed,
        out_specs=(P(("beam", "chan"), None), P("beam", "chan")),
        check_vma=False,
    )
```

```python
import functools

import jax
import jax.numpy as jnp
from jax import lax
from jax.experimental import pallas as pl
from jax.experimental.pallas import tpu as pltpu
from jax.sharding import PartitionSpec as P

ROWS = 16
LANES = 128
PAD = 8
WIDTHS = 8
EARLY = (4, 12)
LATE = tuple(step for step in (4, 8, 12) if step not in EARLY)
SPAN = len(LATE) + 2
LOW = {4: 2, 8: 1, 12: 3}
SPOTS = {LOW[step]: (1 + index, SPAN) for index, step in enumerate(LATE)}
SPOTS.update({LOW[step]: (4 * SPAN + 5 * index, 1) for index, step in enumerate(EARLY)})
MEAN_ROWS = [SPAN * group + SPAN - 1 for group in range(4)] + [4 * SPAN + 5 * index + 4 for index in range(len(EARLY))]
PATH = ((1, 0), (1, 1), (2, 2), (4, 3), (8, 4), (16, 5))

epsilon = 1e-05


def reverse4(value):
    return (value & 1) << 3 | (value & 2) << 1 | (value & 4) >> 1 | (value & 8) >> 3


def lane_index(blocks):
    return lax.broadcasted_iota(jnp.int32, (blocks, LANES), 1)


def moved(here, beyond, lane, part):
    return pltpu.roll(jnp.where(lane >= part, here, beyond), (LANES - part) & 127, axis=1)


def later(ref, blocks, lane, shift):
    whole = shift >> 7
    return moved(ref[pl.ds(whole, blocks), :], ref[pl.ds(whole + 1, blocks), :], lane, shift & 127)


def clear_tail(refs, blocks):
    for ref in refs:
        ref[blocks : blocks + PAD, :] = jnp.zeros((PAD, LANES), jnp.float32)


def uppers(refs, trials):
    return [ref for row, ref in enumerate(refs) if row // trials % 2]


def rows_of(ref):
    return [ref.at[row] for row in range(ref.shape[0])]


def spread_sum(terms):
    strands = [None] * 4
    for index, term in enumerate(terms):
        strand = strands[index % 4]
        strands[index % 4] = term if strand is None else strand + term
    return (strands[0] + strands[1]) + (strands[2] + strands[3])


def packed_words(table_ref, width_ref, row):
    path, cross = jnp.int32(0), jnp.int32(0)
    spot = 0
    for trials, _ in PATH:
        index = row >> (ROWS // trials).bit_length() - 1
        path = path | (table_ref[trials - 1 + index] - 2 * index) << spot
        spot += 1
    spot = 0
    for fresh in (2, 4, 8, 16):
        for trial in range(fresh):
            index = row * fresh + trial
            cross = cross | (table_ref[ROWS * fresh - 1 + index] - 2 * index) << spot
            spot += 1
    words = [path, cross]
    for start in range(0, WIDTHS, 4):
        word = jnp.int32(0)
        for place in range(4):
            word = word | width_ref[start + place] << 8 * place
        words.append(word)
    return words


def local_kernel(
    table_hbm, width_hbm, x_hbm, rows_ref, words_ref,
    table_ref, width_ref, x_ref, small_sem, x_sem, *single,
):
    channels, length = x_ref.shape
    blocks = length // LANES
    stride = blocks + PAD
    groups = channels // 16
    copies = [
        pltpu.make_async_copy(x_hbm, x_ref, x_sem),
        pltpu.make_async_copy(table_hbm, table_ref, small_sem.at[0]),
        pltpu.make_async_copy(width_hbm, width_ref, small_sem.at[1]),
    ]
    for copy in copies:
        copy.start()
    lane = lane_index(blocks)
    normal, single = single[:groups], single[groups:]
    channel = [ref.at[pl.ds(row * stride, stride), :] for ref in normal for row in range(16)]
    inner, quads, eights, sixteens, halves = [single[ROWS * level : ROWS * (level + 1)] for level in range(5)]
    clear_tail(channel[3::4] + list(inner), blocks)
    for level, refs in enumerate((quads, eights, sixteens, halves)):
        clear_tail(uppers(refs, 1 << level), blocks)

    def row_of(refs, row):
        return refs[row][0:blocks, :]

    for copy in copies:
        copy.wait()
    for group in range(groups):
        rows = slice(16 * group, 16 * group + 16)

        def piece(block):
            return x_ref[rows, block * LANES : (block + 1) * LANES].astype(jnp.float32)

        total = spread_sum(piece(block) for block in range(blocks))
        centre = jnp.sum(total, axis=1, keepdims=True) / length
        centre = jnp.broadcast_to(centre, (16, LANES))
        total = spread_sum(jnp.square(piece(block) - centre) for block in range(blocks))
        spread = jnp.sum(total, axis=1, keepdims=True) / length
        gain = jnp.broadcast_to(lax.rsqrt(spread + epsilon), (16, LANES))
        for block in range(blocks):
            value = (piece(block) - centre) * gain
            for half in range(2):
                start = 8 * half * stride + block
                normal[group][pl.ds(start, 8, stride=stride), :] = value[8 * half : 8 * half + 8]
    shift = table_ref[0]
    partial = []
    for quad in range(ROWS):
        pair = row_of(channel, 4 * quad + 1) + row_of(channel, 4 * quad + 2)
        inner[quad][0:blocks, :] = pair + later(channel[4 * quad + 3], blocks, lane, shift)
        partial.append(pair + (row_of(channel, 4 * quad) + row_of(channel, 4 * quad + 3)))
    partial = spread_sum(partial)
    for row in MEAN_ROWS:
        rows_ref[row] = partial
    for quad in range(ROWS):
        quads[quad][0:blocks, :] = row_of(channel, 4 * quad) + later(inner[quad], blocks, lane, shift)
    bands, trials = ROWS, 1
    for source, target in ((quads, eights), (eights, sixteens), (sixteens, halves)):
        fresh = 2 * trials
        for trial in range(fresh):
            shift = table_ref[fresh - 1 + trial]
            for band in range(bands // 2):
                high = later(source[(2 * band + 1) * trials + trial // 2], blocks, lane, shift)
                value = row_of(source, 2 * band * trials + trial // 2) + high
                target[band * fresh + trial][0:blocks, :] = value
        bands, trials = bands // 2, fresh
    mine = reverse4(lax.axis_index("chan") & 15)
    for trial in range(ROWS):
        high = later(halves[8 + trial // 2], blocks, lane, table_ref[ROWS - 1 + trial])
        place = mine ^ trial
        group, low = place >> 2, place & 3
        spot = group * SPAN
        for other, (base, scale) in SPOTS.items():
            spot = jnp.where(low == other, base + scale * group, spot)
        rows_ref[spot] = row_of(halves, trial // 2) + high
    small_lane = lax.broadcasted_iota(jnp.int32, words_ref.shape, 1)
    words = jnp.zeros(words_ref.shape, jnp.int32)
    for index, word in enumerate(packed_words(table_ref, width_ref, mine)):
        words = jnp.where(small_lane == index, word, words)
    words_ref[...] = words


def local_rows(filterbank, shift_table, box_widths):
    channels, length = filterbank.shape
    blocks = length // LANES
    hbm = pl.BlockSpec(memory_space=pltpu.HBM)
    vmem = pl.BlockSpec(memory_space=pltpu.VMEM)
    inputs = [pltpu.with_memory_space_constraint(value, pltpu.HBM) for value in (shift_table, box_widths, filterbank)]
    return pl.pallas_call(
        local_kernel,
        out_shape=(
            jax.ShapeDtypeStruct((4 * SPAN + 5 * len(EARLY), blocks, LANES), jnp.float32),
            jax.ShapeDtypeStruct((8, LANES), jnp.int32),
        ),
        in_specs=[hbm] * 3,
        out_specs=(vmem, vmem),
        scratch_shapes=[
            pltpu.SMEM(shift_table.shape, jnp.int32),
            pltpu.SMEM(box_widths.shape, jnp.int32),
            pltpu.VMEM(filterbank.shape, filterbank.dtype),
            pltpu.SemaphoreType.DMA((2,)),
            pltpu.SemaphoreType.DMA,
            *[pltpu.VMEM((16 * (blocks + PAD), LANES), jnp.float32)] * (channels // 16),
            *[pltpu.VMEM((blocks + PAD, LANES), jnp.float32)] * 5 * ROWS,
        ],
        compiler_params=pltpu.CompilerParams(vmem_limit_bytes=32 << 20),
        name="local_tree",
    )(*inputs)


def mean_path(mean, word, scratch, blocks, lane, row):
    value = mean
    for step in range(0, len(PATH), 3):
        moves = []
        for trials, spot in PATH[step : step + 3]:
            index = row >> (ROWS // trials).bit_length() - 1
            shift = 2 * index + (word >> spot & 1)
            moves = moves + [shift] + [other + shift for other in moves]
        ref = scratch[step // 3]
        ref[0:blocks, :] = value
        value = value + spread_sum(later(ref, blocks, lane, move) for move in moves)
    return value


def cross_tree(me, mean, words, buffers, spare, blocks, lane):
    row = reverse4(me & 15)
    path, cross = words[0], words[1]
    mean = mean_path(mean, path, spare, blocks, lane, row)
    spare[3][0:blocks, :] = mean
    bands, trials = ROWS, 1
    spot = 0
    for source, target in zip(buffers[:-1], buffers[1:]):
        fresh = 2 * trials
        for trial in range(fresh):
            shift = 2 * (row * fresh + trial) + (cross >> spot & 1)
            spot += 1
            old = trial // 2
            if bands == ROWS:
                taken = mean + later(spare[3], blocks, lane, shift)
            for band in range(bands // 2):
                high = later(source[(2 * band + 1) * trials + old], blocks, lane, shift)
                value = source[2 * band * trials + old][0:blocks, :] + high
                if bands == ROWS:
                    value = value - taken
                target[band * fresh + trial][0:blocks, :] = value
        bands, trials = bands // 2, fresh


def finish(rows, widths, out_ref, peaks_ref, values, prefix, *split):
    stride = rows.shape[1]
    blocks = stride - PAD
    length = blocks * LANES
    lane = lax.broadcasted_iota(jnp.int32, (ROWS, LANES), 1)
    flat = rows.reshape(ROWS * stride, LANES)

    total = []
    for block in range(blocks):
        value = jnp.concatenate(
            [flat[pl.ds(block + 8 * half * stride, 8, stride=stride), :] for half in range(2)], axis=0
        )
        values[block] = value
        high = value.astype(jnp.bfloat16)
        rest = (value - high.astype(jnp.float32)).astype(jnp.bfloat16)
        ref, spot = split[block * 4 // blocks], block % (blocks // 4) * ROWS
        ref[pl.ds(spot, ROWS), pl.ds(0, LANES)] = high
        ref[pl.ds(spot, ROWS), pl.ds(LANES, LANES)] = rest
        total.append(value)
    centre = jnp.sum(spread_sum(total), axis=1, keepdims=True) / length
    centre = jnp.broadcast_to(centre, (ROWS, LANES))
    above = lax.broadcasted_iota(jnp.int32, (2 * LANES, 2 * LANES), 0) & 127
    across = lax.broadcasted_iota(jnp.int32, (2 * LANES, 2 * LANES), 1)
    weights = jnp.where(above <= across, 1.0, 0.0).astype(jnp.bfloat16)
    sums = [jnp.dot(ref[...], weights, preferred_element_type=jnp.float32) for ref in split]
    carry = jnp.zeros((ROWS, LANES), jnp.float32)
    prefix[0] = carry
    prefix[1] = carry
    ramp = centre * (lane + 1).astype(jnp.float32)
    drop = centre * LANES
    for block in range(blocks):
        spot = block % (blocks // 4) * ROWS
        part = sums[block * 4 // blocks][spot : spot + ROWS]
        prefix[2 + block] = (part[:, :LANES] - ramp) + carry
        carry = carry + (part[:, LANES:] - drop)

    spread = spread_sum(jnp.square(values[block] - centre) for block in range(blocks))
    spread = jnp.sum(spread, axis=1, keepdims=True) / length
    gain = jnp.broadcast_to(lax.rsqrt(spread + epsilon), (ROWS, LANES))
    for block in range(blocks):
        out_ref[:, pl.ds(block * LANES, LANES)] = ((values[block] - centre) * gain).astype(jnp.bfloat16)

    peaks = jnp.zeros((ROWS, LANES), jnp.float32)
    backs = [2 * LANES - width for width in widths]
    heres = [prefix[back >> 7] for back in backs]
    best = [None] * len(widths)
    for block in range(blocks):
        now = prefix[2 + block]
        for index, back in enumerate(backs):
            beyond = prefix[(back >> 7) + block + 1]
            gap = now - moved(heres[index], beyond, lane, back & 127)
            best[index] = gap if best[index] is None else jnp.maximum(best[index], gap)
            heres[index] = beyond
    for index, width in enumerate(widths):
        peak = jnp.max(best[index], axis=1, keepdims=True)
        scale = gain * lax.rsqrt(jnp.full((ROWS, LANES), width, jnp.int32).astype(jnp.float32))
        peaks = jnp.where(lane == index, peak * scale, peaks)
    peaks_ref[...] = jnp.transpose(peaks)[: len(widths)]


def cross_kernel(
    channels, count, finishing, words_ref, *rest,
):
    plane, rest = rest[:4], rest[4:]
    early, rest = rest[: len(EARLY)], rest[len(EARLY) :]
    late, rest = rest[: len(LATE)], rest[len(LATE) :]
    passed, (mean_ref, *rest) = rest[:3], rest[3:]
    blocks = mean_ref.shape[1]
    lane = lane_index(blocks)
    if finishing:
        out_ref, peaks_ref, first, final, *single, values, prefix, s0, s1, s2, s3 = rest
    else:
        series_ref, first, final, *single = rest
    words = [words_ref[0, index] for index in range(2 + WIDTHS // 4)]
    spare, single = single[:4], single[4:]
    buffers = [rows_of(first), single[:ROWS], single[ROWS : 2 * ROWS], single[2 * ROWS :], rows_of(final)]
    clear_tail(spare, blocks)
    for level, refs in enumerate(buffers[:4]):
        clear_tail(uppers(refs, 1 << level), blocks)
    me = lax.axis_index("chan")
    here = me & 15

    def place(offset, value):
        first[here ^ offset, pl.ds(0, blocks), :] = value

    offsets = (0, 2, 1, 3)
    for group, offset in enumerate(offsets):
        place(offset, plane[group][0])
        for index, step in enumerate(LATE):
            place(step + offset, late[index][group])
        for index, step in enumerate(EARLY):
            place(step + offset, passed[group - 1][index] if group else early[index][0])
    mean = mean_ref[0]
    if finishing:
        for ref in late:
            mean = mean + ref[4]
        for ref in passed:
            mean = mean + ref[len(EARLY)]
    mean = mean / (channels * count)
    cross_tree(me, mean, words, buffers, spare, blocks, lane)
    if finishing:
        finish(final, unpacked_widths(words), out_ref, peaks_ref, values, prefix, s0, s1, s2, s3)
    else:
        for trial in range(ROWS):
            series_ref[trial] = final[trial, pl.ds(0, blocks), :]


def unpacked_widths(words):
    return [words[2 + index // 4] >> 8 * (index % 4) & 255 for index in range(WIDTHS)]


def finish_kernel(words_ref, series_ref, out_ref, peaks_ref, rows, *scratch):
    blocks = series_ref.shape[1]
    words = [words_ref[0, index] for index in range(2 + WIDTHS // 4)]
    for trial in range(ROWS):
        rows[trial, pl.ds(0, blocks), :] = series_ref[trial]
    finish(rows, unpacked_widths(words), out_ref, peaks_ref, *scratch)


def row_scratch(blocks):
    return pltpu.VMEM((ROWS, blocks + PAD, LANES), jnp.float32)


def finish_scratch(blocks):
    return [
        pltpu.VMEM((blocks, ROWS, LANES), jnp.float32),
        pltpu.VMEM((blocks + 2, ROWS, LANES), jnp.float32),
        *[pltpu.VMEM((blocks // 4 * ROWS, 2 * LANES), jnp.bfloat16)] * 4,
    ]


def final_shapes(blocks):
    return (
        jax.ShapeDtypeStruct((ROWS, blocks * LANES), jnp.bfloat16),
        jax.ShapeDtypeStruct((WIDTHS, ROWS), jnp.float32),
    )


def swapped(block, distance):
    count = lax.axis_size("chan")
    return lax.ppermute(block, "chan", [(device, device ^ distance) for device in range(count)])


def advance(rows_in, shifts, start):
    count, length = rows_in.shape
    padded = jnp.concatenate([rows_in, jnp.zeros_like(rows_in)], axis=1)
    moved = lax.dynamic_slice_in_dim(padded, jnp.minimum(2 * start, length), length, 1)
    moved = jnp.concatenate([moved, jnp.zeros((count, 2 * count), moved.dtype)], axis=1)
    width = length + 2 * count
    flat = jnp.concatenate([moved.reshape(-1), jnp.zeros((2 * count,), moved.dtype)])
    skewed = flat.reshape(count, width + 2)[:, :length]
    odd = jnp.concatenate([skewed[:, 1:], jnp.zeros((count, 1), moved.dtype)], axis=1)
    parity = shifts - 2 * (start + jnp.arange(count, dtype=jnp.int32))
    return jnp.where((parity == 1)[:, None], odd, skewed)


def wider_sections(current, shift_table, me, section_count):
    half = ROWS // 2
    position = reverse4(me % 16)
    for bit in range(4, section_count):
        side = me >> bit & 1
        trials_now = 2 * ROWS << bit
        theirs = lax.dynamic_slice_in_dim(current, (1 - side) * half, half, 0)
        ours = lax.dynamic_slice_in_dim(current, side * half, half, 0)
        arrived = swapped(theirs, 1 << bit)
        lower = jnp.where(side == 0, ours, arrived)
        upper = jnp.where(side == 0, arrived, ours)
        first_trial = 2 * (position * ROWS + side * half)
        shifts = lax.dynamic_slice_in_dim(shift_table, trials_now - 1 + first_trial, ROWS)
        current = jnp.repeat(lower, 2, axis=0) + advance(jnp.repeat(upper, 2, axis=0), shifts, first_trial)
        position = 2 * position + side
    return current


def shards(filterbank, shift_table, box_widths):
    channels, length = filterbank.shape
    blocks = length // LANES
    count = lax.axis_size("chan")
    section_count = count.bit_length() - 1
    rows, words = local_rows(filterbank, shift_table, box_widths)
    small = section_count == 4

    early = [swapped(rows[4 * SPAN + 5 * index : 4 * SPAN + 5 * index + 5], step) for index, step in enumerate(EARLY)]
    plane = [rows] + [
        swapped(rows[SPAN * group : SPAN * (group + 1)], offset) for group, offset in ((1, 2), (2, 1), (3, 3))
    ]
    mean = sum(part[SPAN - 1 : SPAN] for part in plane)
    late = [
        swapped(jnp.concatenate([part[1 + index : 2 + index] for part in plane] + [mean], axis=0), step)
        for index, step in enumerate(LATE)
    ]
    column = sum(part[4:] for part in early)
    passed = [
        swapped(jnp.concatenate([part[group : group + 1] for part in early] + [column], axis=0), offset)
        for group, offset in ((1, 2), (2, 1), (3, 3))
    ]
    mean = mean + column
    arrived = [*plane, *early, *late, *passed]
    if not small:
        mean = lax.psum(rows[SPAN - 1 : SPAN], "chan")

    vmem = pl.BlockSpec(memory_space=pltpu.VMEM)
    params = pltpu.CompilerParams(vmem_limit_bytes=32 << 20)
    call = pl.pallas_call(
        functools.partial(cross_kernel, channels, count, small),
        out_shape=final_shapes(blocks)
        if small
        else jax.ShapeDtypeStruct((ROWS, blocks, LANES), jnp.float32),
        in_specs=[vmem] * (len(arrived) + 2),
        out_specs=(vmem, vmem) if small else vmem,
        scratch_shapes=[
            *[row_scratch(blocks)] * 2,
            *[pltpu.VMEM((blocks + PAD, LANES), jnp.float32)] * (4 + 3 * ROWS),
            *(finish_scratch(blocks) if small else []),
        ],
        compiler_params=params,
        name="cross_tree",
    )
    result = call(words, *arrived, mean)
    if small:
        return tuple(result)
    me = lax.axis_index("chan")
    current = wider_sections(result.reshape(ROWS, length), shift_table, me, section_count)
    return tuple(
        pl.pallas_call(
            finish_kernel,
            out_shape=final_shapes(blocks),
            in_specs=[vmem, vmem],
            out_specs=(vmem, vmem),
            scratch_shapes=[row_scratch(blocks)] + finish_scratch(blocks),
            compiler_params=params,
            name="finish",
        )(words, current.reshape(ROWS, blocks, LANES))
    )


def solution(mesh):
    placed = (P(("beam", "chan"), None), P(), P())
    return jax.shard_map(
        shards,
        mesh=mesh,
        in_specs=placed,
        out_specs=(P(("beam", "chan"), None), P("beam", "chan")),
        check_vma=False,
    )
```
